32 devices in a mesh: gx: 8 (over z, x), gy: 4 (over y, core).
Axes of the slice: x: 2, y: 2, z: 4, core: 2. Of those that a mesh axis runs over, the one named last changes fastest.
Arguments:
- vectors: float32 [2, 128, 128, 548], P(None, 'gx', 'gy'), may hold values from -6 to 6
- diffusivity: float32 [128, 128], P('gx', 'gy'), may hold values from 0.2 to 0.25
- vertical_factor: float32 [548, 548], replicated, may hold values from -4 to 4, as said below
- weight_first: float32 [548, 768], replicated, may hold values from -0.25 to 0.25
- bias_first: float32 [768], replicated, may hold values from -3 to 3
- weight_second: float32 [768, 768], replicated, may hold values from -0.21875 to 0.21875
- bias_second: float32 [768], replicated, may hold values from -3 to 3
- weight_out: float32 [768, 616], replicated, may hold values from -0.21875 to 0.21875
- error_inverse: float32 [616, 616], replicated, may hold values from -4 to 4, as said below
- observed_column: int32 [16384], P(('gx', 'gy')), may hold values from 0 to 16383, as said below
- owner_count: int32 [32], P(('gx', 'gy')), may hold values from 16 to 512
- observed_state: float32 [16384, 548], P(('gx', 'gy')), may hold values from -6 to 6
- channel_mask: int32 [32, 616], replicated, may hold values 0 or 1
Outputs:
- products: float32 [2, 128, 128, 548], P(None, 'gx', 'gy')
The draws below stay inside these ranges and needn't reach their ends.
Inputs may be any that keep to these rules, and one draw needn't show every extreme that they name: `observed_column`: tile (a, b) holds the cells i with i // 16 = a and j with j // 32 = b. Among the used slots of one owner at most 16 lie in any one tile, and some tile receives exactly 16 from every owner. Unused slots hold valid columns. `vertical_factor`: the identity plus a dense random part; well conditioned. `error_inverse`: symmetric positive definite with a dominant diagonal.
All inputs are finite; a program needn't handle non-finite values.
Results may differ from the reference program's by a relative error of at most 0.0003.
Values sent between devices are 32-bit elements; how exact they have to be, the bound alone decides.
No kernel may reach another device: no remote copies, remote signals or barrier semaphores. Data moves between devices by JAX's collectives and lax.ppermute only.
A program may use at most 128 MiB of HBM per device.

```python
import jax
import jax.numpy as jnp
from jax import lax

LEVELS = 548
UNITS = 768
CHANNELS = 616
SWEEPS = 4
CX = 16
CY = 32
SLOTS = 512
NX = 128
NY = 128
BUCKET = 16
N_GY = 4
DEVICES = 32


def obs_layout(key):
    key_shift = jax.random.fold_in(key, 11)
    key_count = jax.random.fold_in(key, 12)
    key_full = jax.random.fold_in(key, 13)
    key_order = jax.random.fold_in(key, 14)
    key_cell = jax.random.fold_in(key, 15)
    key_owner = jax.random.fold_in(key, 16)
    key_often = jax.random.fold_in(key, 17)
    key_side = jax.random.fold_in(key, 18)
    key_along = jax.random.fold_in(key, 19)
    key_which = jax.random.fold_in(key, 20)
    owners = DEVICES
    shifts = jax.random.randint(key_shift, (owners, 1), 0, 3)
    owner_cap = jnp.right_shift(jnp.full((owners, 1), BUCKET, jnp.int32), shifts)
    counts = jax.random.randint(key_count, (owners, DEVICES), 0, owner_cap + 1)
    full_dest = jax.random.randint(key_full, (), 0, DEVICES)
    counts = jnp.where(jnp.arange(DEVICES)[None, :] == full_dest, BUCKET, counts)
    full_owner = jax.random.randint(key_owner, (), 0, owners)
    counts = jnp.where(jnp.arange(owners)[:, None] == full_owner, BUCKET, counts)
    position = jnp.arange(SLOTS, dtype=jnp.int32)
    within = position % BUCKET
    target = position // BUCKET
    active = (within[None, :] < counts[:, target]).astype(jnp.int32)
    randoms = jax.random.randint(key_order, (owners, SLOTS), 0, SLOTS)
    scores = (1 - active) * SLOTS * SLOTS + randoms * SLOTS + position[None, :]
    ordering = jnp.argsort(scores, axis=1, stable=True)
    target_sorted = jnp.take_along_axis(jnp.broadcast_to(target[None, :], (owners, SLOTS)), ordering, axis=1)
    spread_cell = jax.random.randint(key_cell, (owners, SLOTS), 0, CX * CY)
    favoured_side = jax.random.randint(key_side, (DEVICES, 4), 0, 4)
    favoured_along = jax.random.randint(key_along, (DEVICES, 4), 0, CX * CY)
    which = jax.random.randint(key_which, (owners, SLOTS), 0, 4)
    often = jax.random.randint(key_often, (owners, SLOTS), 0, 3) == 0
    side = favoured_side[target_sorted, which]
    along = favoured_along[target_sorted, which]
    along_row = along % CX
    along_col = along % CY
    side_row = jnp.where(side == 0, 3, jnp.where(side == 1, CX - 4, along_row))
    side_col = jnp.where(side == 2, 3, jnp.where(side == 3, CY - 4, along_col))
    local_cell = jnp.where(often, side_row * CY + side_col, spread_cell)
    tile_a = target_sorted // N_GY
    tile_b = target_sorted % N_GY
    grid_row = tile_a * CX + local_cell // CY
    grid_col = tile_b * CY + local_cell % CY
    column = grid_row * (CY * N_GY) + grid_col
    return (column.reshape(-1).astype(jnp.int32), jnp.sum(counts, axis=1).astype(jnp.int32))


def draw_observed_column(key, part):
    return obs_layout(key)[0]


def draw_owner_count(key, part):
    return obs_layout(key)[1]


def draw_vertical_factor(key, part):
    noise = jax.random.normal(jax.random.fold_in(key, 21), (LEVELS, LEVELS), jnp.float32)
    return jnp.eye(LEVELS, dtype=jnp.float32) + 0.6 * noise / jnp.sqrt(jnp.float32(LEVELS))


def draw_error_inverse(key, part):
    noise = jax.random.normal(jax.random.fold_in(key, 31), (CHANNELS, CHANNELS), jnp.float32)
    diagonal = jax.random.uniform(jax.random.fold_in(key, 32), (CHANNELS,), jnp.float32, 1.5, 3.0)
    symmetric = (noise + noise.T) * (0.5 / jnp.sqrt(2.0 * CHANNELS))
    return symmetric + jnp.diag(diagonal)


def touch_ends(drawn, key, least, high):
    longest = drawn.shape.index(max(drawn.shape))
    spots = []
    for shift in (0, 1):
        where = [jax.random.randint(jax.random.fold_in(key, axis), (), 0, length) for axis, length in enumerate(drawn.shape)]
        where[longest] = (where[longest] + shift) % drawn.shape[longest]
        spots.append(tuple(where))
    return drawn.at[spots[0]].set(least).at[spots[1]].set(high)


def shard_levels(own_key, dims, cuts, smallest, top_value):
    loudness, own = 1.0, jax.random.fold_in(own_key, 6)
    for dim, shards_of in cuts:
        heights = jnp.exp(jax.random.uniform(jax.random.fold_in(own, dim), (shards_of,), jnp.float32, smallest / len(cuts), top_value / len(cuts)))
        loudness = loudness * jnp.repeat(heights, dims[dim] // shards_of).reshape([-1 if axis == dim else 1 for axis in range(len(dims))])
    return loudness


def bell_draw(rng, extent, spread, reach, cuts=(), kind=jnp.bfloat16):
    level = shard_levels(rng, extent, cuts, -0.22, 0.18) if cuts else 1.0
    values = jax.random.normal(rng, extent, jnp.float32) * spread * level
    return jnp.minimum(jnp.maximum(values, -reach), reach).astype(kind)


def setup_inputs(seed: int = 0) -> dict:
    seeds = jax.random.split(jax.random.key(seed), 14)
    return {
        "vectors": bell_draw(seeds[0], (2, NX, NY, LEVELS), 1.0, 6.0, ((1, 8), (2, 4)), jnp.float32),
        "diffusivity": jnp.clip(0.2 + 0.049999997 * jax.random.uniform(seeds[1], (NX, NY), jnp.float32) ** shard_levels(seeds[1], (NX, NY), ((0, 8), (1, 4)), -0.2, 0.2), 0.2, 0.25),
        "vertical_factor": draw_vertical_factor(jax.random.fold_in(seeds[13], 71), 0),
        "weight_first": bell_draw(seeds[3], (LEVELS, UNITS), LEVELS ** -0.5, 0.25, (), jnp.float32),
        "bias_first": bell_draw(seeds[4], (UNITS,), 0.5, 3.0, (), jnp.float32),
        "weight_second": bell_draw(seeds[5], (UNITS, UNITS), UNITS ** -0.5, 0.21875, (), jnp.float32),
        "bias_second": bell_draw(seeds[6], (UNITS,), 0.5, 3.0, (), jnp.float32),
        "weight_out": bell_draw(seeds[7], (UNITS, CHANNELS), UNITS ** -0.5, 0.21875, (), jnp.float32),
        "error_inverse": draw_error_inverse(jax.random.fold_in(seeds[13], 71), 0),
        "observed_column": draw_observed_column(jax.random.fold_in(seeds[13], 71), 0),
        "owner_count": draw_owner_count(jax.random.fold_in(seeds[13], 71), 0),
        "observed_state": bell_draw(seeds[11], (DEVICES * SLOTS, LEVELS), 1.0, 6.0, ((0, 32),), jnp.float32),
        "channel_mask": touch_ends((jax.random.randint(seeds[12], (DEVICES, CHANNELS), 0, 4) < 3).astype(jnp.int32), jax.random.fold_in(seeds[12], 1), 0, 1),
    }


HIGH = lax.Precision.HIGHEST


def laplace(field):
    padded = jnp.pad(field, ((0, 0), (1, 1), (1, 1), (0, 0)))
    beside_all = padded[:, 2:, 1:-1] + padded[:, :-2, 1:-1] + padded[:, 1:-1, 2:] + padded[:, 1:-1, :-2]
    return beside_all - 4.0 * field


def network(profile, perturb, gate, weight_first, bias_first, weight_second, bias_second, weight_out, error_inverse):
    hidden_one = jnp.tanh(jnp.dot(profile, weight_first, precision=HIGH) + bias_first)
    hidden_two = jnp.tanh(jnp.dot(hidden_one, weight_second, precision=HIGH) + bias_second)
    slope_one = 1.0 - hidden_one * hidden_one
    slope_two = 1.0 - hidden_two * hidden_two
    tangent = jnp.einsum("vnk,kh->vnh", perturb, weight_first, precision=HIGH) * slope_one
    tangent = jnp.einsum("vnh,hg->vng", tangent, weight_second, precision=HIGH) * slope_two
    tangent = jnp.einsum("vng,gc->vnc", tangent, weight_out, precision=HIGH)
    weighted = gate * jnp.einsum("vnc,cd->vnd", gate * tangent, error_inverse, precision=HIGH)
    gradient = jnp.einsum("vnc,gc->vng", weighted, weight_out, precision=HIGH) * slope_two
    gradient = jnp.einsum("vng,hg->vnh", gradient, weight_second, precision=HIGH) * slope_one
    return jnp.einsum("vnh,kh->vnk", gradient, weight_first, precision=HIGH)


def reference(vectors, diffusivity, vertical_factor, weight_first, bias_first, weight_second, bias_second, weight_out, error_inverse, observed_column, owner_count, observed_state, channel_mask):
    shape = vectors.shape
    increment = jnp.dot(vectors.reshape(-1, LEVELS), vertical_factor.T, precision=HIGH).reshape(shape)
    coeff = diffusivity[None, :, :, None]
    for sweep in range(SWEEPS):
        increment = increment + coeff * laplace(increment)
    states = increment.reshape(2, NX * NY, LEVELS)

    def owner_work(packed):
        columns, used_count, profile, mask_row = packed
        in_use = (jnp.arange(SLOTS, dtype=jnp.int32) < used_count).astype(jnp.float32)
        gate = mask_row.astype(jnp.float32)[None, :] * in_use[:, None]
        perturb = states[:, columns]
        return network(profile, perturb, gate, weight_first, bias_first, weight_second, bias_second, weight_out, error_inverse)

    gradient = lax.map(owner_work, (observed_column.reshape(DEVICES, SLOTS), owner_count, observed_state.reshape(DEVICES, SLOTS, LEVELS), channel_mask))
    gradient = jnp.transpose(gradient, (1, 0, 2, 3)).reshape(2, DEVICES * SLOTS, LEVELS)
    field = jnp.zeros((2, NX * NY, LEVELS), jnp.float32).at[:, observed_column].add(gradient)
    field = field.reshape(shape)
    for sweep in range(SWEEPS):
        field = field + laplace(coeff * field)
    return vectors + jnp.dot(field.reshape(-1, LEVELS), vertical_factor, precision=HIGH).reshape(shape)
```

```python
import functools

import jax
import jax.numpy as jnp
from jax import lax
from jax.experimental import pallas as pl
from jax.experimental.pallas import tpu as pltpu
from jax.sharding import PartitionSpec as P

SWEEPS = 4
WIDE = 256
LANES = 128
BF = jnp.bfloat16
F32 = jnp.float32
NN = ((1,), (0,))
NT = ((1,), (1,))
TN = ((0,), (0,))


def up(size, unit):
    return -(-size // unit) * unit


def split(value):
    high = value.astype(BF)
    return high, (value - high.astype(F32)).astype(BF)


def mm(left, right, dims=NN):
    return lax.dot_general(left, right, (dims, ((), ())), preferred_element_type=F32)


def mm3(left_high, left_low, right_high, right_low, dims=NN):
    return mm(left_high, right_high, dims) + (
        mm(left_high, right_low, dims) + mm(left_low, right_high, dims)
    )


def iota(shape, axis):
    return lax.broadcasted_iota(jnp.int32, shape, axis)


def call(kernel, out_shape, flops, moved, scratch=(), vmem=48, **more):
    return pl.pallas_call(
        kernel,
        out_shape=out_shape,
        scratch_shapes=list(scratch),
        compiler_params=pltpu.CompilerParams(vmem_limit_bytes=vmem * 1024 * 1024),
        cost_estimate=pl.CostEstimate(flops=flops, bytes_accessed=moved, transcendentals=0),
        **more,
    )


def shaped(shape, dtype=F32):
    return jax.ShapeDtypeStruct(shape, dtype)


def pack_kernel(bucket, dest_ref, cell_ref, state_ref, out_ref, high_ref, low_ref):
    levels, slots = state_ref.shape
    devices = slots // bucket
    dest = dest_ref[...]
    same = (iota((devices, slots), 0) == dest).astype(F32)
    before = (iota((slots, slots), 0) < iota((slots, slots), 1)).astype(BF)
    rank = jnp.sum(same * mm(same.astype(BF), before), axis=0, keepdims=True)
    place = dest * bucket + rank.astype(jnp.int32)
    pick = (iota((slots, slots), 0) == place).astype(BF)
    high_ref[...] = jnp.zeros_like(high_ref)
    low_ref[...] = jnp.zeros_like(low_ref)
    high, low = split(state_ref[...])
    high_ref[:levels, :] = high
    low_ref[:levels, :] = low
    mark = up(levels, 16)
    tall = jnp.where(iota((16, slots), 0) == 0, cell_ref[...], 0.0)
    high, low = split(tall)
    high_ref[mark : mark + 16, :] = high
    low_ref[mark : mark + 16, :] = low
    out_ref[...] = mm(pick, high_ref[...], NT) + mm(pick, low_ref[...], NT)


def prep_kernel(factor_ref, first_ref, second_ref, out_t_ref, error_ref, *refs):
    outs, (pad_a, pad_b) = refs[:10], refs[10:]

    def put(values, high_ref, low_ref):
        rows, cols = values.shape
        if (rows, cols) != high_ref.shape:
            high_ref[...] = jnp.zeros_like(high_ref)
            low_ref[...] = jnp.zeros_like(low_ref)
        high, low = split(values)
        high_ref[:rows, :cols] = high
        low_ref[:rows, :cols] = low

    put(first_ref[...], outs[0], outs[1])
    put(second_ref[...], outs[2], outs[3])
    put(out_t_ref[...], outs[4], outs[5])
    put(error_ref[...], outs[6], outs[7])
    put(factor_ref[...].T, pad_a, pad_b)
    rows = pad_a.shape[1]
    units = outs[8].shape[1]

    def step(j, _):
        cols = pl.ds(pl.multiple_of(j * WIDE, WIDE), WIDE)
        got = mm3(pad_a[...], pad_b[...], outs[0][:rows, cols], outs[1][:rows, cols])
        high, low = split(got)
        outs[8][:, cols] = high
        outs[9][:, cols] = low
        return 0

    lax.fori_loop(0, units // WIDE, step, 0)


def fill(ext, tile, xlo, xhi, ylo, yhi):
    rows, wide, levels = tile.shape
    w = SWEEPS
    last = up(levels, LANES) - LANES
    ext[:, :, last:] = jnp.zeros((ext.shape[0], ext.shape[1], ext.shape[2] - last), F32)
    ext[w : w + rows, :wide, :levels] = tile
    ext[:w, :wide, :levels] = xlo
    ext[w + rows :, :wide, :levels] = xhi
    ext[:, wide : wide + w, :levels] = yhi
    ext[:, wide + w :, :levels] = ylo


def diffuse_kernel(
    tile_ref, coeff_ref, xlo_ref, xhi_ref, ylo_ref, yhi_ref, ahigh_ref, alow_ref,
    out_ref, cb_ref, ext, work, high_ref, low_ref,
):
    w = SWEEPS
    rows, wide, levels = tile_ref.shape[1:]
    tall = rows + 2 * w
    fill(
        ext,
        tile_ref[0],
        xlo_ref[0, :, :, :levels],
        xhi_ref[0, :, :, :levels],
        ylo_ref[0, :, :, :levels],
        yhi_ref[0, :, :, :levels],
    )

    def spread(ref):
        column = ref[0, :, :, levels : levels + 1]
        return jnp.broadcast_to(column, column.shape[:2] + (LANES,))

    cb_ref[w : w + rows, :wide, :] = coeff_ref[...]
    cb_ref[:w, :wide, :] = spread(xlo_ref)
    cb_ref[w + rows :, :wide, :] = spread(xhi_ref)
    cb_ref[:, wide : wide + w, :] = spread(yhi_ref)
    cb_ref[:, wide + w :, :] = spread(ylo_ref)
    around = wide + 2 * w

    def chunk(j, _):
        lanes = pl.ds(pl.multiple_of(j * LANES, LANES), LANES)
        for sweep in range(SWEEPS):
            for i in range(sweep + 1, tall - 1 - sweep):
                if sweep == 0:
                    above, mid, below = (ext[k, :, lanes] for k in (i - 1, i, i + 1))
                else:
                    above, mid, below = (work[(sweep + 1) % 2, k] for k in (i - 1, i, i + 1))
                beside = above + below + pltpu.roll(mid, 1, 0) + pltpu.roll(mid, around - 1, 0)
                new = mid + cb_ref[i] * (beside - 4.0 * mid)
                if sweep == SWEEPS - 1:
                    high, low = split(new[:wide])
                    here = pl.ds((i - w) * wide, wide)
                    high_ref[here, lanes] = high
                    low_ref[here, lanes] = low
                else:
                    work[sweep % 2, i] = new
        return 0

    lax.fori_loop(0, ext.shape[2] // LANES, chunk, 0)
    deep = ext.shape[2]

    def step(j, _):
        cols = pl.ds(pl.multiple_of(j * WIDE, WIDE), WIDE)
        out_ref[0, :, cols] = mm3(
            high_ref[...], low_ref[...], ahigh_ref[:deep, cols], alow_ref[:deep, cols]
        )
        return 0

    lax.fori_loop(0, out_ref.shape[2] // WIDE, step, 0)


def hidden_kernel(
    mark, bucket, x_ref, w1h, w1l, b1_ref, w2h, w2l, b2_ref, mask_ref,
    s1_ref, s2_ref, gate_ref, one_ref, one_t_ref, high_ref, low_ref,
):
    slots, deep = x_ref.shape
    cells = one_ref.shape[1]
    devices, channels = mask_ref.shape
    index = x_ref[:, mark : mark + 1]
    cell = index.astype(jnp.int32) - 1
    live = index > 0.5
    one_ref[...] = (iota((slots, cells), 1) == cell).astype(BF)
    flat = jnp.broadcast_to(index, (slots, LANES)).T[0:1, :].astype(jnp.int32) - 1
    one_t_ref[...] = (iota((cells, slots), 0) == flat).astype(BF)
    first = iota((slots, devices), 1) * bucket
    at = iota((slots, devices), 0)
    from_owner = ((at >= first) & (at < first + bucket) & live).astype(BF)
    gate_ref[...] = jnp.zeros_like(gate_ref)
    gate_ref[:, :channels] = mm(from_owner, mask_ref[...].astype(F32).astype(BF))
    high, low = split(x_ref[...])
    high_ref[:, :deep] = high
    low_ref[:, :deep] = low
    units = s1_ref.shape[1]

    def one(j, _):
        cols = pl.ds(pl.multiple_of(j * WIDE, WIDE), WIDE)
        got = mm3(high_ref[:, :deep], low_ref[:, :deep], w1h[:deep, cols], w1l[:deep, cols])
        hidden = jnp.tanh(got + b1_ref[:, cols])
        s1_ref[:, cols] = 1.0 - hidden * hidden
        s2_ref[:, cols] = hidden
        return 0

    lax.fori_loop(0, units // WIDE, one, 0)
    high, low = split(s2_ref[...])
    high_ref[...] = high
    low_ref[...] = low

    def two(j, _):
        cols = pl.ds(pl.multiple_of(j * WIDE, WIDE), WIDE)
        got = mm3(high_ref[...], low_ref[...], w2h[:, cols], w2l[:, cols])
        hidden = jnp.tanh(got + b2_ref[:, cols])
        s2_ref[:, cols] = 1.0 - hidden * hidden
        return 0

    lax.fori_loop(0, units // WIDE, two, 0)


def net_kernel(
    q_ref, one_ref, one_t_ref, s1_ref, s2_ref, gate_ref,
    w2h, w2l, woh, wol, eh, el, ah, al,
    out_ref, x1h, x1l, x2h, x2l,
):
    units = s1_ref.shape[1]

    def cols_of(j):
        return pl.ds(pl.multiple_of(j * WIDE, WIDE), WIDE)

    def store(pair, cols, value):
        high, low = split(value)
        pair[0][:, cols] = high
        pair[1][:, cols] = low

    def layer(source, weights, scale_ref, target, dims, times):
        def step(j, _):
            cols = cols_of(j)
            if dims == NN:
                right = (weights[0][:, cols], weights[1][:, cols])
            else:
                right = (weights[0][cols, :], weights[1][cols, :])
            got = mm3(source[0][...], source[1][...], *right, dims)
            for scale in scale_ref:
                got = got * scale[:, cols]
            store(target, cols, got)
            return 0

        lax.fori_loop(0, times, step, 0)

    def choose(source, picker, scale_ref, target):
        def step(j, _):
            cols = cols_of(j)
            got = mm(picker[...], source[0][:, cols]) + mm(picker[...], source[1][:, cols])
            for scale in scale_ref:
                got = got * scale[:, cols]
            store(target, cols, got)
            return 0

        lax.fori_loop(0, units // WIDE, step, 0)

    one, two = (x1h, x1l), (x2h, x2l)
    times = units // WIDE
    high, low = split(q_ref[0])
    x1h[...] = high
    x1l[...] = low
    choose(one, one_ref, [s1_ref], two)
    layer(two, (w2h, w2l), [s2_ref], one, NN, times)
    layer(one, (woh, wol), [gate_ref], two, NT, woh.shape[0] // WIDE)
    layer(two, (eh, el), [gate_ref], one, NN, times)
    layer(one, (woh, wol), [s2_ref], two, NN, times)
    layer(two, (w2h, w2l), [s1_ref], one, NT, times)
    choose(one, one_t_ref, [], two)
    rows, wide, levels = out_ref.shape
    for start in range(0, levels, WIDE):
        stop = min(start + WIDE, levels)
        here = pl.ds(start, WIDE)
        got = mm3(x2h[...], x2l[...], ah[here, :], al[here, :], NT)
        out_ref[:, :, start:stop] = got.reshape(rows, wide, WIDE)[:, :, : stop - start]


def finish_kernel(
    field_ref, base_ref, xlo_ref, xhi_ref, ylo_ref, yhi_ref, cb_ref, *refs
):
    out_ref, ext, work, total = refs[-4:]
    w = SWEEPS
    rows, wide, levels = field_ref.shape
    tall = rows + 2 * w
    fill(ext, field_ref[...], xlo_ref[...], xhi_ref[...], ylo_ref[...], yhi_ref[...])
    around = wide + 2 * w

    def chunk(j, _):
        lanes = pl.ds(pl.multiple_of(j * LANES, LANES), LANES)
        for sweep in range(SWEEPS):

            def read(k):
                value = ext[k, :, lanes] if sweep == 0 else work[(sweep + 1) % 2, k]
                return value, cb_ref[k] * value

            above = read(sweep)
            mid = read(sweep + 1)
            for i in range(sweep + 1, tall - 1 - sweep):
                below = read(i + 1)
                scaled = mid[1]
                beside = (
                    above[1] + below[1]
                    + pltpu.roll(scaled, 1, 0) + pltpu.roll(scaled, around - 1, 0)
                )
                new = mid[0] + (beside - 4.0 * scaled)
                if sweep == SWEEPS - 1:
                    total[i - w, :, lanes] = new[:wide]
                else:
                    work[sweep % 2, i] = new
                above, mid = mid, below
        return 0

    lax.fori_loop(0, ext.shape[2] // LANES, chunk, 0)
    out_ref[0] = base_ref[0] + total[:, :, :levels]


def shift(value, axis, by):
    count = lax.axis_size(axis)
    return lax.ppermute(
        value, axis, [(i, i + by) for i in range(count) if 0 <= i + by < count]
    )


def halo(cut):
    xlo = shift(cut(0, 1), "gx", 1)
    xhi = shift(cut(0, 0), "gx", -1)
    last = jnp.concatenate(
        [xlo[..., -SWEEPS:, :], cut(1, 1), xhi[..., -SWEEPS:, :]], axis=-3
    )
    head = jnp.concatenate(
        [xlo[..., :SWEEPS, :], cut(1, 0), xhi[..., :SWEEPS, :]], axis=-3
    )
    ylo = shift(last, "gy", 1)
    yhi = shift(head, "gy", -1)
    return xlo, xhi, ylo, yhi


def strip(array, axis, side):
    size = array.shape[axis]
    if side:
        return lax.slice_in_dim(array, size - SWEEPS, size, axis=axis)
    return lax.slice_in_dim(array, 0, SWEEPS, axis=axis)


def body(
    vectors, diffusivity, vertical_factor, weight_first, bias_first, weight_second,
    bias_second, weight_out, error_inverse, observed_column, owner_count,
    observed_state, channel_mask,
):
    pairs, tile_x, tile_y, levels = vectors.shape
    count_y = lax.axis_size("gy")
    devices = lax.axis_size("gx") * count_y
    slots = observed_column.shape[0]
    bucket = slots // devices
    cells = tile_x * tile_y
    grid_wide = tile_y * count_y
    units = weight_second.shape[0]
    deep = up(levels, LANES)
    tall, around = tile_x + 2 * SWEEPS, tile_y + 2 * SWEEPS
    full_l, full_u = up(levels, WIDE), up(units, WIDE)
    full_c = up(error_inverse.shape[0], WIDE)
    mark = up(levels, 16)

    def withc(dim, side):
        cut = strip(vectors, dim + 1, side)
        coeff = strip(diffusivity, dim, side)[None, :, :, None]
        coeff = jnp.broadcast_to(coeff, cut.shape[:3] + (1,))
        return jnp.concatenate([cut, coeff], axis=-1)

    xlo, xhi, ylo, yhi = halo(withc)

    position = jnp.arange(slots, dtype=jnp.int32)
    grid_row = observed_column // grid_wide
    grid_col = observed_column % grid_wide
    target = grid_row // tile_x * count_y + grid_col // tile_y
    dest = jnp.where(position < owner_count[0], target, -1)
    cell = (grid_row % tile_x * tile_y + grid_col % tile_y + 1).astype(F32)
    packed = call(
        functools.partial(pack_kernel, bucket),
        shaped((slots, deep)),
        flops=6 * slots * slots * deep,
        moved=8 * slots * deep,
        scratch=[pltpu.VMEM((deep, slots), BF)] * 2,
    )(dest[None, :], cell[None, :], observed_state.T)
    carried = lax.all_to_all(
        packed.reshape(devices, bucket, deep), ("gx", "gy"), split_axis=0, concat_axis=0,
        tiled=True,
    ).reshape(slots, deep)

    sizes = [(full_l, full_u), (full_u, full_u), (full_c, full_u), (full_c, full_c), (full_l, full_u)]
    w1h, w1l, w2h, w2l, woh, wol, eh, el, ah, al = call(
        prep_kernel,
        [shaped(size, BF) for size in sizes for _ in range(2)],
        flops=6 * full_l * full_l * full_u,
        moved=8 * 5 * full_u * full_u,
        scratch=[pltpu.VMEM((full_l, full_l), BF)] * 2,
    )(vertical_factor, weight_first, weight_second, weight_out.T, error_inverse)

    coeff = jnp.broadcast_to(diffusivity[:, :, None], (tile_x, tile_y, LANES))
    whole = pl.BlockSpec(memory_space=pltpu.VMEM)

    def per(shape):
        return pl.BlockSpec((1,) + shape[1:], lambda v: (v,) + (0,) * (len(shape) - 1))

    def fixed(shape):
        return pl.BlockSpec(shape, lambda v: (0,) * len(shape), pipeline_mode=pl.Buffered(1))

    queries, spread = call(
        diffuse_kernel,
        [shaped((pairs, cells, full_u)), shaped((tall, around, LANES))],
        flops=6 * pairs * cells * deep * full_u,
        moved=8 * pairs * tall * around * deep,
        scratch=[
            pltpu.VMEM((tall, around, deep), F32),
            pltpu.VMEM((2, tall, around, LANES), F32),
            pltpu.VMEM((cells, deep), BF),
            pltpu.VMEM((cells, deep), BF),
        ],
        grid=(pairs,),
        in_specs=[
            per(vectors.shape), fixed(coeff.shape), per(xlo.shape), per(xhi.shape),
            per(ylo.shape), per(yhi.shape), fixed(ah.shape), fixed(al.shape),
        ],
        out_specs=[per((pairs, cells, full_u)), pl.BlockSpec((tall, around, LANES), lambda v: (0, 0, 0))],
    )(vectors, coeff, xlo, xhi, ylo, yhi, ah, al)

    s1, s2, gate, one, one_t = call(
        functools.partial(hidden_kernel, mark, bucket),
        [
            shaped((slots, full_u)), shaped((slots, full_u)), shaped((slots, full_c)),
            shaped((slots, cells), BF), shaped((cells, slots), BF),
        ],
        flops=12 * slots * full_u * full_u,
        moved=8 * slots * full_u,
        scratch=[pltpu.VMEM((slots, full_u), BF)] * 2,
    )(carried, w1h, w1l, bias_first[None, :], w2h, w2l, bias_second[None, :], channel_mask)

    fields = []
    for v in range(pairs):
        fields.append(
            call(
                net_kernel,
                shaped((tile_x, tile_y, levels)),
                flops=36 * slots * full_u * full_u,
                moved=4 * 5 * full_u * full_u,
                scratch=[pltpu.VMEM((slots, full_u), BF)] * 4,
                grid=(1,),
                in_specs=[pl.BlockSpec((1, cells, full_u), functools.partial(lambda v, i: (v, 0, 0), v))]
                + [whole] * 13,
                out_specs=whole,
            )(queries, one, one_t, s1, s2, gate, w2h, w2l, woh, wol, eh, el, ah, al)
        )

    out = None
    for v in range(pairs):
        field = fields[v]
        fx = halo(lambda dim, side: strip(field, dim, side))
        at = functools.partial(lambda v, i: (v, 0, 0, 0), v)
        block = pl.BlockSpec((1, tile_x, tile_y, levels), at)
        carry = [] if out is None else [out]
        out = call(
            finish_kernel,
            shaped(vectors.shape),
            flops=40 * tall * around * deep,
            moved=12 * cells * deep,
            scratch=[
                pltpu.VMEM((tall, around, deep), F32),
                pltpu.VMEM((2, tall, around, LANES), F32),
                pltpu.VMEM((tile_x, tile_y, deep), F32),
            ],
            grid=(1,),
            in_specs=[whole, block] + [whole] * 5 + [pl.BlockSpec(memory_space=pl.ANY)] * len(carry),
            out_specs=block,
            input_output_aliases={7: 0} if carry else {},
        )(field, vectors, *fx, spread, *carry)
    return out


def solution(mesh):
    in_specs = (
        P(None, "gx", "gy", None),
        P("gx", "gy"),
        P(),
        P(),
        P(),
        P(),
        P(),
        P(),
        P(),
        P(("gx", "gy")),
        P(("gx", "gy")),
        P(("gx", "gy"), None),
        P(),
    )
    out_specs = P(None, "gx", "gy", None)
    return jax.shard_map(body, mesh=mesh, in_specs=in_specs, out_specs=out_specs, check_vma=False)
```

```python
import functools

import jax
import jax.numpy as jnp
from jax import lax
from jax.experimental import pallas as pl
from jax.experimental.pallas import tpu as pltpu
from jax.sharding import PartitionSpec as P

SWEEPS = 4
WIDE = 256
LANES = 128
BF = jnp.bfloat16
F32 = jnp.float32
NN = ((1,), (0,))
NT = ((1,), (1,))


def up(size, unit):
    return -(-size // unit) * unit


def split(value):
    high = value.astype(BF)
    return high, (value - high.astype(F32)).astype(BF)


def mm(left, right, dims=NN):
    return lax.dot_general(left, right, (dims, ((), ())), preferred_element_type=F32)


def mm3(left_high, left_low, right_high, right_low, dims=NN):
    return mm(left_high, right_high, dims) + (
        mm(left_high, right_low, dims) + mm(left_low, right_high, dims)
    )


def columns(size):
    return [pl.ds(start, WIDE) for start in range(0, size, WIDE)]


def iota(shape, axis):
    return lax.broadcasted_iota(jnp.int32, shape, axis)


def call(kernel, out_shape, flops, moved, scratch=(), vmem=48, **more):
    return pl.pallas_call(
        kernel,
        out_shape=out_shape,
        scratch_shapes=list(scratch),
        compiler_params=pltpu.CompilerParams(vmem_limit_bytes=vmem * 1024 * 1024),
        cost_estimate=pl.CostEstimate(flops=flops, bytes_accessed=moved, transcendentals=0),
        **more,
    )


def shaped(shape, dtype=F32):
    return jax.ShapeDtypeStruct(shape, dtype)


def pack_kernel(bucket, dest_ref, cell_ref, state_ref, out_ref, high_ref, low_ref):
    levels, slots = state_ref.shape
    devices = slots // bucket
    dest = dest_ref[...]
    same = (iota((devices, slots), 0) == dest).astype(F32)
    before = (iota((slots, slots), 0) < iota((slots, slots), 1)).astype(BF)
    rank = jnp.sum(same * mm(same.astype(BF), before), axis=0, keepdims=True)
    place = dest * bucket + rank.astype(jnp.int32)
    pick = (iota((slots, slots), 0) == place).astype(BF)
    high_ref[...] = jnp.zeros_like(high_ref)
    low_ref[...] = jnp.zeros_like(low_ref)
    high, low = split(state_ref[...])
    high_ref[:levels, :] = high
    low_ref[:levels, :] = low
    mark = up(levels, 16)
    tall = jnp.where(iota((16, slots), 0) == 0, cell_ref[...], 0.0)
    high, low = split(tall)
    high_ref[mark : mark + 16, :] = high
    low_ref[mark : mark + 16, :] = low
    out_ref[...] = mm(pick, high_ref[...], NT) + mm(pick, low_ref[...], NT)


def prep_kernel(factor_ref, first_ref, second_ref, out_t_ref, error_ref, *refs):
    outs, (pad_a, pad_b) = refs[:10], refs[10:]

    def put(values, high_ref, low_ref):
        rows, cols = values.shape
        if (rows, cols) != high_ref.shape:
            high_ref[...] = jnp.zeros_like(high_ref)
            low_ref[...] = jnp.zeros_like(low_ref)
        high, low = split(values)
        high_ref[:rows, :cols] = high
        low_ref[:rows, :cols] = low

    put(first_ref[...], outs[0], outs[1])
    put(second_ref[...], outs[2], outs[3])
    put(out_t_ref[...], outs[4], outs[5])
    put(error_ref[...], outs[6], outs[7])
    put(factor_ref[...].T, pad_a, pad_b)
    rows = pad_a.shape[1]
    for cols in columns(outs[8].shape[1]):
        got = mm3(pad_a[...], pad_b[...], outs[0][:rows, cols], outs[1][:rows, cols])
        high, low = split(got)
        outs[8][:, cols] = high
        outs[9][:, cols] = low


def fill(ext, tile, xlo, xhi, beside, clo, chi):
    rows, wide, levels = tile.shape
    w = SWEEPS
    last = up(levels, LANES) - LANES
    ext[:, :, last:] = jnp.zeros((ext.shape[0], ext.shape[1], ext.shape[2] - last), F32)
    ext[w : w + rows, :wide, :levels] = tile
    ext[:w, :wide, :levels] = xlo[:, :, :levels]
    ext[w + rows :, :wide, :levels] = xhi[:, :, :levels]
    ext[w : w + rows, wide:, :levels] = beside[:, :, :levels]
    ext[:w, wide:, :levels] = clo[:, :, :levels]
    ext[w + rows :, wide:, :levels] = chi[:, :, :levels]


def diffuse_kernel(given, tile_ref, coeff_ref, *refs):
    strips, (ahigh_ref, alow_ref), refs = refs[:5], refs[5:7], refs[7:]
    ext, work, high_ref, low_ref = refs[-4:]
    out_ref = refs[0]
    w = SWEEPS
    rows, wide, levels = tile_ref.shape[1:]
    tall = rows + 2 * w
    around = wide + 2 * w
    fill(ext, tile_ref[0], *strips)
    if given:
        cb_ref = coeff_ref
    else:
        cb_ref = refs[1]

        def spread(ref):
            column = ref[:, :, levels : levels + 1]
            return jnp.broadcast_to(column, column.shape[:2] + (LANES,))

        xlo, xhi, beside, clo, chi = strips
        cb_ref[w : w + rows, :wide, :] = coeff_ref[...]
        cb_ref[:w, :wide, :] = spread(xlo)
        cb_ref[w + rows :, :wide, :] = spread(xhi)
        cb_ref[w : w + rows, wide:, :] = spread(beside)
        cb_ref[:w, wide:, :] = spread(clo)
        cb_ref[w + rows :, wide:, :] = spread(chi)

    def chunk(j, _):
        lanes = pl.ds(pl.multiple_of(j * LANES, LANES), LANES)
        for sweep in range(SWEEPS):
            for i in range(sweep + 1, tall - 1 - sweep):
                if sweep == 0:
                    above, mid, below = (ext[k, :, lanes] for k in (i - 1, i, i + 1))
                else:
                    above, mid, below = (work[(sweep + 1) % 2, k] for k in (i - 1, i, i + 1))
                beside = above + below + pltpu.roll(mid, 1, 0) + pltpu.roll(mid, around - 1, 0)
                new = mid + cb_ref[i] * (beside - 4.0 * mid)
                if sweep == SWEEPS - 1:
                    high, low = split(new[:wide])
                    here = pl.ds((i - w) * wide, wide)
                    high_ref[here, lanes] = high
                    low_ref[here, lanes] = low
                else:
                    work[sweep % 2, i] = new
        return 0

    lax.fori_loop(0, ext.shape[2] // LANES, chunk, 0)
    deep = ext.shape[2]
    for cols in columns(out_ref.shape[1]):
        out_ref[:, cols] = mm3(
            high_ref[...], low_ref[...], ahigh_ref[:deep, cols], alow_ref[:deep, cols]
        )


def hidden_kernel(
    mark, bucket, x_ref, w1h, w1l, b1_ref, w2h, w2l, b2_ref, mask_ref,
    s1_ref, s2_ref, gate_ref, one_ref, one_t_ref, high_ref, low_ref,
):
    slots, deep = x_ref.shape
    cells = one_ref.shape[1]
    devices, channels = mask_ref.shape
    index = x_ref[:, mark : mark + 1]
    cell = index.astype(jnp.int32) - 1
    live = index > 0.5
    one_ref[...] = (iota((slots, cells), 1) == cell).astype(BF)
    flat = jnp.broadcast_to(index, (slots, LANES)).T[0:1, :].astype(jnp.int32) - 1
    one_t_ref[...] = (iota((cells, slots), 0) == flat).astype(BF)
    first = iota((slots, devices), 1) * bucket
    at = iota((slots, devices), 0)
    from_owner = ((at >= first) & (at < first + bucket) & live).astype(BF)
    gate_ref[...] = jnp.zeros_like(gate_ref)
    gate_ref[:, :channels] = mm(from_owner, mask_ref[...].astype(F32).astype(BF))
    high, low = split(x_ref[...])
    high_ref[:, :deep] = high
    low_ref[:, :deep] = low
    units = s1_ref.shape[1]

    for cols in columns(units):
        got = mm3(high_ref[:, :deep], low_ref[:, :deep], w1h[:deep, cols], w1l[:deep, cols])
        hidden = jnp.tanh(got + b1_ref[:, cols])
        s1_ref[:, cols] = 1.0 - hidden * hidden
        s2_ref[:, cols] = hidden
    high, low = split(s2_ref[...])
    high_ref[...] = high
    low_ref[...] = low
    for cols in columns(units):
        got = mm3(high_ref[...], low_ref[...], w2h[:, cols], w2l[:, cols])
        hidden = jnp.tanh(got + b2_ref[:, cols])
        s2_ref[:, cols] = 1.0 - hidden * hidden


def net_kernel(
    q_ref, one_ref, one_t_ref, s1_ref, s2_ref, gate_ref,
    w2h, w2l, woh, wol, eh, el, ah, al,
    out_ref, xhead, xtail, yhead, ytail, x1h, x1l, x2h, x2l,
):
    units = s1_ref.shape[1]

    def store(pair, cols, value):
        high, low = split(value)
        pair[0][:, cols] = high
        pair[1][:, cols] = low

    def layer(source, weights, scale, target, dims, size):
        for cols in columns(size):
            if dims == NN:
                right = (weights[0][:, cols], weights[1][:, cols])
            else:
                right = (weights[0][cols, :], weights[1][cols, :])
            got = mm3(source[0][...], source[1][...], *right, dims)
            store(target, cols, got * scale[:, cols])

    def choose(source, picker, scale, target):
        for cols in columns(units):
            got = mm(picker[...], source[0][:, cols]) + mm(picker[...], source[1][:, cols])
            store(target, cols, got if scale is None else got * scale[:, cols])

    one, two = (x1h, x1l), (x2h, x2l)
    for cols in columns(units):
        store(one, cols, q_ref[:, cols])
    choose(one, one_ref, s1_ref, two)
    layer(two, (w2h, w2l), s2_ref, one, NN, units)
    layer(one, (woh, wol), gate_ref, two, NT, woh.shape[0])
    layer(two, (eh, el), gate_ref, one, NN, eh.shape[1])
    layer(one, (woh, wol), s2_ref, two, NN, units)
    layer(two, (w2h, w2l), s1_ref, one, NT, units)
    choose(one, one_t_ref, None, two)
    rows, wide, levels = out_ref.shape
    for start in range(0, levels, WIDE):
        stop = min(start + WIDE, levels)
        here = pl.ds(start, WIDE)
        got = mm3(x2h[...], x2l[...], ah[here, :], al[here, :], NT)
        got = got.reshape(rows, wide, WIDE)[:, :, : stop - start]
        out_ref[:, :, start:stop] = got
        xhead[:, :, start:stop] = got[:SWEEPS]
        xtail[:, :, start:stop] = got[rows - SWEEPS :]
        yhead[:, :, start:stop] = got[:, :SWEEPS]
        ytail[:, :, start:stop] = got[:, wide - SWEEPS :]


def finish_kernel(field_ref, base_ref, cb_ref, *refs):
    out_ref, ext, work, total = refs[-4:]
    w = SWEEPS
    rows, wide, levels = field_ref.shape
    tall = rows + 2 * w
    fill(ext, field_ref[...], *refs[:5])
    around = wide + 2 * w

    def chunk(j, _):
        lanes = pl.ds(pl.multiple_of(j * LANES, LANES), LANES)
        for sweep in range(SWEEPS):

            def read(k):
                value = ext[k, :, lanes] if sweep == 0 else work[(sweep + 1) % 2, k]
                return value, cb_ref[k] * value

            above = read(sweep)
            mid = read(sweep + 1)
            for i in range(sweep + 1, tall - 1 - sweep):
                below = read(i + 1)
                scaled = mid[1]
                beside = (
                    above[1] + below[1]
                    + pltpu.roll(scaled, 1, 0) + pltpu.roll(scaled, around - 1, 0)
                )
                new = mid[0] + (beside - 4.0 * scaled)
                if sweep == SWEEPS - 1:
                    total[i - w, :, lanes] = new[:wide]
                else:
                    work[sweep % 2, i] = new
                above, mid = mid, below
        return 0

    lax.fori_loop(0, ext.shape[2] // LANES, chunk, 0)
    out_ref[0] = base_ref[0] + total[:, :, :levels]


def shift(value, axis, by):
    count = lax.axis_size(axis)
    return lax.ppermute(
        value, axis, [(i, i + by) for i in range(count) if 0 <= i + by < count]
    )


def halo(xhead, xtail, yhead, ytail):
    xlo = shift(xtail, "gx", 1)
    xhi = shift(xhead, "gx", -1)
    ylo = shift(ytail, "gy", 1)
    yhi = shift(yhead, "gy", -1)
    beside = jnp.concatenate([yhi, ylo], axis=1)
    clo = shift(strip(beside, 0, 1), "gx", 1)
    chi = shift(strip(beside, 0, 0), "gx", -1)
    return xlo, xhi, beside, clo, chi


def strip(array, axis, side):
    size = array.shape[axis]
    if side:
        return lax.slice_in_dim(array, size - SWEEPS, size, axis=axis)
    return lax.slice_in_dim(array, 0, SWEEPS, axis=axis)


def body(
    vectors, diffusivity, vertical_factor, weight_first, bias_first, weight_second,
    bias_second, weight_out, error_inverse, observed_column, owner_count,
    observed_state, channel_mask,
):
    pairs, tile_x, tile_y, levels = vectors.shape
    count_y = lax.axis_size("gy")
    devices = lax.axis_size("gx") * count_y
    slots = observed_column.shape[0]
    bucket = slots // devices
    cells = tile_x * tile_y
    grid_wide = tile_y * count_y
    units = weight_second.shape[0]
    deep = up(levels, LANES)
    tall, around = tile_x + 2 * SWEEPS, tile_y + 2 * SWEEPS
    full_l, full_u = up(levels, WIDE), up(units, WIDE)
    full_c = up(error_inverse.shape[0], WIDE)
    mark = up(levels, 16)

    def withc(dim, side):
        cut = strip(vectors[0], dim, side)
        return jnp.concatenate([cut, strip(diffusivity, dim, side)[:, :, None]], axis=-1)

    sides = ((0, 0), (0, 1), (1, 0), (1, 1))
    strips = [halo(*(withc(*side) for side in sides))]
    for v in range(1, pairs):
        strips.append(halo(*(strip(vectors[v], *side) for side in sides)))

    position = jnp.arange(slots, dtype=jnp.int32)
    grid_row = observed_column // grid_wide
    grid_col = observed_column % grid_wide
    target = grid_row // tile_x * count_y + grid_col // tile_y
    dest = jnp.where(position < owner_count[0], target, -1)
    cell = (grid_row % tile_x * tile_y + grid_col % tile_y + 1).astype(F32)
    packed = call(
        functools.partial(pack_kernel, bucket),
        shaped((slots, deep)),
        flops=6 * slots * slots * deep,
        moved=8 * slots * deep,
        scratch=[pltpu.VMEM((deep, slots), BF)] * 2,
    )(dest[None, :], cell[None, :], observed_state.T)
    carried = lax.all_to_all(
        packed.reshape(devices, bucket, deep), ("gx", "gy"), split_axis=0,
        concat_axis=0, tiled=True,
    ).reshape(slots, deep)

    sizes = [(full_l, full_u), (full_u, full_u), (full_c, full_u), (full_c, full_c), (full_l, full_u)]
    w1h, w1l, w2h, w2l, woh, wol, eh, el, ah, al = call(
        prep_kernel,
        [shaped(size, BF) for size in sizes for _ in range(2)],
        flops=6 * full_l * full_l * full_u,
        moved=8 * 5 * full_u * full_u,
        scratch=[pltpu.VMEM((full_l, full_l), BF)] * 2,
    )(vertical_factor, weight_first, weight_second, weight_out.T, error_inverse)

    coeff = jnp.broadcast_to(diffusivity[:, :, None], (tile_x, tile_y, LANES))
    whole = pl.BlockSpec(memory_space=pltpu.VMEM)

    def block(v):
        return pl.BlockSpec((1, tile_x, tile_y, levels), lambda i: (v, 0, 0, 0))

    queries = []
    for v in range(pairs):
        got = call(
            functools.partial(diffuse_kernel, v > 0),
            [shaped((cells, full_u))] + [shaped((tall, around, LANES))] * (v == 0),
            flops=6 * cells * deep * full_u,
            moved=8 * tall * around * deep,
            scratch=[
                pltpu.VMEM((tall, around, deep), F32),
                pltpu.VMEM((2, tall, around, LANES), F32),
                pltpu.VMEM((cells, deep), BF),
                pltpu.VMEM((cells, deep), BF),
            ],
            grid=(1,),
            in_specs=[block(v)] + [whole] * 8,
            out_specs=[whole] * (2 - (v > 0)),
        )(vectors, spread if v else coeff, *strips[v], ah, al)
        queries.append(got[0])
        if v == 0:
            spread = got[1]

    s1, s2, gate, one, one_t = call(
        functools.partial(hidden_kernel, mark, bucket),
        [
            shaped((slots, full_u)), shaped((slots, full_u)), shaped((slots, full_c)),
            shaped((slots, cells), BF), shaped((cells, slots), BF),
        ],
        flops=12 * slots * full_u * full_u,
        moved=8 * slots * full_u,
        scratch=[pltpu.VMEM((slots, full_u), BF)] * 2,
    )(carried, w1h, w1l, bias_first[None, :], w2h, w2l, bias_second[None, :], channel_mask)

    fields = []
    for v in range(pairs):
        fields.append(
            call(
                net_kernel,
                [shaped((tile_x, tile_y, levels))]
                + [shaped((SWEEPS, tile_y, levels))] * 2
                + [shaped((tile_x, SWEEPS, levels))] * 2,
                flops=36 * slots * full_u * full_u,
                moved=4 * 5 * full_u * full_u,
                scratch=[pltpu.VMEM((slots, full_u), BF)] * 4,
            )(queries[v], one, one_t, s1, s2, gate, w2h, w2l, woh, wol, eh, el, ah, al)
        )

    out = None
    for v in range(pairs):
        around_field = halo(*fields[v][1:])
        carry = [] if out is None else [out]
        out = call(
            finish_kernel,
            shaped(vectors.shape),
            flops=40 * tall * around * deep,
            moved=12 * cells * deep,
            scratch=[
                pltpu.VMEM((tall, around, deep), F32),
                pltpu.VMEM((2, tall, around, LANES), F32),
                pltpu.VMEM((tile_x, tile_y, deep), F32),
            ],
            grid=(1,),
            in_specs=[whole, block(v)] + [whole] * 6
            + [pl.BlockSpec(memory_space=pl.ANY)] * len(carry),
            out_specs=block(v),
            input_output_aliases={8: 0} if carry else {},
        )(fields[v][0], vectors, spread, *around_field, *carry)
    return out


def solution(mesh):
    in_specs = (
        P(None, "gx", "gy", None),
        P("gx", "gy"),
        P(),
        P(),
        P(),
        P(),
        P(),
        P(),
        P(),
        P(("gx", "gy")),
        P(("gx", "gy")),
        P(("gx", "gy"), None),
        P(),
    )
    out_specs = P(None, "gx", "gy", None)
    return jax.shard_map(body, mesh=mesh, in_specs=in_specs, out_specs=out_specs, check_vma=False)
```

```python
import functools

import jax
import jax.numpy as jnp
from jax import lax
from jax.experimental import pallas as pl
from jax.experimental.pallas import tpu as pltpu
from jax.sharding import PartitionSpec as P

SWEEPS = 4
WIDE = 256
LANES = 128
BF = jnp.bfloat16
F32 = jnp.float32
NN = ((1,), (0,))
NT = ((1,), (1,))


def up(size, unit):
    return -(-size // unit) * unit


def split(value):
    high = value.astype(BF)
    return high, (value - high.astype(F32)).astype(BF)


def mm(left, right, dims=NN):
    return lax.dot_general(left, right, (dims, ((), ())), preferred_element_type=F32)


def mm3(left_high, left_low, right_high, right_low, dims=NN):
    return mm(left_high, right_high, dims) + (
        mm(left_high, right_low, dims) + mm(left_low, right_high, dims)
    )


def halves(size):
    half = size // 2
    return [pl.ds(0, half), pl.ds(half, half)] if half % 16 == 0 else [pl.ds(0, size)]


def iota(shape, axis):
    return lax.broadcasted_iota(jnp.int32, shape, axis)


def call(kernel, out_shape, flops, moved, scratch=(), vmem=48, **more):
    return pl.pallas_call(
        kernel,
        out_shape=out_shape,
        scratch_shapes=list(scratch),
        compiler_params=pltpu.CompilerParams(vmem_limit_bytes=vmem * 1024 * 1024),
        cost_estimate=pl.CostEstimate(flops=flops, bytes_accessed=moved, transcendentals=0),
        **more,
    )


def shaped(shape, dtype=F32):
    return jax.ShapeDtypeStruct(shape, dtype)


def pack_kernel(bucket, dest_ref, cell_ref, state_ref, out_ref, high_ref, low_ref):
    levels, slots = state_ref.shape
    devices = slots // bucket
    dest = dest_ref[...]
    same = (iota((devices, slots), 0) == dest).astype(F32)
    before = (iota((slots, slots), 0) < iota((slots, slots), 1)).astype(BF)
    rank = jnp.sum(same * mm(same.astype(BF), before), axis=0, keepdims=True)
    place = dest * bucket + rank.astype(jnp.int32)
    pick = (iota((slots, slots), 0) == place).astype(BF)
    high_ref[...] = jnp.zeros_like(high_ref)
    low_ref[...] = jnp.zeros_like(low_ref)
    high, low = split(state_ref[...])
    high_ref[:levels, :] = high
    low_ref[:levels, :] = low
    mark = up(levels, 16)
    tall = jnp.where(iota((16, slots), 0) == 0, cell_ref[...], 0.0)
    high, low = split(tall)
    high_ref[mark : mark + 16, :] = high
    low_ref[mark : mark + 16, :] = low
    out_ref[...] = mm(pick, high_ref[...], NT) + mm(pick, low_ref[...], NT)


def prep_kernel(factor_ref, first_ref, second_ref, out_t_ref, error_ref, *refs):
    outs, (pad_a, pad_b) = refs[:10], refs[10:]

    def put(values, high_ref, low_ref):
        rows, cols = values.shape
        if (rows, cols) != high_ref.shape:
            high_ref[...] = jnp.zeros_like(high_ref)
            low_ref[...] = jnp.zeros_like(low_ref)
        high, low = split(values)
        high_ref[:rows, :cols] = high
        low_ref[:rows, :cols] = low

    put(first_ref[...], outs[0], outs[1])
    put(second_ref[...], outs[2], outs[3])
    put(out_t_ref[...], outs[4], outs[5])
    put(error_ref[...], outs[6], outs[7])
    put(factor_ref[...].T, pad_a, pad_b)
    rows = pad_a.shape[1]
    for part in halves(pad_a.shape[0]):
        got = mm3(pad_a[part, :], pad_b[part, :], outs[0][:rows, :], outs[1][:rows, :])
        high, low = split(got)
        outs[8][part, :] = high
        outs[9][part, :] = low


def cut_kernel(vectors_ref, coeff_ref, *outs):
    pairs, rows, wide, levels = vectors_ref.shape
    w = SWEEPS
    parts = (
        (slice(0, w), slice(None)), (slice(rows - w, rows), slice(None)),
        (slice(None), slice(0, w)), (slice(None), slice(wide - w, wide)),
    )
    for v in range(pairs):
        for k, part in enumerate(parts):
            out = outs[4 * v + k]
            out[:, :, :levels] = vectors_ref[(v,) + part]
            if v == 0:
                out[:, :, levels:] = coeff_ref[part][:, :, :1]


def fill(ext, tile, xlo, xhi, ylo, yhi):
    rows, wide, levels = tile.shape
    w = SWEEPS
    last = up(levels, LANES) - LANES
    ext[:, :, last:] = jnp.zeros((ext.shape[0], ext.shape[1], ext.shape[2] - last), F32)
    ext[w : w + rows, :wide, :levels] = tile
    ext[:w, :wide, :levels] = xlo[:, :, :levels]
    ext[w + rows :, :wide, :levels] = xhi[:, :, :levels]
    ext[:, wide : wide + w, :levels] = yhi[:, :, :levels]
    ext[:, wide + w :, :levels] = ylo[:, :, :levels]


def diffuse_kernel(given, tile_ref, coeff_ref, *refs):
    strips, (ahigh_ref, alow_ref), refs = refs[:4], refs[4:6], refs[6:]
    ext, work, high_ref, low_ref = refs[-4:]
    out_ref = refs[0]
    w = SWEEPS
    rows, wide, levels = tile_ref.shape[1:]
    tall = rows + 2 * w
    around = wide + 2 * w
    fill(ext, tile_ref[0], *strips)
    if given:
        cb_ref = coeff_ref
    else:
        cb_ref = refs[1]

        def spread(ref):
            column = ref[:, :, levels : levels + 1]
            return jnp.broadcast_to(column, column.shape[:2] + (LANES,))

        xlo, xhi, ylo, yhi = strips
        cb_ref[w : w + rows, :wide, :] = coeff_ref[...]
        cb_ref[:w, :wide, :] = spread(xlo)
        cb_ref[w + rows :, :wide, :] = spread(xhi)
        cb_ref[:, wide : wide + w, :] = spread(yhi)
        cb_ref[:, wide + w :, :] = spread(ylo)

    def chunk(j, _):
        lanes = pl.ds(pl.multiple_of(j * LANES, LANES), LANES)
        for sweep in range(SWEEPS):
            for i in range(sweep + 1, tall - 1 - sweep):
                if sweep == 0:
                    above, mid, below = (ext[k, :, lanes] for k in (i - 1, i, i + 1))
                else:
                    above, mid, below = (work[(sweep + 1) % 2, k] for k in (i - 1, i, i + 1))
                beside = above + below + pltpu.roll(mid, 1, 0) + pltpu.roll(mid, around - 1, 0)
                new = mid + cb_ref[i] * (beside - 4.0 * mid)
                if sweep == SWEEPS - 1:
                    high, low = split(new[:wide])
                    here = pl.ds((i - w) * wide, wide)
                    high_ref[here, lanes] = high
                    low_ref[here, lanes] = low
                else:
                    work[sweep % 2, i] = new
        return 0

    lax.fori_loop(0, ext.shape[2] // LANES, chunk, 0)
    deep = ext.shape[2]
    for part in halves(out_ref.shape[0]):
        out_ref[part, :] = mm3(
            high_ref[part, :], low_ref[part, :], ahigh_ref[:deep, :], alow_ref[:deep, :]
        )


def hidden_kernel(
    mark, bucket, x_ref, w1h, w1l, b1_ref, w2h, w2l, b2_ref, mask_ref,
    s1_ref, s2_ref, gate_ref, one_ref, one_t_ref, high_ref, low_ref,
):
    slots, deep = x_ref.shape
    cells = one_ref.shape[1]
    devices, channels = mask_ref.shape
    index = x_ref[:, mark : mark + 1]
    cell = index.astype(jnp.int32) - 1
    live = index > 0.5
    one_ref[...] = (iota((slots, cells), 1) == cell).astype(BF)
    flat = jnp.broadcast_to(index, (slots, LANES)).T[0:1, :].astype(jnp.int32) - 1
    one_t_ref[...] = (iota((cells, slots), 0) == flat).astype(BF)
    first = iota((slots, devices), 1) * bucket
    at = iota((slots, devices), 0)
    from_owner = ((at >= first) & (at < first + bucket) & live).astype(BF)
    gate_ref[...] = jnp.zeros_like(gate_ref)
    gate_ref[:, :channels] = mm(from_owner, mask_ref[...].astype(F32).astype(BF))
    high, low = split(x_ref[...])
    high_ref[:, :deep] = high
    low_ref[:, :deep] = low

    parts = halves(slots)
    for part in parts:
        got = mm3(high_ref[part, :deep], low_ref[part, :deep], w1h[:deep, :], w1l[:deep, :])
        hidden = jnp.tanh(got + b1_ref[...])
        s1_ref[part, :] = 1.0 - hidden * hidden
        high, low = split(hidden)
        high_ref[part, :] = high
        low_ref[part, :] = low
    for part in parts:
        got = mm3(high_ref[part, :], low_ref[part, :], w2h[...], w2l[...])
        hidden = jnp.tanh(got + b2_ref[...])
        s2_ref[part, :] = 1.0 - hidden * hidden


def net_kernel(
    q_ref, one_ref, one_t_ref, s1_ref, s2_ref, gate_ref,
    w2h, w2l, woh, wol, eh, el, ah, al,
    out_ref, xhead, xtail, yhead, ytail, x1h, x1l, x2h, x2l,
):
    def store(pair, part, value):
        high, low = split(value)
        pair[0][part, :] = high
        pair[1][part, :] = low

    def layer(source, weights, scale, target, dims):
        for part in halves(scale.shape[0]):
            got = mm3(source[0][part, :], source[1][part, :], *weights, dims)
            store(target, part, got * scale[part, :])

    def choose(source, picker, scale, target):
        for part in halves(picker.shape[0]):
            got = mm(picker[part, :], source[0][...]) + mm(picker[part, :], source[1][...])
            store(target, part, got if scale is None else got * scale[part, :])

    one, two = (x1h, x1l), (x2h, x2l)
    second = (w2h[...], w2l[...])
    last = (woh[...], wol[...])
    store(one, pl.ds(0, q_ref.shape[0]), q_ref[...])
    choose(one, one_ref, s1_ref, two)
    layer(two, second, s2_ref, one, NN)
    layer(one, last, gate_ref, two, NT)
    layer(two, (eh[...], el[...]), gate_ref, one, NN)
    layer(one, last, s2_ref, two, NN)
    layer(two, second, s1_ref, one, NT)
    choose(one, one_t_ref, None, two)
    rows, wide, levels = out_ref.shape
    for k, part in enumerate(halves(x2h.shape[0])):
        got = mm3(x2h[part, :], x2l[part, :], ah[...], al[...], NT)
        tall = got.shape[0] // wide
        got = got.reshape(tall, wide, got.shape[1])[:, :, :levels]
        here = pl.ds(k * tall, tall)
        out_ref[here] = got
        if k == 0:
            xhead[...] = got[:SWEEPS]
        if (k + 1) * tall == rows:
            xtail[...] = got[tall - SWEEPS :]
        yhead[here] = got[:, :SWEEPS]
        ytail[here] = got[:, wide - SWEEPS :]


def finish_kernel(field_ref, base_ref, cb_ref, *refs):
    out_ref, ext, work, total = refs[-4:]
    w = SWEEPS
    rows, wide, levels = field_ref.shape
    tall = rows + 2 * w
    fill(ext, field_ref[...], *refs[:4])
    around = wide + 2 * w

    def chunk(j, _):
        lanes = pl.ds(pl.multiple_of(j * LANES, LANES), LANES)
        for sweep in range(SWEEPS):

            def read(k):
                value = ext[k, :, lanes] if sweep == 0 else work[(sweep + 1) % 2, k]
                return value, cb_ref[k] * value

            above = read(sweep)
            mid = read(sweep + 1)
            for i in range(sweep + 1, tall - 1 - sweep):
                below = read(i + 1)
                scaled = mid[1]
                beside = (
                    above[1] + below[1]
                    + pltpu.roll(scaled, 1, 0) + pltpu.roll(scaled, around - 1, 0)
                )
                new = mid[0] + (beside - 4.0 * scaled)
                if sweep == SWEEPS - 1:
                    total[i - w, :, lanes] = new[:wide]
                else:
                    work[sweep % 2, i] = new
                above, mid = mid, below
        return 0

    lax.fori_loop(0, ext.shape[2] // LANES, chunk, 0)
    out_ref[0] = base_ref[0] + total[:, :, :levels]


def shift(value, axis, by):
    count = lax.axis_size(axis)
    return lax.ppermute(
        value, axis, [(i, i + by) for i in range(count) if 0 <= i + by < count]
    )


def halo(xhead, xtail, yhead, ytail):
    xlo = shift(xtail, "gx", 1)
    xhi = shift(xhead, "gx", -1)
    last = jnp.concatenate([xlo[:, -SWEEPS:], ytail, xhi[:, -SWEEPS:]], axis=0)
    head = jnp.concatenate([xlo[:, :SWEEPS], yhead, xhi[:, :SWEEPS]], axis=0)
    ylo = shift(last, "gy", 1)
    yhi = shift(head, "gy", -1)
    return xlo, xhi, ylo, yhi


def body(
    vectors, diffusivity, vertical_factor, weight_first, bias_first, weight_second,
    bias_second, weight_out, error_inverse, observed_column, owner_count,
    observed_state, channel_mask,
):
    pairs, tile_x, tile_y, levels = vectors.shape
    count_y = lax.axis_size("gy")
    devices = lax.axis_size("gx") * count_y
    slots = observed_column.shape[0]
    bucket = slots // devices
    cells = tile_x * tile_y
    grid_wide = tile_y * count_y
    units = weight_second.shape[0]
    deep = up(levels, LANES)
    tall, around = tile_x + 2 * SWEEPS, tile_y + 2 * SWEEPS
    full_l, full_u = up(levels, WIDE), up(units, WIDE)
    full_c = up(error_inverse.shape[0], WIDE)
    mark = up(levels, 16)

    coeff = jnp.broadcast_to(diffusivity[:, :, None], (tile_x, tile_y, LANES))
    shapes = []
    for v in range(pairs):
        deep_v = levels + (v == 0)
        shapes += [shaped((SWEEPS, tile_y, deep_v))] * 2 + [shaped((tile_x, SWEEPS, deep_v))] * 2
    cuts = call(cut_kernel, shapes, flops=0, moved=8 * vectors.size, vmem=16)(vectors, coeff)
    strips = [halo(*cuts[4 * v : 4 * v + 4]) for v in range(pairs)]

    position = jnp.arange(slots, dtype=jnp.int32)
    grid_row = observed_column // grid_wide
    grid_col = observed_column % grid_wide
    target = grid_row // tile_x * count_y + grid_col // tile_y
    dest = jnp.where(position < owner_count[0], target, -1)
    cell = (grid_row % tile_x * tile_y + grid_col % tile_y + 1).astype(F32)
    packed = call(
        functools.partial(pack_kernel, bucket),
        shaped((slots, deep)),
        flops=6 * slots * slots * deep,
        moved=8 * slots * deep,
        scratch=[pltpu.VMEM((deep, slots), BF)] * 2,
        vmem=12,
    )(dest[None, :], cell[None, :], observed_state.T)
    carried = lax.all_to_all(
        packed.reshape(devices, bucket, deep), ("gx", "gy"), split_axis=0,
        concat_axis=0, tiled=True,
    ).reshape(slots, deep)

    sizes = [(full_l, full_u), (full_u, full_u), (full_c, full_u), (full_c, full_c), (full_l, full_u)]
    w1h, w1l, w2h, w2l, woh, wol, eh, el, ah, al = call(
        prep_kernel,
        [shaped(size, BF) for size in sizes for _ in range(2)],
        flops=6 * full_l * full_l * full_u,
        moved=8 * 5 * full_u * full_u,
        scratch=[pltpu.VMEM((full_l, full_l), BF)] * 2,
        vmem=30,
    )(vertical_factor, weight_first, weight_second, weight_out.T, error_inverse)

    whole = pl.BlockSpec(memory_space=pltpu.VMEM)

    def block(v):
        return pl.BlockSpec((1, tile_x, tile_y, levels), lambda i: (v, 0, 0, 0))

    queries = []
    for v in range(pairs):
        got = call(
            functools.partial(diffuse_kernel, v > 0),
            [shaped((cells, full_u))] + [shaped((tall, around, LANES))] * (v == 0),
            flops=6 * cells * deep * full_u,
            moved=8 * tall * around * deep,
            scratch=[
                pltpu.VMEM((tall, around, deep), F32),
                pltpu.VMEM((2, tall, around, LANES), F32),
                pltpu.VMEM((cells, deep), BF),
                pltpu.VMEM((cells, deep), BF),
            ],
            grid=(1,),
            vmem=18,
            in_specs=[block(v)] + [whole] * 7,
            out_specs=[whole] * (2 - (v > 0)),
        )(vectors, spread if v else coeff, *strips[v], ah, al)
        queries.append(got[0])
        if v == 0:
            spread = got[1]

    s1, s2, gate, one, one_t = call(
        functools.partial(hidden_kernel, mark, bucket),
        [
            shaped((slots, full_u)), shaped((slots, full_u)), shaped((slots, full_c)),
            shaped((slots, cells), BF), shaped((cells, slots), BF),
        ],
        flops=12 * slots * full_u * full_u,
        moved=8 * slots * full_u,
        scratch=[pltpu.VMEM((slots, full_u), BF)] * 2,
        vmem=20,
    )(carried, w1h, w1l, bias_first[None, :], w2h, w2l, bias_second[None, :], channel_mask)

    fields = []
    for v in range(pairs):
        fields.append(
            call(
                net_kernel,
                [shaped((tile_x, tile_y, levels))]
                + [shaped((SWEEPS, tile_y, levels))] * 2
                + [shaped((tile_x, SWEEPS, levels))] * 2,
                flops=36 * slots * full_u * full_u,
                moved=4 * 5 * full_u * full_u,
                scratch=[pltpu.VMEM((slots, full_u), BF)] * 4,
                vmem=26,
            )(queries[v], one, one_t, s1, s2, gate, w2h, w2l, woh, wol, eh, el, ah, al)
        )

    out = None
    for v in range(pairs):
        around_field = halo(*fields[v][1:])
        carry = [] if out is None else [out]
        out = call(
            finish_kernel,
            shaped(vectors.shape),
            flops=40 * tall * around * deep,
            moved=12 * cells * deep,
            scratch=[
                pltpu.VMEM((tall, around, deep), F32),
                pltpu.VMEM((2, tall, around, LANES), F32),
                pltpu.VMEM((tile_x, tile_y, deep), F32),
            ],
            grid=(1,),
            vmem=18,
            in_specs=[whole, block(v)] + [whole] * 5
            + [pl.BlockSpec(memory_space=pl.ANY)] * len(carry),
            out_specs=block(v),
            input_output_aliases={7: 0} if carry else {},
        )(fields[v][0], vectors, spread, *around_field, *carry)
    return out


def solution(mesh):
    in_specs = (
        P(None, "gx", "gy", None),
        P("gx", "gy"),
        P(),
        P(),
        P(),
        P(),
        P(),
        P(),
        P(),
        P(("gx", "gy")),
        P(("gx", "gy")),
        P(("gx", "gy"), None),
        P(),
    )
    out_specs = P(None, "gx", "gy", None)
    return jax.shard_map(body, mesh=mesh, in_specs=in_specs, out_specs=out_specs, check_vma=False)
```

```python
import functools

import jax
import jax.numpy as jnp
from jax import lax
from jax.experimental import pallas as pl
from jax.experimental.pallas import tpu as pltpu
from jax.sharding import PartitionSpec as P

SWEEPS = 4
WIDE = 256
LANES = 128
BF = jnp.bfloat16
F32 = jnp.float32
NN = ((1,), (0,))
NT = ((1,), (1,))


def up(size, unit):
    return -(-size // unit) * unit


def split(value):
    high = value.astype(BF)
    return high, (value - high.astype(F32)).astype(BF)


def mm(left, right, dims=NN):
    return lax.dot_general(left, right, (dims, ((), ())), preferred_element_type=F32)


def mm3(left_high, left_low, right_high, right_low, dims=NN):
    return mm(left_high, right_high, dims) + (
        mm(left_high, right_low, dims) + mm(left_low, right_high, dims)
    )


def halves(size):
    half = size // 2
    return [pl.ds(0, half), pl.ds(half, half)] if half % 16 == 0 else [pl.ds(0, size)]


def iota(shape, axis):
    return lax.broadcasted_iota(jnp.int32, shape, axis)


def call(kernel, out_shape, flops, moved, scratch=(), vmem=48, **more):
    return pl.pallas_call(
        kernel,
        out_shape=out_shape,
        scratch_shapes=list(scratch),
        compiler_params=pltpu.CompilerParams(vmem_limit_bytes=vmem * 1024 * 1024),
        cost_estimate=pl.CostEstimate(flops=flops, bytes_accessed=moved, transcendentals=0),
        **more,
    )


def shaped(shape, dtype=F32):
    return jax.ShapeDtypeStruct(shape, dtype)


def pack_kernel(bucket, dest_ref, cell_ref, state_ref, out_ref, high_ref, low_ref):
    levels, slots = state_ref.shape
    devices = slots // bucket
    dest = dest_ref[...]
    same = (iota((devices, slots), 0) == dest).astype(F32)
    before = (iota((slots, slots), 0) < iota((slots, slots), 1)).astype(BF)
    rank = jnp.sum(same * mm(same.astype(BF), before), axis=0, keepdims=True)
    place = dest * bucket + rank.astype(jnp.int32)
    pick = (iota((slots, slots), 0) == place).astype(BF)
    high_ref[...] = jnp.zeros_like(high_ref)
    low_ref[...] = jnp.zeros_like(low_ref)
    high, low = split(state_ref[...])
    high_ref[:levels, :] = high
    low_ref[:levels, :] = low
    mark = up(levels, 16)
    tall = jnp.where(iota((16, slots), 0) == 0, cell_ref[...], 0.0)
    high, low = split(tall)
    high_ref[mark : mark + 16, :] = high
    low_ref[mark : mark + 16, :] = low
    out_ref[...] = mm(pick, high_ref[...], NT) + mm(pick, low_ref[...], NT)


def prep_kernel(*refs):
    ins, (first_out, stack_out), refs = refs[:5], refs[5:7], refs[7:]
    raw, (first, stack, turned, in_sem, out_sem) = refs[:5], refs[5:]
    fetch = [
        pltpu.make_async_copy(ins[k], raw[k], in_sem.at[k]) for k in range(5)
    ]
    for copy in fetch:
        copy.start()
    sends = []

    def send(source, target):
        copy = pltpu.make_async_copy(source, target, out_sem.at[len(sends)])
        copy.start()
        sends.append(copy)

    def put(values, ref):
        rows, cols = values.shape
        if (rows, cols) != ref.shape[1:]:
            ref[...] = jnp.zeros_like(ref)
        ref[0, :rows, :cols], ref[1, :rows, :cols] = split(values)

    fetch[0].wait()
    put(raw[0][...].T, turned)
    fetch[1].wait()
    put(raw[1][...], first)
    send(first, first_out)
    deep = turned.shape[2]
    for part in halves(turned.shape[1]):
        got = mm3(turned[0, part, :], turned[1, part, :], first[0, :deep], first[1, :deep])
        stack[3, 0, part, :], stack[3, 1, part, :] = split(got)
    send(stack.at[3], stack_out.at[3])
    for k in range(3):
        fetch[k + 2].wait()
        put(raw[k + 2][...], stack.at[k])
        send(stack.at[k], stack_out.at[k])
    for copy in sends:
        copy.wait()


def cut_kernel(vectors_ref, coeff_ref, *outs):
    pairs, rows, wide, levels = vectors_ref.shape
    w = SWEEPS
    parts = (
        (slice(0, w), slice(None)), (slice(rows - w, rows), slice(None)),
        (slice(None), slice(0, w)), (slice(None), slice(wide - w, wide)),
    )
    for v in range(pairs):
        for k, part in enumerate(parts):
            out = outs[4 * v + k]
            out[:, :, :levels] = vectors_ref[(v,) + part]
            if v == 0:
                out[:, :, levels:] = coeff_ref[part][:, :, :1]


def fill(ext, tile, xlo, xhi, ylo, yhi):
    rows, wide, levels = tile.shape
    w = SWEEPS
    last = up(levels, LANES) - LANES
    ext[:, :, last:] = jnp.zeros((ext.shape[0], ext.shape[1], ext.shape[2] - last), F32)
    ext[w : w + rows, :wide, :levels] = tile
    ext[:w, :wide, :levels] = xlo[:, :, :levels]
    ext[w + rows :, :wide, :levels] = xhi[:, :, :levels]
    ext[:, wide : wide + w, :levels] = yhi[:, :, :levels]
    ext[:, wide + w :, :levels] = ylo[:, :, :levels]


def diffuse_kernel(given, tile_ref, coeff_ref, *refs):
    strips, stack_ref, refs = refs[:4], refs[4], refs[5:]
    ext, work, high_ref, low_ref, both, sem = refs[-6:]
    out_ref = refs[0]
    fetch = pltpu.make_async_copy(stack_ref.at[3], both, sem)
    fetch.start()
    w = SWEEPS
    rows, wide, levels = tile_ref.shape[1:]
    tall = rows + 2 * w
    around = wide + 2 * w
    fill(ext, tile_ref[0], *strips)
    if given:
        cb_ref = coeff_ref
    else:
        cb_ref = refs[1]

        def spread(ref):
            column = ref[:, :, levels : levels + 1]
            return jnp.broadcast_to(column, column.shape[:2] + (LANES,))

        xlo, xhi, ylo, yhi = strips
        cb_ref[w : w + rows, :wide, :] = coeff_ref[...]
        cb_ref[:w, :wide, :] = spread(xlo)
        cb_ref[w + rows :, :wide, :] = spread(xhi)
        cb_ref[:, wide : wide + w, :] = spread(yhi)
        cb_ref[:, wide + w :, :] = spread(ylo)

    def chunk(j, _):
        lanes = pl.ds(pl.multiple_of(j * LANES, LANES), LANES)
        for sweep in range(SWEEPS):
            for i in range(sweep + 1, tall - 1 - sweep):
                if sweep == 0:
                    above, mid, below = (ext[k, :, lanes] for k in (i - 1, i, i + 1))
                else:
                    above, mid, below = (work[(sweep + 1) % 2, k] for k in (i - 1, i, i + 1))
                beside = above + below + pltpu.roll(mid, 1, 0) + pltpu.roll(mid, around - 1, 0)
                new = mid + cb_ref[i] * (beside - 4.0 * mid)
                if sweep == SWEEPS - 1:
                    high, low = split(new[:wide])
                    here = pl.ds((i - w) * wide, wide)
                    high_ref[here, lanes] = high
                    low_ref[here, lanes] = low
                else:
                    work[sweep % 2, i] = new
        return 0

    lax.fori_loop(0, ext.shape[2] // LANES, chunk, 0)
    deep = ext.shape[2]
    fetch.wait()
    for part in halves(out_ref.shape[0]):
        out_ref[part, :] = mm3(
            high_ref[part, :], low_ref[part, :], both[0, :deep], both[1, :deep]
        )


def hidden_kernel(
    mark, bucket, x_ref, first_ref, b1_ref, stack_ref, b2_ref, mask_ref,
    scale_ref, one_ref, one_t_ref, high_ref, low_ref, first, second, sems,
):
    fetch_first = pltpu.make_async_copy(first_ref, first, sems.at[0])
    fetch_second = pltpu.make_async_copy(stack_ref.at[0], second, sems.at[1])
    fetch_first.start()
    fetch_second.start()
    s1_ref, s2_ref, gate_ref = (scale_ref.at[k] for k in range(3))
    slots, deep = x_ref.shape
    cells = one_ref.shape[1]
    devices, channels = mask_ref.shape
    index = x_ref[:, mark : mark + 1]
    cell = index.astype(jnp.int32) - 1
    live = index > 0.5
    one_ref[...] = (iota((slots, cells), 1) == cell).astype(BF)
    flat = jnp.broadcast_to(index, (slots, LANES)).T[0:1, :].astype(jnp.int32) - 1
    one_t_ref[...] = (iota((cells, slots), 0) == flat).astype(BF)
    begin = iota((slots, devices), 1) * bucket
    at = iota((slots, devices), 0)
    from_owner = ((at >= begin) & (at < begin + bucket) & live).astype(BF)
    gate_ref[...] = jnp.zeros_like(gate_ref)
    gate_ref[:, :channels] = mm(from_owner, mask_ref[...].astype(F32).astype(BF))
    high, low = split(x_ref[...])
    high_ref[:, :deep] = high
    low_ref[:, :deep] = low
    parts = halves(slots)
    fetch_first.wait()
    for part in parts:
        got = mm3(high_ref[part, :deep], low_ref[part, :deep], first[0, :deep], first[1, :deep])
        hidden = jnp.tanh(got + b1_ref[...])
        s1_ref[part, :] = 1.0 - hidden * hidden
        high, low = split(hidden)
        high_ref[part, :] = high
        low_ref[part, :] = low
    fetch_second.wait()
    for part in parts:
        got = mm3(high_ref[part, :], low_ref[part, :], second[0], second[1])
        hidden = jnp.tanh(got + b2_ref[...])
        s2_ref[part, :] = 1.0 - hidden * hidden


LAYERS = ((0, 0, 1), (1, 1, 2), (2, 0, 2), (1, 0, 1), (0, 1, 0))


def table(values, layer):
    value = jnp.int32(values[0])
    for k in range(1, len(values)):
        value = jnp.where(layer == k, values[k], value)
    return value


def net_kernel(
    q_ref, one_ref, one_t_ref, scale_ref, stack_ref,
    out_ref, xhead, xtail, yhead, ytail, x1, top, low, acc_top, acc_low, stack, sems,
):
    fetch = [
        pltpu.make_async_copy(stack_ref.at[k], stack.at[k], sems.at[k]) for k in range(4)
    ]
    for copy in fetch:
        copy.start()
    slots = q_ref.shape[0]
    half = slots // 2
    first, second = pl.ds(0, half), pl.ds(half, half)

    def pick(picker):
        return mm(picker, x1[0]) + mm(picker, x1[1])

    def close(acc, scale, part, target):
        target[0], target[1] = split(acc[...] * scale_ref[scale, part, :])

    x1[0], x1[1] = split(q_ref[...])
    acc_top[...] = pick(one_ref[first, :])
    acc_low[...] = pick(one_ref[second, :])
    close(acc_top, 0, first, top)
    fetch[0].wait()
    scales = [0] + [entry[2] for entry in LAYERS]

    def step(layer, _):
        for k in (1, 2):

            @pl.when(layer == k)
            def _():
                fetch[k].wait()

        weight = table([entry[0] for entry in LAYERS], layer)
        turned = table([entry[1] for entry in LAYERS], layer)
        before, after = table(scales[:-1], layer), table(scales[1:], layer)

        def run(dims):
            acc_top[...] = mm3(top[0], top[1], stack[weight, 0], stack[weight, 1], dims)
            close(acc_low, before, second, low)
            acc_low[...] = mm3(low[0], low[1], stack[weight, 0], stack[weight, 1], dims)
            close(acc_top, after, first, top)

        @pl.when(turned == 0)
        def _():
            run(NN)

        @pl.when(turned == 1)
        def _():
            run(NT)

        return 0

    lax.fori_loop(0, len(LAYERS), step, 0)
    close(acc_low, scales[-1], second, low)
    for part in halves(one_t_ref.shape[0]):
        got = mm(one_t_ref[part, :half], top[0]) + mm(one_t_ref[part, :half], top[1])
        got = got + mm(one_t_ref[part, half:], low[0]) + mm(one_t_ref[part, half:], low[1])
        x1[0, part, :], x1[1, part, :] = split(got)
    fetch[3].wait()
    rows, wide, levels = out_ref.shape
    for k, part in enumerate(halves(rows * wide)):
        got = mm3(x1[0, part, :], x1[1, part, :], stack[3, 0], stack[3, 1], NT)
        tall = got.shape[0] // wide
        got = got.reshape(tall, wide, got.shape[1])[:, :, :levels]
        here = pl.ds(k * tall, tall)
        out_ref[here] = got
        if k == 0:
            xhead[...] = got[:SWEEPS]
        if (k + 1) * tall == rows:
            xtail[...] = got[tall - SWEEPS :]
        yhead[here] = got[:, :SWEEPS]
        ytail[here] = got[:, wide - SWEEPS :]


def finish_kernel(field_ref, base_ref, cb_ref, *refs):
    out_ref, ext, work, total = refs[-4:]
    w = SWEEPS
    rows, wide, levels = field_ref.shape
    tall = rows + 2 * w
    fill(ext, field_ref[...], *refs[:4])
    around = wide + 2 * w

    def chunk(j, _):
        lanes = pl.ds(pl.multiple_of(j * LANES, LANES), LANES)
        for sweep in range(SWEEPS):

            def read(k):
                value = ext[k, :, lanes] if sweep == 0 else work[(sweep + 1) % 2, k]
                return value, cb_ref[k] * value

            above = read(sweep)
            mid = read(sweep + 1)
            for i in range(sweep + 1, tall - 1 - sweep):
                below = read(i + 1)
                scaled = mid[1]
                beside = (
                    above[1] + below[1]
                    + pltpu.roll(scaled, 1, 0) + pltpu.roll(scaled, around - 1, 0)
                )
                new = mid[0] + (beside - 4.0 * scaled)
                if sweep == SWEEPS - 1:
                    total[i - w, :, lanes] = new[:wide]
                else:
                    work[sweep % 2, i] = new
                above, mid = mid, below
        return 0

    lax.fori_loop(0, ext.shape[2] // LANES, chunk, 0)
    out_ref[0] = base_ref[0] + total[:, :, :levels]


def shift(value, axis, by):
    count = lax.axis_size(axis)
    return lax.ppermute(
        value, axis, [(i, i + by) for i in range(count) if 0 <= i + by < count]
    )


def halo(xhead, xtail, yhead, ytail):
    xlo = shift(xtail, "gx", 1)
    xhi = shift(xhead, "gx", -1)
    last = jnp.concatenate([xlo[:, -SWEEPS:], ytail, xhi[:, -SWEEPS:]], axis=0)
    head = jnp.concatenate([xlo[:, :SWEEPS], yhead, xhi[:, :SWEEPS]], axis=0)
    ylo = shift(last, "gy", 1)
    yhi = shift(head, "gy", -1)
    return xlo, xhi, ylo, yhi


def body(
    vectors, diffusivity, vertical_factor, weight_first, bias_first, weight_second,
    bias_second, weight_out, error_inverse, observed_column, owner_count,
    observed_state, channel_mask,
):
    pairs, tile_x, tile_y, levels = vectors.shape
    count_y = lax.axis_size("gy")
    devices = lax.axis_size("gx") * count_y
    slots = observed_column.shape[0]
    bucket = slots // devices
    cells = tile_x * tile_y
    grid_wide = tile_y * count_y
    units = weight_second.shape[0]
    deep = up(levels, LANES)
    tall, around = tile_x + 2 * SWEEPS, tile_y + 2 * SWEEPS
    full_l, full_u = up(levels, WIDE), up(units, WIDE)
    full_c = up(error_inverse.shape[0], WIDE)
    mark = up(levels, 16)

    coeff = jnp.broadcast_to(diffusivity[:, :, None], (tile_x, tile_y, LANES))
    shapes = []
    for v in range(pairs):
        deep_v = levels + (v == 0)
        shapes += [shaped((SWEEPS, tile_y, deep_v))] * 2 + [shaped((tile_x, SWEEPS, deep_v))] * 2
    cuts = call(cut_kernel, shapes, flops=0, moved=8 * vectors.size, vmem=16)(vectors, coeff)
    strips = [halo(*cuts[4 * v : 4 * v + 4]) for v in range(pairs)]

    position = jnp.arange(slots, dtype=jnp.int32)
    grid_row = observed_column // grid_wide
    grid_col = observed_column % grid_wide
    target = grid_row // tile_x * count_y + grid_col // tile_y
    dest = jnp.where(position < owner_count[0], target, -1)
    cell = (grid_row % tile_x * tile_y + grid_col % tile_y + 1).astype(F32)
    packed = call(
        functools.partial(pack_kernel, bucket),
        shaped((slots, deep)),
        flops=6 * slots * slots * deep,
        moved=8 * slots * deep,
        scratch=[pltpu.VMEM((deep, slots), BF)] * 2,
        vmem=12,
    )(dest[None, :], cell[None, :], observed_state.T)
    carried = lax.all_to_all(
        packed.reshape(devices, bucket, deep), ("gx", "gy"), split_axis=0,
        concat_axis=0, tiled=True,
    ).reshape(slots, deep)

    side = max(full_l, full_u, full_c)
    far = pl.BlockSpec(memory_space=pltpu.HBM)
    weights = (vertical_factor, weight_first, weight_second, weight_out.T, error_inverse)
    first, stack = call(
        prep_kernel,
        [pltpu.HBM((2, full_l, side), BF), pltpu.HBM((4, 2, side, side), BF)],
        flops=6 * full_l * full_l * full_u,
        moved=8 * 5 * full_u * full_u,
        scratch=[pltpu.VMEM(weight.shape, F32) for weight in weights]
        + [
            pltpu.VMEM((2, full_l, side), BF), pltpu.VMEM((4, 2, side, side), BF),
            pltpu.VMEM((2, side, full_l), BF),
            pltpu.SemaphoreType.DMA((5,)), pltpu.SemaphoreType.DMA((5,)),
        ],
        vmem=34,
        in_specs=[far] * 5,
        out_specs=[far] * 2,
    )(*[pltpu.with_memory_space_constraint(weight, pltpu.HBM) for weight in weights])
    first, stack = (pltpu.with_memory_space_constraint(x, pltpu.HBM) for x in (first, stack))

    whole = pl.BlockSpec(memory_space=pltpu.VMEM)

    def wide_bias(bias):
        return jnp.pad(bias, (0, side - bias.shape[0]))[None, :]

    def block(v):
        return pl.BlockSpec((1, tile_x, tile_y, levels), lambda i: (v, 0, 0, 0))

    queries = []
    for v in range(pairs):
        got = call(
            functools.partial(diffuse_kernel, v > 0),
            [shaped((cells, side))] + [shaped((tall, around, LANES))] * (v == 0),
            flops=6 * cells * deep * full_u,
            moved=8 * tall * around * deep,
            scratch=[
                pltpu.VMEM((tall, around, deep), F32),
                pltpu.VMEM((2, tall, around, LANES), F32),
                pltpu.VMEM((cells, deep), BF),
                pltpu.VMEM((cells, deep), BF),
                pltpu.VMEM((2, side, side), BF),
                pltpu.SemaphoreType.DMA,
            ],
            grid=(1,),
            vmem=18,
            in_specs=[block(v)] + [whole] * 5 + [far],
            out_specs=[whole] * (2 - (v > 0)),
        )(vectors, spread if v else coeff, *strips[v], stack)
        queries.append(got[0])
        if v == 0:
            spread = got[1]

    scale, one, one_t = call(
        functools.partial(hidden_kernel, mark, bucket),
        [shaped((3, slots, side)), shaped((slots, cells), BF), shaped((cells, slots), BF)],
        flops=12 * slots * full_u * full_u,
        moved=8 * slots * full_u,
        scratch=[pltpu.VMEM((slots, side), BF)] * 2
        + [
            pltpu.VMEM((2, full_l, side), BF), pltpu.VMEM((2, side, side), BF),
            pltpu.SemaphoreType.DMA((2,)),
        ],
        vmem=24,
        in_specs=[whole, far, whole, far, whole, whole],
    )(carried, first, wide_bias(bias_first), stack, wide_bias(bias_second), channel_mask)

    fields = []
    for v in range(pairs):
        fields.append(
            call(
                net_kernel,
                [shaped((tile_x, tile_y, levels))]
                + [shaped((SWEEPS, tile_y, levels))] * 2
                + [shaped((tile_x, SWEEPS, levels))] * 2,
                flops=36 * slots * full_u * full_u,
                moved=4 * 5 * full_u * full_u,
                scratch=[pltpu.VMEM((2, slots, side), BF)]
                + [pltpu.VMEM((2, slots // 2, side), BF)] * 2
                + [pltpu.VMEM((slots // 2, side), F32)] * 2
                + [
                    pltpu.VMEM((4, 2, side, side), BF),
                    pltpu.SemaphoreType.DMA((4,)),
                ],
                vmem=30,
                in_specs=[whole] * 4 + [far],
            )(queries[v], one, one_t, scale, stack)
        )

    out = None
    for v in range(pairs):
        around_field = halo(*fields[v][1:])
        carry = [] if out is None else [out]
        out = call(
            finish_kernel,
            shaped(vectors.shape),
            flops=40 * tall * around * deep,
            moved=12 * cells * deep,
            scratch=[
                pltpu.VMEM((tall, around, deep), F32),
                pltpu.VMEM((2, tall, around, LANES), F32),
                pltpu.VMEM((tile_x, tile_y, deep), F32),
            ],
            grid=(1,),
            vmem=18,
            in_specs=[whole, block(v)] + [whole] * 5
            + [pl.BlockSpec(memory_space=pl.ANY)] * len(carry),
            out_specs=block(v),
            input_output_aliases={7: 0} if carry else {},
        )(fields[v][0], vectors, spread, *around_field, *carry)
    return out


def solution(mesh):
    in_specs = (
        P(None, "gx", "gy", None),
        P("gx", "gy"),
        P(),
        P(),
        P(),
        P(),
        P(),
        P(),
        P(),
        P(("gx", "gy")),
        P(("gx", "gy")),
        P(("gx", "gy"), None),
        P(),
    )
    out_specs = P(None, "gx", "gy", None)
    return jax.shard_map(body, mesh=mesh, in_specs=in_specs, out_specs=out_specs, check_vma=False)
```

```python
import functools

import jax
import jax.numpy as jnp
from jax import lax
from jax.experimental import pallas as pl
from jax.experimental.pallas import tpu as pltpu
from jax.sharding import PartitionSpec as P

SWEEPS = 4
WIDE = 256
LANES = 128
BF = jnp.bfloat16
F32 = jnp.float32
NN = ((1,), (0,))
NT = ((1,), (1,))


def up(size, unit):
    return -(-size // unit) * unit


def split(value):
    high = value.astype(BF)
    return high, (value - high.astype(F32)).astype(BF)


def mm(left, right, dims=NN):
    return lax.dot_general(left, right, (dims, ((), ())), preferred_element_type=F32)


def mm3(left_high, left_low, right_high, right_low, dims=NN):
    return mm(left_high, right_high, dims) + (
        mm(left_high, right_low, dims) + mm(left_low, right_high, dims)
    )


def halves(size):
    half = size // 2
    return [pl.ds(0, half), pl.ds(half, half)] if half % 16 == 0 else [pl.ds(0, size)]


def iota(shape, axis):
    return lax.broadcasted_iota(jnp.int32, shape, axis)


def call(kernel, out_shape, flops, moved, scratch=(), vmem=48, **more):
    return pl.pallas_call(
        kernel,
        out_shape=out_shape,
        scratch_shapes=list(scratch),
        compiler_params=pltpu.CompilerParams(vmem_limit_bytes=vmem * 1024 * 1024),
        cost_estimate=pl.CostEstimate(flops=flops, bytes_accessed=moved, transcendentals=0),
        **more,
    )


def shaped(shape, dtype=F32):
    return jax.ShapeDtypeStruct(shape, dtype)


def pack_kernel(bucket, dest_ref, cell_ref, state_ref, out_ref, high_ref, low_ref):
    levels, slots = state_ref.shape
    devices = slots // bucket
    dest = dest_ref[...]
    same = (iota((devices, slots), 0) == dest).astype(F32)
    before = (iota((slots, slots), 0) < iota((slots, slots), 1)).astype(BF)
    rank = jnp.sum(same * mm(same.astype(BF), before), axis=0, keepdims=True)
    place = dest * bucket + rank.astype(jnp.int32)
    pick = (iota((slots, slots), 0) == place).astype(BF)
    high_ref[...] = jnp.zeros_like(high_ref)
    low_ref[...] = jnp.zeros_like(low_ref)
    high, low = split(state_ref[...])
    high_ref[:levels, :] = high
    low_ref[:levels, :] = low
    mark = up(levels, 16)
    tall = jnp.where(iota((16, slots), 0) == 0, cell_ref[...], 0.0)
    high, low = split(tall)
    high_ref[mark : mark + 16, :] = high
    low_ref[mark : mark + 16, :] = low
    out_ref[...] = mm(pick, high_ref[...], NT) + mm(pick, low_ref[...], NT)


def prep_kernel(*refs):
    ins, (first_out, stack_out), refs = refs[:5], refs[5:7], refs[7:]
    raw, (first, stack, turned, in_sem, out_sem) = refs[:5], refs[5:]
    fetch = [
        pltpu.make_async_copy(ins[k], raw[k], in_sem.at[k]) for k in range(5)
    ]
    for copy in fetch:
        copy.start()
    sends = []

    def send(source, target):
        copy = pltpu.make_async_copy(source, target, out_sem.at[len(sends)])
        copy.start()
        sends.append(copy)

    def put(values, ref):
        rows, cols = values.shape
        if (rows, cols) != ref.shape[1:]:
            ref[...] = jnp.zeros_like(ref)
        ref[0, :rows, :cols], ref[1, :rows, :cols] = split(values)

    fetch[0].wait()
    put(raw[0][...].T, turned)
    fetch[1].wait()
    put(raw[1][...], first)
    send(first, first_out)
    deep = turned.shape[2]
    for part in halves(turned.shape[1]):
        got = mm3(turned[0, part, :], turned[1, part, :], first[0, :deep], first[1, :deep])
        stack[3, 0, part, :], stack[3, 1, part, :] = split(got)
    send(stack.at[3], stack_out.at[3])
    for k in range(3):
        fetch[k + 2].wait()
        put(raw[k + 2][...], stack.at[k])
        send(stack.at[k], stack_out.at[k])
    for copy in sends:
        copy.wait()


def coeff_column(coeff_ref, row):
    wide = coeff_ref.shape[1]
    spread = jnp.broadcast_to(coeff_ref[row : row + 1, :], (wide, wide))
    diagonal = iota((wide, wide), 0) == iota((wide, wide), 1)
    return jnp.sum(jnp.where(diagonal, spread, 0.0), axis=1, keepdims=True)


def cut_kernel(v, side_ref, vectors_ref, coeff_ref, xa, xb, yhead, ytail, *refs):
    bufs, sems = refs[:4], refs[4]
    rows, wide, levels = vectors_ref.shape[1:]
    w = SWEEPS
    parts = (
        vectors_ref.at[v, pl.ds(0, w)],
        vectors_ref.at[v, pl.ds(rows - w, w)],
        vectors_ref.at[v, :, pl.ds(0, 8)],
        vectors_ref.at[v, :, pl.ds(wide - 8, 8)],
    )
    copies = [pltpu.make_async_copy(parts[k], bufs[k], sems.at[k]) for k in range(4)]
    for copy in copies:
        copy.start()
    even = side_ref[0] == 0
    if v == 0:
        columns = [coeff_column(coeff_ref, row) for row in range(rows)]
        for row in range(w):
            head, tail = columns[row], columns[rows - w + row]
            xa[row, :, levels:] = jnp.where(even, tail, head)
            xb[row, :, levels:] = jnp.where(even, head, tail)
        for row in range(rows):
            yhead[row, :, levels:] = columns[row][:w]
            ytail[row, :, levels:] = columns[row][wide - w :]
    for copy in copies:
        copy.wait()
    head, tail = bufs[0][...], bufs[1][...]
    xa[:, :, :levels] = jnp.where(even, tail, head)
    xb[:, :, :levels] = jnp.where(even, head, tail)
    yhead[:, :, :levels] = bufs[2][:, :w]
    ytail[:, :, :levels] = bufs[3][:, 8 - w :]


def join_kernel(side_ref, ra, rb, yhead, ytail, ya, yb):
    w = SWEEPS
    rows = yhead.shape[0]
    wide = ra.shape[1]
    even_x, even_y = side_ref[0] == 0, side_ref[1] == 0

    for here, first, second in (
        (pl.ds(0, w), rb, ra),
        (pl.ds(w + rows, w), ra, rb),
    ):
        head = jnp.where(even_x, first[:, :w], second[:, :w])
        tail = jnp.where(even_x, first[:, wide - w :], second[:, wide - w :])
        ya[here] = jnp.where(even_y, tail, head)
        yb[here] = jnp.where(even_y, head, tail)
    here = pl.ds(w, rows)
    ya[here] = jnp.where(even_y, ytail[...], yhead[...])
    yb[here] = jnp.where(even_y, yhead[...], ytail[...])


def fill(ext, side_ref, tile, ra, rb, qa, qb, part):
    rows, wide = tile.shape[:2]
    w = SWEEPS
    even_y = side_ref[1] == 0
    upper = jnp.where(side_ref[0] == 0, w + rows, 0)
    tile_part, strip_part = part
    ext[w : w + rows, :wide, tile_part] = tile
    ext[pl.ds(upper, w), :wide, tile_part] = strip_part(ra)
    ext[pl.ds(w + rows - upper, w), :wide, tile_part] = strip_part(rb)
    qa, qb = strip_part(qa), strip_part(qb)
    ext[:, wide : wide + w, tile_part] = jnp.where(even_y, qa, qb)
    ext[:, wide + w :, tile_part] = jnp.where(even_y, qb, qa)


def fill_levels(ext, side_ref, tile, *strips):
    levels = tile.shape[2]
    last = up(levels, LANES) - LANES
    ext[:, :, last:] = jnp.zeros((ext.shape[0], ext.shape[1], ext.shape[2] - last), F32)
    part = (pl.ds(0, levels), lambda ref: ref[:, :, :levels])
    fill(ext, side_ref, tile, *strips, part)


def diffuse_kernel(given, side_ref, tile_ref, coeff_ref, *refs):
    strips, stack_ref, refs = refs[:4], refs[4], refs[5:]
    ext, work, high_ref, low_ref, both, sem = refs[-6:]
    out_ref = refs[0]
    fetch = pltpu.make_async_copy(stack_ref.at[3], both, sem)
    fetch.start()
    w = SWEEPS
    rows, wide, levels = tile_ref.shape[1:]
    tall = rows + 2 * w
    around = wide + 2 * w
    fill_levels(ext, side_ref, tile_ref[0], *strips)
    if given:
        cb_ref = coeff_ref
    else:
        cb_ref = refs[1]

        def spread(ref):
            column = ref[:, :, levels : levels + 1]
            return jnp.broadcast_to(column, column.shape[:2] + (LANES,))

        own = jnp.stack(
            [jnp.broadcast_to(coeff_column(coeff_ref, k), (wide, LANES)) for k in range(rows)]
        )
        fill(cb_ref, side_ref, own, *strips, (pl.ds(0, LANES), spread))

    def chunk(j, _):
        lanes = pl.ds(pl.multiple_of(j * LANES, LANES), LANES)
        for sweep in range(SWEEPS):
            for i in range(sweep + 1, tall - 1 - sweep):
                if sweep == 0:
                    above, mid, below = (ext[k, :, lanes] for k in (i - 1, i, i + 1))
                else:
                    above, mid, below = (work[(sweep + 1) % 2, k] for k in (i - 1, i, i + 1))
                beside = above + below + pltpu.roll(mid, 1, 0) + pltpu.roll(mid, around - 1, 0)
                new = mid + cb_ref[i] * (beside - 4.0 * mid)
                if sweep == SWEEPS - 1:
                    high, low = split(new[:wide])
                    here = pl.ds((i - w) * wide, wide)
                    high_ref[here, lanes] = high
                    low_ref[here, lanes] = low
                else:
                    work[sweep % 2, i] = new
        return 0

    lax.fori_loop(0, ext.shape[2] // LANES, chunk, 0)
    deep = ext.shape[2]
    fetch.wait()
    for part in halves(out_ref.shape[0]):
        out_ref[part, :] = mm3(
            high_ref[part, :], low_ref[part, :], both[0, :deep], both[1, :deep]
        )


def hidden_kernel(
    mark, bucket, x_ref, first_ref, b1_ref, stack_ref, b2_ref, mask_ref,
    scale_ref, one_ref, one_t_ref, high_ref, low_ref, first, second, sems,
):
    fetch_first = pltpu.make_async_copy(first_ref, first, sems.at[0])
    fetch_second = pltpu.make_async_copy(stack_ref.at[0], second, sems.at[1])
    fetch_first.start()
    fetch_second.start()
    s1_ref, s2_ref, gate_ref = (scale_ref.at[k] for k in range(3))
    slots, deep = x_ref.shape
    cells = one_ref.shape[1]
    devices, channels = mask_ref.shape
    index = x_ref[:, mark : mark + 1]
    cell = index.astype(jnp.int32) - 1
    live = index > 0.5
    one_ref[...] = (iota((slots, cells), 1) == cell).astype(BF)
    flat = jnp.broadcast_to(index, (slots, LANES)).T[0:1, :].astype(jnp.int32) - 1
    one_t_ref[...] = (iota((cells, slots), 0) == flat).astype(BF)
    begin = iota((slots, devices), 1) * bucket
    at = iota((slots, devices), 0)
    from_owner = ((at >= begin) & (at < begin + bucket) & live).astype(BF)
    gate_ref[...] = jnp.zeros_like(gate_ref)
    gate_ref[:, :channels] = mm(from_owner, mask_ref[...].astype(F32).astype(BF))
    high, low = split(x_ref[...])
    high_ref[:, :deep] = high
    low_ref[:, :deep] = low
    parts = halves(slots)
    fetch_first.wait()
    for part in parts:
        got = mm3(high_ref[part, :deep], low_ref[part, :deep], first[0, :deep], first[1, :deep])
        hidden = jnp.tanh(got + b1_ref[...])
        s1_ref[part, :] = 1.0 - hidden * hidden
        high, low = split(hidden)
        high_ref[part, :] = high
        low_ref[part, :] = low
    fetch_second.wait()
    for part in parts:
        got = mm3(high_ref[part, :], low_ref[part, :], second[0], second[1])
        hidden = jnp.tanh(got + b2_ref[...])
        s2_ref[part, :] = 1.0 - hidden * hidden


LAYERS = ((0, 0, 1), (1, 1, 2), (2, 0, 2), (1, 0, 1), (0, 1, 0))


def table(values, layer):
    value = jnp.int32(values[0])
    for k in range(1, len(values)):
        value = jnp.where(layer == k, values[k], value)
    return value


def net_kernel(
    side_ref, q_ref, one_ref, one_t_ref, scale_ref, stack_ref,
    out_ref, xa, xb, yhead, ytail, x1, top, low, acc_top, acc_low, stack, sems,
):
    fetch = [
        pltpu.make_async_copy(stack_ref.at[k], stack.at[k], sems.at[k]) for k in range(4)
    ]
    for copy in fetch:
        copy.start()
    slots = q_ref.shape[0]
    half = slots // 2
    first, second = pl.ds(0, half), pl.ds(half, half)

    def pick(picker):
        return mm(picker, x1[0]) + mm(picker, x1[1])

    def close(acc, scale, part, target):
        target[0], target[1] = split(acc[...] * scale_ref[scale, part, :])

    x1[0], x1[1] = split(q_ref[...])
    acc_top[...] = pick(one_ref[first, :])
    acc_low[...] = pick(one_ref[second, :])
    close(acc_top, 0, first, top)
    fetch[0].wait()
    scales = [0] + [entry[2] for entry in LAYERS]

    def step(layer, _):
        for k in (1, 2):

            @pl.when(layer == k)
            def _():
                fetch[k].wait()

        weight = table([entry[0] for entry in LAYERS], layer)
        turned = table([entry[1] for entry in LAYERS], layer)
        before, after = table(scales[:-1], layer), table(scales[1:], layer)

        def run(dims):
            acc_top[...] = mm3(top[0], top[1], stack[weight, 0], stack[weight, 1], dims)
            close(acc_low, before, second, low)
            acc_low[...] = mm3(low[0], low[1], stack[weight, 0], stack[weight, 1], dims)
            close(acc_top, after, first, top)

        @pl.when(turned == 0)
        def _():
            run(NN)

        @pl.when(turned == 1)
        def _():
            run(NT)

        return 0

    lax.fori_loop(0, len(LAYERS), step, 0)
    close(acc_low, scales[-1], second, low)
    for part in halves(one_t_ref.shape[0]):
        got = mm(one_t_ref[part, :half], top[0]) + mm(one_t_ref[part, :half], top[1])
        got = got + mm(one_t_ref[part, half:], low[0]) + mm(one_t_ref[part, half:], low[1])
        x1[0, part, :], x1[1, part, :] = split(got)
    fetch[3].wait()
    rows, wide, levels = out_ref.shape
    for k, part in enumerate(halves(rows * wide)):
        got = mm3(x1[0, part, :], x1[1, part, :], stack[3, 0], stack[3, 1], NT)
        tall = got.shape[0] // wide
        got = got.reshape(tall, wide, got.shape[1])[:, :, :levels]
        here = pl.ds(k * tall, tall)
        out_ref[here] = got
        yhead[here] = got[:, :SWEEPS]
        ytail[here] = got[:, wide - SWEEPS :]
    even = side_ref[0] == 0
    head, tail = out_ref[:SWEEPS], out_ref[rows - SWEEPS :]
    xa[...] = jnp.where(even, tail, head)
    xb[...] = jnp.where(even, head, tail)


def finish_kernel(side_ref, field_ref, base_ref, cb_ref, *refs):
    out_ref, ext, work, total = refs[-4:]
    w = SWEEPS
    rows, wide, levels = field_ref.shape
    tall = rows + 2 * w
    fill_levels(ext, side_ref, field_ref[...], *refs[:4])
    around = wide + 2 * w

    def chunk(j, _):
        lanes = pl.ds(pl.multiple_of(j * LANES, LANES), LANES)
        for sweep in range(SWEEPS):

            def read(k):
                value = ext[k, :, lanes] if sweep == 0 else work[(sweep + 1) % 2, k]
                return value, cb_ref[k] * value

            above = read(sweep)
            mid = read(sweep + 1)
            for i in range(sweep + 1, tall - 1 - sweep):
                below = read(i + 1)
                scaled = mid[1]
                beside = (
                    above[1] + below[1]
                    + pltpu.roll(scaled, 1, 0) + pltpu.roll(scaled, around - 1, 0)
                )
                new = mid[0] + (beside - 4.0 * scaled)
                if sweep == SWEEPS - 1:
                    total[i - w, :, lanes] = new[:wide]
                else:
                    work[sweep % 2, i] = new
                above, mid = mid, below
        return 0

    lax.fori_loop(0, ext.shape[2] // LANES, chunk, 0)
    out_ref[0] = base_ref[0] + total[:, :, :levels]


def swap(value, axis, start):
    pairs = [(i, i + 1) for i in range(start, lax.axis_size(axis) - 1, 2)]
    return lax.ppermute(value, axis, pairs + [(j, i) for i, j in pairs])


def halo(sides, xa, xb, yhead, ytail):
    ra = swap(xa, "gx", 0)
    rb = swap(xb, "gx", 1)
    whole = pl.BlockSpec(memory_space=pltpu.VMEM)
    tall = yhead.shape[0] + 2 * SWEEPS
    ya, yb = call(
        join_kernel,
        [shaped((tall,) + yhead.shape[1:])] * 2,
        flops=0,
        moved=16 * yhead.size,
        vmem=8,
        in_specs=[pl.BlockSpec(memory_space=pltpu.SMEM)] + [whole] * 4,
    )(sides, ra, rb, yhead, ytail)
    qa = swap(ya, "gy", 0)
    qb = swap(yb, "gy", 1)
    return ra, rb, qa, qb


def body(
    vectors, diffusivity, vertical_factor, weight_first, bias_first, weight_second,
    bias_second, weight_out, error_inverse, observed_column, owner_count,
    observed_state, channel_mask,
):
    pairs, tile_x, tile_y, levels = vectors.shape
    count_y = lax.axis_size("gy")
    devices = lax.axis_size("gx") * count_y
    slots = observed_column.shape[0]
    bucket = slots // devices
    cells = tile_x * tile_y
    grid_wide = tile_y * count_y
    units = weight_second.shape[0]
    deep = up(levels, LANES)
    tall, around = tile_x + 2 * SWEEPS, tile_y + 2 * SWEEPS
    full_l, full_u = up(levels, WIDE), up(units, WIDE)
    full_c = up(error_inverse.shape[0], WIDE)
    mark = up(levels, 16)

    sides = jnp.stack([lax.axis_index("gx") % 2, lax.axis_index("gy") % 2]).astype(jnp.int32)
    whole = pl.BlockSpec(memory_space=pltpu.VMEM)
    far = pl.BlockSpec(memory_space=pltpu.HBM)
    scalars = pl.BlockSpec(memory_space=pltpu.SMEM)
    base = pltpu.with_memory_space_constraint(vectors, pltpu.HBM)
    strips = []
    for v in range(pairs):
        deep_v = levels + (v == 0)
        cuts = call(
            functools.partial(cut_kernel, v),
            [shaped((SWEEPS, tile_y, deep_v))] * 2 + [shaped((tile_x, SWEEPS, deep_v))] * 2,
            flops=0,
            moved=4 * vectors.size,
            vmem=12,
            scratch=[pltpu.VMEM((SWEEPS, tile_y, levels), F32)] * 2
            + [pltpu.VMEM((tile_x, 8, levels), F32)] * 2
            + [pltpu.SemaphoreType.DMA((4,))],
            in_specs=[scalars, far, whole],
        )(sides, base, diffusivity)
        strips.append(halo(sides, *cuts))

    position = jnp.arange(slots, dtype=jnp.int32)
    grid_row = observed_column // grid_wide
    grid_col = observed_column % grid_wide
    target = grid_row // tile_x * count_y + grid_col // tile_y
    dest = jnp.where(position < owner_count[0], target, -1)
    cell = (grid_row % tile_x * tile_y + grid_col % tile_y + 1).astype(F32)
    packed = call(
        functools.partial(pack_kernel, bucket),
        shaped((slots, deep)),
        flops=6 * slots * slots * deep,
        moved=8 * slots * deep,
        scratch=[pltpu.VMEM((deep, slots), BF)] * 2,
        vmem=12,
    )(dest[None, :], cell[None, :], observed_state.T)
    carried = lax.all_to_all(
        packed.reshape(devices, bucket, deep), ("gx", "gy"), split_axis=0,
        concat_axis=0, tiled=True,
    ).reshape(slots, deep)

    side = max(full_l, full_u, full_c)
    weights = (vertical_factor, weight_first, weight_second, weight_out.T, error_inverse)
    first, stack = call(
        prep_kernel,
        [pltpu.HBM((2, full_l, side), BF), pltpu.HBM((4, 2, side, side), BF)],
        flops=6 * full_l * full_l * full_u,
        moved=8 * 5 * full_u * full_u,
        scratch=[pltpu.VMEM(weight.shape, F32) for weight in weights]
        + [
            pltpu.VMEM((2, full_l, side), BF), pltpu.VMEM((4, 2, side, side), BF),
            pltpu.VMEM((2, side, full_l), BF),
            pltpu.SemaphoreType.DMA((5,)), pltpu.SemaphoreType.DMA((5,)),
        ],
        vmem=34,
        in_specs=[far] * 5,
        out_specs=[far] * 2,
    )(*[pltpu.with_memory_space_constraint(weight, pltpu.HBM) for weight in weights])
    first, stack = (pltpu.with_memory_space_constraint(x, pltpu.HBM) for x in (first, stack))

    def wide_bias(bias):
        return jnp.pad(bias, (0, side - bias.shape[0]))[None, :]

    def block(v):
        return pl.BlockSpec((1, tile_x, tile_y, levels), lambda i: (v, 0, 0, 0))

    queries = []
    for v in range(pairs):
        got = call(
            functools.partial(diffuse_kernel, v > 0),
            [shaped((cells, side))] + [shaped((tall, around, LANES))] * (v == 0),
            flops=6 * cells * deep * full_u,
            moved=8 * tall * around * deep,
            scratch=[
                pltpu.VMEM((tall, around, deep), F32),
                pltpu.VMEM((2, tall, around, LANES), F32),
                pltpu.VMEM((cells, deep), BF),
                pltpu.VMEM((cells, deep), BF),
                pltpu.VMEM((2, side, side), BF),
                pltpu.SemaphoreType.DMA,
            ],
            grid=(1,),
            vmem=18,
            in_specs=[scalars, block(v)] + [whole] * 5 + [far],
            out_specs=[whole] * (2 - (v > 0)),
        )(sides, vectors, spread if v else diffusivity, *strips[v], stack)
        queries.append(got[0])
        if v == 0:
            spread = got[1]

    scale, one, one_t = call(
        functools.partial(hidden_kernel, mark, bucket),
        [shaped((3, slots, side)), shaped((slots, cells), BF), shaped((cells, slots), BF)],
        flops=12 * slots * full_u * full_u,
        moved=8 * slots * full_u,
        scratch=[pltpu.VMEM((slots, side), BF)] * 2
        + [
            pltpu.VMEM((2, full_l, side), BF), pltpu.VMEM((2, side, side), BF),
            pltpu.SemaphoreType.DMA((2,)),
        ],
        vmem=24,
        in_specs=[whole, far, whole, far, whole, whole],
    )(carried, first, wide_bias(bias_first), stack, wide_bias(bias_second), channel_mask)

    fields = []
    for v in range(pairs):
        fields.append(
            call(
                net_kernel,
                [shaped((tile_x, tile_y, levels))]
                + [shaped((SWEEPS, tile_y, levels))] * 2
                + [shaped((tile_x, SWEEPS, levels))] * 2,
                flops=36 * slots * full_u * full_u,
                moved=4 * 5 * full_u * full_u,
                scratch=[pltpu.VMEM((2, slots, side), BF)]
                + [pltpu.VMEM((2, slots // 2, side), BF)] * 2
                + [pltpu.VMEM((slots // 2, side), F32)] * 2
                + [
                    pltpu.VMEM((4, 2, side, side), BF),
                    pltpu.SemaphoreType.DMA((4,)),
                ],
                vmem=30,
                in_specs=[scalars] + [whole] * 4 + [far],
            )(sides, queries[v], one, one_t, scale, stack)
        )

    out = None
    for v in range(pairs):
        around_field = halo(sides, *fields[v][1:])
        carry = [] if out is None else [out]
        out = call(
            finish_kernel,
            shaped(vectors.shape),
            flops=40 * tall * around * deep,
            moved=12 * cells * deep,
            scratch=[
                pltpu.VMEM((tall, around, deep), F32),
                pltpu.VMEM((2, tall, around, LANES), F32),
                pltpu.VMEM((tile_x, tile_y, deep), F32),
            ],
            grid=(1,),
            vmem=18,
            in_specs=[scalars, whole, block(v)] + [whole] * 5
            + [pl.BlockSpec(memory_space=pl.ANY)] * len(carry),
            out_specs=block(v),
            input_output_aliases={8: 0} if carry else {},
        )(sides, fields[v][0], vectors, spread, *around_field, *carry)
    return out


def solution(mesh):
    in_specs = (
        P(None, "gx", "gy", None),
        P("gx", "gy"),
        P(),
        P(),
        P(),
        P(),
        P(),
        P(),
        P(),
        P(("gx", "gy")),
        P(("gx", "gy")),
        P(("gx", "gy"), None),
        P(),
    )
    out_specs = P(None, "gx", "gy", None)
    return jax.shard_map(body, mesh=mesh, in_specs=in_specs, out_specs=out_specs, check_vma=False)
```

```python
import functools

import jax
import jax.numpy as jnp
from jax import lax
from jax.experimental import pallas as pl
from jax.experimental.pallas import tpu as pltpu
from jax.sharding import PartitionSpec as P

SWEEPS = 4
WIDE = 256
LANES = 128
BF = jnp.bfloat16
F32 = jnp.float32
NN = ((1,), (0,))
NT = ((1,), (1,))


def up(size, unit):
    return -(-size // unit) * unit


def split(value):
    high = value.astype(BF)
    return high, (value - high.astype(F32)).astype(BF)


def mm(left, right, dims=NN):
    return lax.dot_general(left, right, (dims, ((), ())), preferred_element_type=F32)


def mm3(left_high, left_low, right_high, right_low, dims=NN):
    return mm(left_high, right_high, dims) + (
        mm(left_high, right_low, dims) + mm(left_low, right_high, dims)
    )


def halves(size):
    half = size // 2
    return [pl.ds(0, half), pl.ds(half, half)] if half % 16 == 0 else [pl.ds(0, size)]


def iota(shape, axis):
    return lax.broadcasted_iota(jnp.int32, shape, axis)


def call(kernel, out_shape, flops, moved, scratch=(), vmem=48, **more):
    return pl.pallas_call(
        kernel,
        out_shape=out_shape,
        scratch_shapes=list(scratch),
        compiler_params=pltpu.CompilerParams(vmem_limit_bytes=vmem * 1024 * 1024),
        cost_estimate=pl.CostEstimate(flops=flops, bytes_accessed=moved, transcendentals=0),
        **more,
    )


def shaped(shape, dtype=F32):
    return jax.ShapeDtypeStruct(shape, dtype)


def pack_kernel(bucket, dest_ref, cell_ref, state_ref, out_ref, high_ref, low_ref):
    levels, slots = state_ref.shape
    devices = slots // bucket
    dest = dest_ref[...]
    same = (iota((devices, slots), 0) == dest).astype(F32)
    before = (iota((slots, slots), 0) < iota((slots, slots), 1)).astype(BF)
    rank = jnp.sum(same * mm(same.astype(BF), before), axis=0, keepdims=True)
    place = dest * bucket + rank.astype(jnp.int32)
    pick = (iota((slots, slots), 0) == place).astype(BF)
    high_ref[...] = jnp.zeros_like(high_ref)
    low_ref[...] = jnp.zeros_like(low_ref)
    high, low = split(state_ref[...])
    high_ref[:levels, :] = high
    low_ref[:levels, :] = low
    mark = up(levels, 16)
    tall = jnp.where(iota((16, slots), 0) == 0, cell_ref[...], 0.0)
    high, low = split(tall)
    high_ref[mark : mark + 16, :] = high
    low_ref[mark : mark + 16, :] = low
    out_ref[...] = mm(pick, high_ref[...], NT) + mm(pick, low_ref[...], NT)


def prep_kernel(*refs):
    ins, (first_out, stack_out), refs = refs[:5], refs[5:7], refs[7:]
    raw, (first, stack, turned, in_sem, out_sem) = refs[:5], refs[5:]
    fetch = [
        pltpu.make_async_copy(ins[k], raw[k], in_sem.at[k]) for k in range(5)
    ]
    for copy in fetch:
        copy.start()
    sends = []

    def send(source, target):
        copy = pltpu.make_async_copy(source, target, out_sem.at[len(sends)])
        copy.start()
        sends.append(copy)

    def put(values, ref):
        rows, cols = values.shape
        if (rows, cols) != ref.shape[1:]:
            ref[...] = jnp.zeros_like(ref)
        ref[0, :rows, :cols], ref[1, :rows, :cols] = split(values)

    fetch[0].wait()
    put(raw[0][...].T, turned)
    fetch[1].wait()
    put(raw[1][...], first)
    send(first, first_out)
    for copy in fetch[2:]:
        copy.wait()
    rows = up(raw[0].shape[1], LANES)
    stack[3, :, rows:, :] = jnp.zeros((2,) + (stack.shape[2] - rows, stack.shape[3]), BF)
    parts = halves(rows)
    for k in range(3):
        if k < len(parts):
            part = parts[k]
            got = mm3(turned[0, part, :], turned[1, part, :], first[0], first[1])
            stack[3, 0, part, :], stack[3, 1, part, :] = split(got)
        put(raw[k + 2][...], stack.at[k])
    for k in range(4):
        send(stack.at[k], stack_out.at[k])
    for copy in sends:
        copy.wait()


def coeff_column(coeff_ref, row):
    wide = coeff_ref.shape[1]
    spread = jnp.broadcast_to(coeff_ref[row : row + 1, :], (wide, wide))
    diagonal = iota((wide, wide), 0) == iota((wide, wide), 1)
    return jnp.sum(jnp.where(diagonal, spread, 0.0), axis=1, keepdims=True)


def cut_kernel(v, side_ref, vectors_ref, coeff_ref, xa, xb, yhead, ytail, *refs):
    bufs, sems = refs[:4], refs[4]
    rows, wide, levels = vectors_ref.shape[1:]
    w = SWEEPS
    parts = (
        vectors_ref.at[v, pl.ds(0, w)],
        vectors_ref.at[v, pl.ds(rows - w, w)],
        vectors_ref.at[v, :, pl.ds(0, 8)],
        vectors_ref.at[v, :, pl.ds(wide - 8, 8)],
    )
    copies = [pltpu.make_async_copy(parts[k], bufs[k], sems.at[k]) for k in range(4)]
    for copy in copies:
        copy.start()
    even = side_ref[0] == 0
    if v == 0:
        columns = [coeff_column(coeff_ref, row) for row in range(rows)]
        for row in range(w):
            head, tail = columns[row], columns[rows - w + row]
            xa[row, :, levels:] = jnp.where(even, tail, head)
            xb[row, :, levels:] = jnp.where(even, head, tail)
        for row in range(rows):
            yhead[row, :, levels:] = columns[row][:w]
            ytail[row, :, levels:] = columns[row][wide - w :]
    for copy in copies:
        copy.wait()
    head, tail = bufs[0][...], bufs[1][...]
    xa[:, :, :levels] = jnp.where(even, tail, head)
    xb[:, :, :levels] = jnp.where(even, head, tail)
    yhead[:, :, :levels] = bufs[2][:, :w]
    ytail[:, :, :levels] = bufs[3][:, 8 - w :]


def join_kernel(side_ref, ra, rb, yhead, ytail, ya, yb):
    w = SWEEPS
    rows = yhead.shape[0]
    wide = ra.shape[1]
    even_x, even_y = side_ref[0] == 0, side_ref[1] == 0

    for here, first, second in (
        (pl.ds(0, w), rb, ra),
        (pl.ds(w + rows, w), ra, rb),
    ):
        head = jnp.where(even_x, first[:, :w], second[:, :w])
        tail = jnp.where(even_x, first[:, wide - w :], second[:, wide - w :])
        ya[here] = jnp.where(even_y, tail, head)
        yb[here] = jnp.where(even_y, head, tail)
    here = pl.ds(w, rows)
    ya[here] = jnp.where(even_y, ytail[...], yhead[...])
    yb[here] = jnp.where(even_y, yhead[...], ytail[...])


def fill(ext, side_ref, tile, ra, rb, qa, qb, part):
    rows, wide = tile.shape[:2]
    w = SWEEPS
    even_y = side_ref[1] == 0
    upper = jnp.where(side_ref[0] == 0, w + rows, 0)
    tile_part, strip_part = part
    ext[w : w + rows, :wide, tile_part] = tile
    ext[pl.ds(upper, w), :wide, tile_part] = strip_part(ra)
    ext[pl.ds(w + rows - upper, w), :wide, tile_part] = strip_part(rb)
    qa, qb = strip_part(qa), strip_part(qb)
    ext[:, wide : wide + w, tile_part] = jnp.where(even_y, qa, qb)
    ext[:, wide + w :, tile_part] = jnp.where(even_y, qb, qa)


def fill_levels(ext, side_ref, tile, *strips):
    levels = tile.shape[2]
    last = up(levels, LANES) - LANES
    ext[:, :, last:] = jnp.zeros((ext.shape[0], ext.shape[1], ext.shape[2] - last), F32)
    part = (pl.ds(0, levels), lambda ref: ref[:, :, :levels])
    fill(ext, side_ref, tile, *strips, part)


def diffuse_kernel(given, side_ref, tile_ref, coeff_ref, *refs):
    strips, stack_ref, refs = refs[:4], refs[4], refs[5:]
    ext, work, high_ref, low_ref, both, sem = refs[-6:]
    out_ref = refs[0]
    fetch = pltpu.make_async_copy(stack_ref.at[3], both, sem)
    fetch.start()
    w = SWEEPS
    rows, wide, levels = tile_ref.shape[1:]
    tall = rows + 2 * w
    around = wide + 2 * w
    fill_levels(ext, side_ref, tile_ref[0], *strips)
    if given:
        cb_ref = coeff_ref
    else:
        cb_ref = refs[1]

        def spread(ref):
            column = ref[:, :, levels : levels + 1]
            return jnp.broadcast_to(column, column.shape[:2] + (LANES,))

        own = jnp.stack(
            [jnp.broadcast_to(coeff_column(coeff_ref, k), (wide, LANES)) for k in range(rows)]
        )
        fill(cb_ref.at[0], side_ref, own, *strips, (pl.ds(0, LANES), spread))
        cb_ref[1] = 1.0 - 4.0 * cb_ref[0]

    def chunk(j, _):
        lanes = pl.ds(pl.multiple_of(j * LANES, LANES), LANES)
        for sweep in range(SWEEPS):
            for i in range(sweep + 1, tall - 1 - sweep):
                if sweep == 0:
                    above, mid, below = (ext[k, :, lanes] for k in (i - 1, i, i + 1))
                else:
                    above, mid, below = (work[(sweep + 1) % 2, k] for k in (i - 1, i, i + 1))
                beside = above + below + pltpu.roll(mid, 1, 0) + pltpu.roll(mid, around - 1, 0)
                new = cb_ref[1, i] * mid + cb_ref[0, i] * beside
                if sweep == SWEEPS - 1:
                    high, low = split(new[:wide])
                    here = pl.ds((i - w) * wide, wide)
                    high_ref[here, lanes] = high
                    low_ref[here, lanes] = low
                else:
                    work[sweep % 2, i] = new
        return 0

    lax.fori_loop(0, ext.shape[2] // LANES, chunk, 0)
    deep = ext.shape[2]
    fetch.wait()
    for part in halves(out_ref.shape[0]):
        out_ref[part, :] = mm3(
            high_ref[part, :], low_ref[part, :], both[0, :deep], both[1, :deep]
        )


def hidden_kernel(
    mark, bucket, x_ref, first_ref, b1_ref, stack_ref, b2_ref, mask_ref,
    scale_ref, one_ref, one_t_ref, high_ref, low_ref, x_buf, first, second, sems,
):
    fetch_x = pltpu.make_async_copy(x_ref, x_buf, sems.at[2])
    fetch_x.start()
    fetch_first = pltpu.make_async_copy(first_ref, first, sems.at[0])
    fetch_second = pltpu.make_async_copy(stack_ref.at[0], second, sems.at[1])
    fetch_first.start()
    fetch_second.start()
    s1_ref, s2_ref, gate_ref = (scale_ref.at[k] for k in range(3))
    slots, deep = x_ref.shape
    cells = one_ref.shape[1]
    devices, channels = mask_ref.shape
    fetch_x.wait()
    x_ref = x_buf
    index = x_ref[:, mark : mark + 1]
    cell = index.astype(jnp.int32) - 1
    live = index > 0.5
    one_ref[...] = (iota((slots, cells), 1) == cell).astype(BF)
    flat = jnp.broadcast_to(index, (slots, LANES)).T[0:1, :].astype(jnp.int32) - 1
    one_t_ref[...] = (iota((cells, slots), 0) == flat).astype(BF)
    begin = iota((slots, devices), 1) * bucket
    at = iota((slots, devices), 0)
    from_owner = ((at >= begin) & (at < begin + bucket) & live).astype(BF)
    gate_ref[...] = jnp.zeros_like(gate_ref)
    gate_ref[:, :channels] = mm(from_owner, mask_ref[...].astype(F32).astype(BF))
    high, low = split(x_ref[...])
    high_ref[:, :deep] = high
    low_ref[:, :deep] = low
    parts = halves(slots)
    fetch_first.wait()
    for part in parts:
        got = mm3(high_ref[part, :deep], low_ref[part, :deep], first[0, :deep], first[1, :deep])
        hidden = jnp.tanh(got + b1_ref[...])
        s1_ref[part, :] = 1.0 - hidden * hidden
        high, low = split(hidden)
        high_ref[part, :] = high
        low_ref[part, :] = low
    fetch_second.wait()
    for part in parts:
        got = mm3(high_ref[part, :], low_ref[part, :], second[0], second[1])
        hidden = jnp.tanh(got + b2_ref[...])
        s2_ref[part, :] = 1.0 - hidden * hidden


LAYERS = ((0, 0, 1), (1, 1, 2), (2, 0, 2), (1, 0, 1), (0, 1, 0))


def table(values, layer):
    value = jnp.int32(values[0])
    for k in range(1, len(values)):
        value = jnp.where(layer == k, values[k], value)
    return value


def net_kernel(
    side_ref, q_ref, one_ref, one_t_ref, scale_ref, stack_ref,
    out_ref, xa, xb, yhead, ytail, x1, top, low, acc_top, acc_low, stack, sems,
):
    fetch = [
        pltpu.make_async_copy(stack_ref.at[k], stack.at[k], sems.at[k]) for k in range(4)
    ]
    for copy in fetch:
        copy.start()
    slots = q_ref.shape[0]
    half = slots // 2
    first, second = pl.ds(0, half), pl.ds(half, half)

    def pick(picker):
        return mm(picker, x1[0]) + mm(picker, x1[1])

    def close(acc, scale, part, target):
        target[0], target[1] = split(acc[...] * scale_ref[scale, part, :])

    x1[0], x1[1] = split(q_ref[...])
    acc_top[...] = pick(one_ref[first, :])
    acc_low[...] = pick(one_ref[second, :])
    close(acc_top, 0, first, top)
    fetch[0].wait()
    scales = [0] + [entry[2] for entry in LAYERS]

    def step(layer, _):
        for k in (1, 2):

            @pl.when(layer == k)
            def _():
                fetch[k].wait()

        weight = table([entry[0] for entry in LAYERS], layer)
        turned = table([entry[1] for entry in LAYERS], layer)
        before, after = table(scales[:-1], layer), table(scales[1:], layer)

        def run(dims):
            acc_top[...] = mm3(top[0], top[1], stack[weight, 0], stack[weight, 1], dims)
            close(acc_low, before, second, low)
            acc_low[...] = mm3(low[0], low[1], stack[weight, 0], stack[weight, 1], dims)
            close(acc_top, after, first, top)

        @pl.when(turned == 0)
        def _():
            run(NN)

        @pl.when(turned == 1)
        def _():
            run(NT)

        return 0

    lax.fori_loop(0, len(LAYERS), step, 0)
    close(acc_low, scales[-1], second, low)
    for part in halves(one_t_ref.shape[0]):
        got = mm(one_t_ref[part, :half], top[0]) + mm(one_t_ref[part, :half], top[1])
        got = got + mm(one_t_ref[part, half:], low[0]) + mm(one_t_ref[part, half:], low[1])
        x1[0, part, :], x1[1, part, :] = split(got)
    fetch[3].wait()
    rows, wide, levels = out_ref.shape
    for k, part in enumerate(halves(rows * wide)):
        got = mm3(x1[0, part, :], x1[1, part, :], stack[3, 0], stack[3, 1], NT)
        tall = got.shape[0] // wide
        got = got.reshape(tall, wide, got.shape[1])[:, :, :levels]
        here = pl.ds(k * tall, tall)
        out_ref[here] = got
        yhead[here] = got[:, :SWEEPS]
        ytail[here] = got[:, wide - SWEEPS :]
    even = side_ref[0] == 0
    head, tail = out_ref[:SWEEPS], out_ref[rows - SWEEPS :]
    xa[...] = jnp.where(even, tail, head)
    xb[...] = jnp.where(even, head, tail)


def finish_kernel(side_ref, field_ref, base_ref, cb_ref, *refs):
    out_ref, ext, work, total = refs[-4:]
    w = SWEEPS
    rows, wide, levels = field_ref.shape
    tall = rows + 2 * w
    fill_levels(ext, side_ref, field_ref[...], *refs[:4])
    around = wide + 2 * w

    def chunk(j, _):
        lanes = pl.ds(pl.multiple_of(j * LANES, LANES), LANES)
        for sweep in range(SWEEPS):

            def read(k):
                value = ext[k, :, lanes] if sweep == 0 else work[(sweep + 1) % 2, k]
                return value, cb_ref[0, k] * value

            above = read(sweep)
            mid = read(sweep + 1)
            for i in range(sweep + 1, tall - 1 - sweep):
                below = read(i + 1)
                scaled = mid[1]
                beside = (
                    above[1] + below[1]
                    + pltpu.roll(scaled, 1, 0) + pltpu.roll(scaled, around - 1, 0)
                )
                new = cb_ref[1, i] * mid[0] + beside
                if sweep == SWEEPS - 1:
                    total[i - w, :, lanes] = new[:wide]
                else:
                    work[sweep % 2, i] = new
                above, mid = mid, below
        return 0

    lax.fori_loop(0, ext.shape[2] // LANES, chunk, 0)
    out_ref[0] = base_ref[0] + total[:, :, :levels]


def swap(value, axis, start):
    pairs = [(i, i + 1) for i in range(start, lax.axis_size(axis) - 1, 2)]
    return lax.ppermute(value, axis, pairs + [(j, i) for i, j in pairs])


def halo(sides, xa, xb, yhead, ytail):
    ra = swap(xa, "gx", 0)
    rb = swap(xb, "gx", 1)
    whole = pl.BlockSpec(memory_space=pltpu.VMEM)
    tall = yhead.shape[0] + 2 * SWEEPS
    ya, yb = call(
        join_kernel,
        [shaped((tall,) + yhead.shape[1:])] * 2,
        flops=0,
        moved=16 * yhead.size,
        vmem=8,
        in_specs=[pl.BlockSpec(memory_space=pltpu.SMEM)] + [whole] * 4,
    )(sides, ra, rb, yhead, ytail)
    qa = swap(ya, "gy", 0)
    qb = swap(yb, "gy", 1)
    return ra, rb, qa, qb


def body(
    vectors, diffusivity, vertical_factor, weight_first, bias_first, weight_second,
    bias_second, weight_out, error_inverse, observed_column, owner_count,
    observed_state, channel_mask,
):
    pairs, tile_x, tile_y, levels = vectors.shape
    count_y = lax.axis_size("gy")
    devices = lax.axis_size("gx") * count_y
    slots = observed_column.shape[0]
    bucket = slots // devices
    cells = tile_x * tile_y
    grid_wide = tile_y * count_y
    units = weight_second.shape[0]
    deep = up(levels, LANES)
    tall, around = tile_x + 2 * SWEEPS, tile_y + 2 * SWEEPS
    full_l, full_u = up(levels, WIDE), up(units, WIDE)
    full_c = up(error_inverse.shape[0], WIDE)
    mark = up(levels, 16)

    sides = jnp.stack([lax.axis_index("gx") % 2, lax.axis_index("gy") % 2]).astype(jnp.int32)
    whole = pl.BlockSpec(memory_space=pltpu.VMEM)
    far = pl.BlockSpec(memory_space=pltpu.HBM)
    scalars = pl.BlockSpec(memory_space=pltpu.SMEM)
    base = pltpu.with_memory_space_constraint(vectors, pltpu.HBM)
    strips = []
    for v in range(pairs):
        deep_v = levels + (v == 0)
        cuts = call(
            functools.partial(cut_kernel, v),
            [shaped((SWEEPS, tile_y, deep_v))] * 2 + [shaped((tile_x, SWEEPS, deep_v))] * 2,
            flops=0,
            moved=4 * vectors.size,
            vmem=12,
            scratch=[pltpu.VMEM((SWEEPS, tile_y, levels), F32)] * 2
            + [pltpu.VMEM((tile_x, 8, levels), F32)] * 2
            + [pltpu.SemaphoreType.DMA((4,))],
            in_specs=[scalars, far, whole],
        )(sides, base, diffusivity)
        strips.append(halo(sides, *cuts))

    position = jnp.arange(slots, dtype=jnp.int32)
    grid_row = observed_column // grid_wide
    grid_col = observed_column % grid_wide
    target = grid_row // tile_x * count_y + grid_col // tile_y
    dest = jnp.where(position < owner_count[0], target, -1)
    cell = (grid_row % tile_x * tile_y + grid_col % tile_y + 1).astype(F32)
    packed = call(
        functools.partial(pack_kernel, bucket),
        shaped((slots, deep)),
        flops=6 * slots * slots * deep,
        moved=8 * slots * deep,
        scratch=[pltpu.VMEM((deep, slots), BF)] * 2,
        vmem=12,
    )(dest[None, :], cell[None, :], observed_state.T)
    carried = lax.all_to_all(
        packed.reshape(devices, bucket, deep), ("gx", "gy"), split_axis=0,
        concat_axis=0, tiled=True,
    ).reshape(slots, deep)

    side = max(full_l, full_u, full_c)
    weights = (vertical_factor, weight_first, weight_second, weight_out.T, error_inverse)
    first, stack = call(
        prep_kernel,
        [pltpu.HBM((2, full_l, side), BF), pltpu.HBM((4, 2, side, side), BF)],
        flops=6 * full_l * full_l * full_u,
        moved=8 * 5 * full_u * full_u,
        scratch=[pltpu.VMEM(weight.shape, F32) for weight in weights]
        + [
            pltpu.VMEM((2, full_l, side), BF), pltpu.VMEM((4, 2, side, side), BF),
            pltpu.VMEM((2, side, full_l), BF),
            pltpu.SemaphoreType.DMA((5,)), pltpu.SemaphoreType.DMA((5,)),
        ],
        vmem=34,
        in_specs=[far] * 5,
        out_specs=[far] * 2,
    )(*[pltpu.with_memory_space_constraint(weight, pltpu.HBM) for weight in weights])
    first, stack = (pltpu.with_memory_space_constraint(x, pltpu.HBM) for x in (first, stack))

    def wide_bias(bias):
        return jnp.pad(bias, (0, side - bias.shape[0]))[None, :]

    def block(v):
        return pl.BlockSpec((1, tile_x, tile_y, levels), lambda i: (v, 0, 0, 0))

    queries = []
    for v in range(pairs):
        got = call(
            functools.partial(diffuse_kernel, v > 0),
            [shaped((cells, side))] + [shaped((2, tall, around, LANES))] * (v == 0),
            flops=6 * cells * deep * full_u,
            moved=8 * tall * around * deep,
            scratch=[
                pltpu.VMEM((tall, around, deep), F32),
                pltpu.VMEM((2, tall, around, LANES), F32),
                pltpu.VMEM((cells, deep), BF),
                pltpu.VMEM((cells, deep), BF),
                pltpu.VMEM((2, side, side), BF),
                pltpu.SemaphoreType.DMA,
            ],
            grid=(1,),
            vmem=18,
            in_specs=[scalars, block(v)] + [whole] * 5 + [far],
            out_specs=[whole] * (2 - (v > 0)),
        )(sides, vectors, spread if v else diffusivity, *strips[v], stack)
        queries.append(got[0])
        if v == 0:
            spread = got[1]

    scale, one, one_t = call(
        functools.partial(hidden_kernel, mark, bucket),
        [shaped((3, slots, side)), shaped((slots, cells), BF), shaped((cells, slots), BF)],
        flops=12 * slots * full_u * full_u,
        moved=8 * slots * full_u,
        scratch=[pltpu.VMEM((slots, side), BF)] * 2
        + [
            pltpu.VMEM((slots, deep), F32),
            pltpu.VMEM((2, full_l, side), BF), pltpu.VMEM((2, side, side), BF),
            pltpu.SemaphoreType.DMA((3,)),
        ],
        vmem=24,
        in_specs=[far, far, whole, far, whole, whole],
    )(pltpu.with_memory_space_constraint(carried, pltpu.HBM), first, wide_bias(bias_first), stack, wide_bias(bias_second), channel_mask)

    fields = []
    for v in range(pairs):
        fields.append(
            call(
                net_kernel,
                [shaped((tile_x, tile_y, levels))]
                + [shaped((SWEEPS, tile_y, levels))] * 2
                + [shaped((tile_x, SWEEPS, levels))] * 2,
                flops=36 * slots * full_u * full_u,
                moved=4 * 5 * full_u * full_u,
                scratch=[pltpu.VMEM((2, slots, side), BF)]
                + [pltpu.VMEM((2, slots // 2, side), BF)] * 2
                + [pltpu.VMEM((slots // 2, side), F32)] * 2
                + [
                    pltpu.VMEM((4, 2, side, side), BF),
                    pltpu.SemaphoreType.DMA((4,)),
                ],
                vmem=30,
                in_specs=[scalars] + [whole] * 4 + [far],
            )(sides, queries[v], one, one_t, scale, stack)
        )

    out = None
    for v in range(pairs):
        around_field = halo(sides, *fields[v][1:])
        carry = [] if out is None else [out]
        out = call(
            finish_kernel,
            shaped(vectors.shape),
            flops=40 * tall * around * deep,
            moved=12 * cells * deep,
            scratch=[
                pltpu.VMEM((tall, around, deep), F32),
                pltpu.VMEM((2, tall, around, LANES), F32),
                pltpu.VMEM((tile_x, tile_y, deep), F32),
            ],
            grid=(1,),
            vmem=18,
            in_specs=[scalars, whole, block(v)] + [whole] * 5
            + [pl.BlockSpec(memory_space=pl.ANY)] * len(carry),
            out_specs=block(v),
            input_output_aliases={8: 0} if carry else {},
        )(sides, fields[v][0], vectors, spread, *around_field, *carry)
    return out


def solution(mesh):
    in_specs = (
        P(None, "gx", "gy", None),
        P("gx", "gy"),
        P(),
        P(),
        P(),
        P(),
        P(),
        P(),
        P(),
        P(("gx", "gy")),
        P(("gx", "gy")),
        P(("gx", "gy"), None),
        P(),
    )
    out_specs = P(None, "gx", "gy", None)
    return jax.shard_map(body, mesh=mesh, in_specs=in_specs, out_specs=out_specs, check_vma=False)
```

```python
import functools

import jax
import jax.numpy as jnp
from jax import lax
from jax.experimental import pallas as pl
from jax.experimental.pallas import tpu as pltpu
from jax.sharding import PartitionSpec as P

SWEEPS = 4
WIDE = 256
LANES = 128
BF = jnp.bfloat16
F32 = jnp.float32
NN = ((1,), (0,))
NT = ((1,), (1,))


def up(size, unit):
    return -(-size // unit) * unit


def split(value):
    high = value.astype(BF)
    return high, (value - high.astype(F32)).astype(BF)


def mm(left, right, dims=NN):
    return lax.dot_general(left, right, (dims, ((), ())), preferred_element_type=F32)


def mm3(left_high, left_low, right_high, right_low, dims=NN):
    left = jnp.concatenate([left_high, left_low, left_high], axis=dims[0][0])
    right = jnp.concatenate([right_high, right_high, right_low], axis=dims[1][0])
    return mm(left, right, dims)


def halves(size):
    half = size // 2
    return [pl.ds(0, half), pl.ds(half, half)] if half % 16 == 0 else [pl.ds(0, size)]


def iota(shape, axis):
    return lax.broadcasted_iota(jnp.int32, shape, axis)


def call(kernel, out_shape, flops, moved, scratch=(), vmem=48, **more):
    return pl.pallas_call(
        kernel,
        out_shape=out_shape,
        scratch_shapes=list(scratch),
        compiler_params=pltpu.CompilerParams(vmem_limit_bytes=vmem * 1024 * 1024),
        cost_estimate=pl.CostEstimate(flops=flops, bytes_accessed=moved, transcendentals=0),
        **more,
    )


def shaped(shape, dtype=F32):
    return jax.ShapeDtypeStruct(shape, dtype)


def pack_kernel(bucket, dest_ref, cell_ref, state_ref, out_ref, high_ref, low_ref):
    levels, slots = state_ref.shape
    devices = slots // bucket
    dest = dest_ref[...]
    same = (iota((devices, slots), 0) == dest).astype(F32)
    before = (iota((slots, slots), 0) < iota((slots, slots), 1)).astype(BF)
    rank = jnp.sum(same * mm(same.astype(BF), before), axis=0, keepdims=True)
    place = dest * bucket + rank.astype(jnp.int32)
    pick = (iota((slots, slots), 0) == place).astype(BF)
    high_ref[...] = jnp.zeros_like(high_ref)
    low_ref[...] = jnp.zeros_like(low_ref)
    high, low = split(state_ref[...])
    high_ref[:levels, :] = high
    low_ref[:levels, :] = low
    mark = up(levels, 16)
    tall = jnp.where(iota((16, slots), 0) == 0, cell_ref[...], 0.0)
    high, low = split(tall)
    high_ref[mark : mark + 16, :] = high
    low_ref[mark : mark + 16, :] = low
    out_ref[...] = mm(pick, high_ref[...], NT) + mm(pick, low_ref[...], NT)


def prep_kernel(*refs):
    ins, (first_out, stack_out), refs = refs[:5], refs[5:7], refs[7:]
    raw, (first, stack, turned, in_sem, out_sem) = refs[:5], refs[5:]
    fetch = [
        pltpu.make_async_copy(ins[k], raw[k], in_sem.at[k]) for k in range(5)
    ]
    for copy in fetch:
        copy.start()
    sends = []

    def send(source, target):
        copy = pltpu.make_async_copy(source, target, out_sem.at[len(sends)])
        copy.start()
        sends.append(copy)

    def put(values, ref):
        rows, cols = values.shape
        if (rows, cols) != ref.shape[1:]:
            ref[...] = jnp.zeros_like(ref)
        ref[0, :rows, :cols], ref[1, :rows, :cols] = split(values)

    fetch[0].wait()
    put(raw[0][...].T, turned)
    fetch[1].wait()
    put(raw[1][...], first)
    send(first, first_out)
    rows = up(raw[0].shape[1], LANES)
    stack[3, :, rows:, :] = jnp.zeros((2,) + (stack.shape[2] - rows, stack.shape[3]), BF)
    for part in halves(rows):
        got = mm3(turned[0, part, :], turned[1, part, :], first[0], first[1])
        stack[3, 0, part, :], stack[3, 1, part, :] = split(got)
    send(stack.at[3], stack_out.at[3])
    for k in range(3):
        fetch[k + 2].wait()
        put(raw[k + 2][...], stack.at[k])
        send(stack.at[k], stack_out.at[k])
    for copy in sends:
        copy.wait()


def coeff_column(coeff_ref, row):
    wide = coeff_ref.shape[1]
    spread = jnp.broadcast_to(coeff_ref[row : row + 1, :], (wide, wide))
    diagonal = iota((wide, wide), 0) == iota((wide, wide), 1)
    return jnp.sum(jnp.where(diagonal, spread, 0.0), axis=1, keepdims=True)


def cut_kernel(v, side_ref, vectors_ref, coeff_ref, xa, xb, yhead, ytail, *refs):
    bufs, sems = refs[:4], refs[4]
    rows, wide, levels = vectors_ref.shape[1:]
    w = SWEEPS
    parts = (
        vectors_ref.at[v, pl.ds(0, w)],
        vectors_ref.at[v, pl.ds(rows - w, w)],
        vectors_ref.at[v, :, pl.ds(0, 8)],
        vectors_ref.at[v, :, pl.ds(wide - 8, 8)],
    )
    copies = [pltpu.make_async_copy(parts[k], bufs[k], sems.at[k]) for k in range(4)]
    for copy in copies:
        copy.start()
    even = side_ref[0] == 0
    if v == 0:
        columns = [coeff_column(coeff_ref, row) for row in range(rows)]
        for row in range(w):
            head, tail = columns[row], columns[rows - w + row]
            xa[row, :, levels:] = jnp.where(even, tail, head)
            xb[row, :, levels:] = jnp.where(even, head, tail)
        for row in range(rows):
            yhead[row, :, levels:] = columns[row][:w]
            ytail[row, :, levels:] = columns[row][wide - w :]
    for copy in copies:
        copy.wait()
    head, tail = bufs[0][...], bufs[1][...]
    xa[:, :, :levels] = jnp.where(even, tail, head)
    xb[:, :, :levels] = jnp.where(even, head, tail)
    yhead[:, :, :levels] = bufs[2][:, :w]
    ytail[:, :, :levels] = bufs[3][:, 8 - w :]


def join_kernel(side_ref, ra, rb, yhead, ytail, ya, yb):
    w = SWEEPS
    rows = yhead.shape[0]
    wide = ra.shape[1]
    even_x, even_y = side_ref[0] == 0, side_ref[1] == 0

    for here, first, second in (
        (pl.ds(0, w), rb, ra),
        (pl.ds(w + rows, w), ra, rb),
    ):
        head = jnp.where(even_x, first[:, :w], second[:, :w])
        tail = jnp.where(even_x, first[:, wide - w :], second[:, wide - w :])
        ya[here] = jnp.where(even_y, tail, head)
        yb[here] = jnp.where(even_y, head, tail)
    here = pl.ds(w, rows)
    ya[here] = jnp.where(even_y, ytail[...], yhead[...])
    yb[here] = jnp.where(even_y, yhead[...], ytail[...])


def fill(ext, side_ref, tile, ra, rb, qa, qb, part):
    rows, wide = tile.shape[:2]
    w = SWEEPS
    even_y = side_ref[1] == 0
    upper = jnp.where(side_ref[0] == 0, w + rows, 0)
    tile_part, strip_part = part
    ext[w : w + rows, :wide, tile_part] = tile
    ext[pl.ds(upper, w), :wide, tile_part] = strip_part(ra)
    ext[pl.ds(w + rows - upper, w), :wide, tile_part] = strip_part(rb)
    qa, qb = strip_part(qa), strip_part(qb)
    ext[:, wide : wide + w, tile_part] = jnp.where(even_y, qa, qb)
    ext[:, wide + w :, tile_part] = jnp.where(even_y, qb, qa)


def fill_levels(ext, side_ref, tile, *strips):
    levels = tile.shape[2]
    last = up(levels, LANES) - LANES
    ext[:, :, last:] = jnp.zeros((ext.shape[0], ext.shape[1], ext.shape[2] - last), F32)
    part = (pl.ds(0, levels), lambda ref: ref[:, :, :levels])
    fill(ext, side_ref, tile, *strips, part)


def diffuse_kernel(given, side_ref, tile_ref, coeff_ref, *refs):
    strips, stack_ref, refs = refs[:4], refs[4], refs[5:]
    ext, work, high_ref, low_ref, both, sem = refs[-6:]
    out_ref = refs[0]
    fetch = pltpu.make_async_copy(stack_ref.at[3], both, sem)
    fetch.start()
    w = SWEEPS
    rows, wide, levels = tile_ref.shape[1:]
    tall = rows + 2 * w
    around = wide + 2 * w
    fill_levels(ext, side_ref, tile_ref[0], *strips)
    if given:
        cb_ref = coeff_ref
    else:
        cb_ref = refs[1]

        def spread(ref):
            column = ref[:, :, levels : levels + 1]
            return jnp.broadcast_to(column, column.shape[:2] + (LANES,))

        own = jnp.stack(
            [jnp.broadcast_to(coeff_column(coeff_ref, k), (wide, LANES)) for k in range(rows)]
        )
        fill(cb_ref.at[0], side_ref, own, *strips, (pl.ds(0, LANES), spread))
        cb_ref[1] = 1.0 - 4.0 * cb_ref[0]

    def chunk(j, _):
        lanes = pl.ds(pl.multiple_of(j * LANES, LANES), LANES)
        for sweep in range(SWEEPS):
            for i in range(sweep + 1, tall - 1 - sweep):
                if sweep == 0:
                    above, mid, below = (ext[k, :, lanes] for k in (i - 1, i, i + 1))
                else:
                    above, mid, below = (work[(sweep + 1) % 2, k] for k in (i - 1, i, i + 1))
                beside = above + below + pltpu.roll(mid, 1, 0) + pltpu.roll(mid, around - 1, 0)
                new = cb_ref[1, i] * mid + cb_ref[0, i] * beside
                if sweep == SWEEPS - 1:
                    high, low = split(new[:wide])
                    here = pl.ds((i - w) * wide, wide)
                    high_ref[here, lanes] = high
                    low_ref[here, lanes] = low
                else:
                    work[sweep % 2, i] = new
        return 0

    lax.fori_loop(0, ext.shape[2] // LANES, chunk, 0)
    deep = ext.shape[2]
    fetch.wait()
    for part in halves(out_ref.shape[0]):
        out_ref[part, :] = mm3(
            high_ref[part, :], low_ref[part, :], both[0, :deep], both[1, :deep]
        )


def hidden_kernel(
    mark, bucket, x_ref, first_ref, b1_ref, stack_ref, b2_ref, mask_ref,
    scale_ref, one_ref, one_t_ref, high_ref, low_ref, x_buf, first, second, sems,
):
    fetch_x = pltpu.make_async_copy(x_ref, x_buf, sems.at[2])
    fetch_x.start()
    fetch_first = pltpu.make_async_copy(first_ref, first, sems.at[0])
    fetch_second = pltpu.make_async_copy(stack_ref.at[0], second, sems.at[1])
    fetch_first.start()
    fetch_second.start()
    s1_ref, s2_ref, gate_ref = (scale_ref.at[k] for k in range(3))
    slots, deep = x_ref.shape
    cells = one_ref.shape[1]
    devices, channels = mask_ref.shape
    fetch_x.wait()
    x_ref = x_buf
    index = x_ref[:, mark : mark + 1]
    cell = index.astype(jnp.int32) - 1
    live = index > 0.5
    one_ref[...] = (iota((slots, cells), 1) == cell).astype(BF)
    flat = jnp.broadcast_to(index, (slots, LANES)).T[0:1, :].astype(jnp.int32) - 1
    one_t_ref[...] = (iota((cells, slots), 0) == flat).astype(BF)
    begin = iota((slots, devices), 1) * bucket
    at = iota((slots, devices), 0)
    from_owner = ((at >= begin) & (at < begin + bucket) & live).astype(BF)
    gate_ref[...] = jnp.zeros_like(gate_ref)
    gate_ref[:, :channels] = mm(from_owner, mask_ref[...].astype(F32).astype(BF))
    high, low = split(x_ref[...])
    high_ref[:, :deep] = high
    low_ref[:, :deep] = low
    parts = halves(slots)
    fetch_first.wait()
    for part in parts:
        got = mm3(high_ref[part, :deep], low_ref[part, :deep], first[0, :deep], first[1, :deep])
        hidden = jnp.tanh(got + b1_ref[...])
        s1_ref[part, :] = 1.0 - hidden * hidden
        high, low = split(hidden)
        high_ref[part, :] = high
        low_ref[part, :] = low
    fetch_second.wait()
    for part in parts:
        got = mm3(high_ref[part, :], low_ref[part, :], second[0], second[1])
        hidden = jnp.tanh(got + b2_ref[...])
        s2_ref[part, :] = 1.0 - hidden * hidden


LAYERS = ((0, 0, 1), (1, 1, 2), (2, 0, 2), (1, 0, 1), (0, 1, 0))


def table(values, layer):
    value = jnp.int32(values[0])
    for k in range(1, len(values)):
        value = jnp.where(layer == k, values[k], value)
    return value


def net_kernel(
    side_ref, q_ref, one_ref, one_t_ref, scale_ref, stack_ref,
    out_ref, xa, xb, yhead, ytail, x1, top, low, acc_top, acc_low, stack, sems,
):
    fetch = [
        pltpu.make_async_copy(stack_ref.at[k], stack.at[k], sems.at[k]) for k in range(4)
    ]
    for copy in fetch:
        copy.start()
    slots = q_ref.shape[0]
    half = slots // 2
    first, second = pl.ds(0, half), pl.ds(half, half)

    def pick(picker):
        return mm(picker, x1[0]) + mm(picker, x1[1])

    def close(acc, scale, part, target):
        target[0], target[1] = split(acc[...] * scale_ref[scale, part, :])

    x1[0], x1[1] = split(q_ref[...])
    acc_top[...] = pick(one_ref[first, :])
    acc_low[...] = pick(one_ref[second, :])
    close(acc_top, 0, first, top)
    fetch[0].wait()
    scales = [0] + [entry[2] for entry in LAYERS]

    def step(layer, _):
        for k in (1, 2):

            @pl.when(layer == k)
            def _():
                fetch[k].wait()

        weight = table([entry[0] for entry in LAYERS], layer)
        turned = table([entry[1] for entry in LAYERS], layer)
        before, after = table(scales[:-1], layer), table(scales[1:], layer)

        def run(dims):
            acc_top[...] = mm3(top[0], top[1], stack[weight, 0], stack[weight, 1], dims)
            close(acc_low, before, second, low)
            acc_low[...] = mm3(low[0], low[1], stack[weight, 0], stack[weight, 1], dims)
            close(acc_top, after, first, top)

        @pl.when(turned == 0)
        def _():
            run(NN)

        @pl.when(turned == 1)
        def _():
            run(NT)

        return 0

    lax.fori_loop(0, len(LAYERS), step, 0)
    close(acc_low, scales[-1], second, low)
    for part in halves(one_t_ref.shape[0]):
        got = mm(one_t_ref[part, :half], top[0]) + mm(one_t_ref[part, :half], top[1])
        got = got + mm(one_t_ref[part, half:], low[0]) + mm(one_t_ref[part, half:], low[1])
        x1[0, part, :], x1[1, part, :] = split(got)
    fetch[3].wait()
    rows, wide, levels = out_ref.shape
    for k, part in enumerate(halves(rows * wide)):
        got = mm3(x1[0, part, :], x1[1, part, :], stack[3, 0], stack[3, 1], NT)
        tall = got.shape[0] // wide
        got = got.reshape(tall, wide, got.shape[1])[:, :, :levels]
        here = pl.ds(k * tall, tall)
        out_ref[here] = got
        yhead[here] = got[:, :SWEEPS]
        ytail[here] = got[:, wide - SWEEPS :]
    even = side_ref[0] == 0
    head, tail = out_ref[:SWEEPS], out_ref[rows - SWEEPS :]
    xa[...] = jnp.where(even, tail, head)
    xb[...] = jnp.where(even, head, tail)


def finish_kernel(side_ref, field_ref, base_ref, cb_ref, *refs):
    out_ref, ext, work, total = refs[-4:]
    w = SWEEPS
    rows, wide, levels = field_ref.shape
    tall = rows + 2 * w
    fill_levels(ext, side_ref, field_ref[...], *refs[:4])
    around = wide + 2 * w

    def chunk(j, _):
        lanes = pl.ds(pl.multiple_of(j * LANES, LANES), LANES)
        for sweep in range(SWEEPS):

            def read(k):
                value = ext[k, :, lanes] if sweep == 0 else work[(sweep + 1) % 2, k]
                return value, cb_ref[0, k] * value

            above = read(sweep)
            mid = read(sweep + 1)
            for i in range(sweep + 1, tall - 1 - sweep):
                below = read(i + 1)
                scaled = mid[1]
                beside = (
                    above[1] + below[1]
                    + pltpu.roll(scaled, 1, 0) + pltpu.roll(scaled, around - 1, 0)
                )
                new = cb_ref[1, i] * mid[0] + beside
                if sweep == SWEEPS - 1:
                    total[i - w, :, lanes] = new[:wide]
                else:
                    work[sweep % 2, i] = new
                above, mid = mid, below
        return 0

    lax.fori_loop(0, ext.shape[2] // LANES, chunk, 0)
    out_ref[0] = base_ref[0] + total[:, :, :levels]


def swap(value, axis, start):
    pairs = [(i, i + 1) for i in range(start, lax.axis_size(axis) - 1, 2)]
    return lax.ppermute(value, axis, pairs + [(j, i) for i, j in pairs])


def halo(sides, xa, xb, yhead, ytail):
    ra = swap(xa, "gx", 0)
    rb = swap(xb, "gx", 1)
    whole = pl.BlockSpec(memory_space=pltpu.VMEM)
    tall = yhead.shape[0] + 2 * SWEEPS
    ya, yb = call(
        join_kernel,
        [shaped((tall,) + yhead.shape[1:])] * 2,
        flops=0,
        moved=16 * yhead.size,
        vmem=8,
        in_specs=[pl.BlockSpec(memory_space=pltpu.SMEM)] + [whole] * 4,
    )(sides, ra, rb, yhead, ytail)
    qa = swap(ya, "gy", 0)
    qb = swap(yb, "gy", 1)
    return ra, rb, qa, qb


def body(
    vectors, diffusivity, vertical_factor, weight_first, bias_first, weight_second,
    bias_second, weight_out, error_inverse, observed_column, owner_count,
    observed_state, channel_mask,
):
    pairs, tile_x, tile_y, levels = vectors.shape
    count_y = lax.axis_size("gy")
    devices = lax.axis_size("gx") * count_y
    slots = observed_column.shape[0]
    bucket = slots // devices
    cells = tile_x * tile_y
    grid_wide = tile_y * count_y
    units = weight_second.shape[0]
    deep = up(levels, LANES)
    tall, around = tile_x + 2 * SWEEPS, tile_y + 2 * SWEEPS
    full_l, full_u = up(levels, WIDE), up(units, WIDE)
    full_c = up(error_inverse.shape[0], WIDE)
    mark = up(levels, 16)

    sides = jnp.stack([lax.axis_index("gx") % 2, lax.axis_index("gy") % 2]).astype(jnp.int32)
    whole = pl.BlockSpec(memory_space=pltpu.VMEM)
    far = pl.BlockSpec(memory_space=pltpu.HBM)
    scalars = pl.BlockSpec(memory_space=pltpu.SMEM)
    base = pltpu.with_memory_space_constraint(vectors, pltpu.HBM)
    strips = []
    for v in range(pairs):
        deep_v = levels + (v == 0)
        cuts = call(
            functools.partial(cut_kernel, v),
            [shaped((SWEEPS, tile_y, deep_v))] * 2 + [shaped((tile_x, SWEEPS, deep_v))] * 2,
            flops=0,
            moved=4 * vectors.size,
            vmem=12,
            scratch=[pltpu.VMEM((SWEEPS, tile_y, levels), F32)] * 2
            + [pltpu.VMEM((tile_x, 8, levels), F32)] * 2
            + [pltpu.SemaphoreType.DMA((4,))],
            in_specs=[scalars, far, whole],
        )(sides, base, diffusivity)
        strips.append(halo(sides, *cuts))

    position = jnp.arange(slots, dtype=jnp.int32)
    grid_row = observed_column // grid_wide
    grid_col = observed_column % grid_wide
    target = grid_row // tile_x * count_y + grid_col // tile_y
    dest = jnp.where(position < owner_count[0], target, -1)
    cell = (grid_row % tile_x * tile_y + grid_col % tile_y + 1).astype(F32)
    packed = call(
        functools.partial(pack_kernel, bucket),
        shaped((slots, deep)),
        flops=6 * slots * slots * deep,
        moved=8 * slots * deep,
        scratch=[pltpu.VMEM((deep, slots), BF)] * 2,
        vmem=12,
    )(dest[None, :], cell[None, :], observed_state.T)
    carried = lax.all_to_all(
        packed.reshape(devices, bucket, deep), ("gx", "gy"), split_axis=0,
        concat_axis=0, tiled=True,
    ).reshape(slots, deep)

    side = max(full_l, full_u, full_c)
    weights = (vertical_factor, weight_first, weight_second, weight_out.T, error_inverse)
    first, stack = call(
        prep_kernel,
        [pltpu.HBM((2, full_l, side), BF), pltpu.HBM((4, 2, side, side), BF)],
        flops=6 * full_l * full_l * full_u,
        moved=8 * 5 * full_u * full_u,
        scratch=[pltpu.VMEM(weight.shape, F32) for weight in weights]
        + [
            pltpu.VMEM((2, full_l, side), BF), pltpu.VMEM((4, 2, side, side), BF),
            pltpu.VMEM((2, side, full_l), BF),
            pltpu.SemaphoreType.DMA((5,)), pltpu.SemaphoreType.DMA((5,)),
        ],
        vmem=27,
        in_specs=[far] * 5,
        out_specs=[far] * 2,
    )(*[pltpu.with_memory_space_constraint(weight, pltpu.HBM) for weight in weights])
    first, stack = (pltpu.with_memory_space_constraint(x, pltpu.HBM) for x in (first, stack))

    def wide_bias(bias):
        return jnp.pad(bias, (0, side - bias.shape[0]))[None, :]

    def block(v):
        return pl.BlockSpec((1, tile_x, tile_y, levels), lambda i: (v, 0, 0, 0))

    queries = []
    for v in range(pairs):
        got = call(
            functools.partial(diffuse_kernel, v > 0),
            [shaped((cells, side))] + [shaped((2, tall, around, LANES))] * (v == 0),
            flops=6 * cells * deep * full_u,
            moved=8 * tall * around * deep,
            scratch=[
                pltpu.VMEM((tall, around, deep), F32),
                pltpu.VMEM((2, tall, around, LANES), F32),
                pltpu.VMEM((cells, deep), BF),
                pltpu.VMEM((cells, deep), BF),
                pltpu.VMEM((2, side, side), BF),
                pltpu.SemaphoreType.DMA,
            ],
            grid=(1,),
            vmem=14,
            in_specs=[scalars, block(v)] + [whole] * 5 + [far],
            out_specs=[whole] * (2 - (v > 0)),
        )(sides, vectors, spread if v else diffusivity, *strips[v], stack)
        queries.append(got[0])
        if v == 0:
            spread = got[1]

    scale, one, one_t = call(
        functools.partial(hidden_kernel, mark, bucket),
        [shaped((3, slots, side)), shaped((slots, cells), BF), shaped((cells, slots), BF)],
        flops=12 * slots * full_u * full_u,
        moved=8 * slots * full_u,
        scratch=[pltpu.VMEM((slots, side), BF)] * 2
        + [
            pltpu.VMEM((slots, deep), F32),
            pltpu.VMEM((2, full_l, side), BF), pltpu.VMEM((2, side, side), BF),
            pltpu.SemaphoreType.DMA((3,)),
        ],
        vmem=18,
        in_specs=[far, far, whole, far, whole, whole],
    )(pltpu.with_memory_space_constraint(carried, pltpu.HBM), first, wide_bias(bias_first), stack, wide_bias(bias_second), channel_mask)

    fields = []
    for v in range(pairs):
        fields.append(
            call(
                net_kernel,
                [shaped((tile_x, tile_y, levels))]
                + [shaped((SWEEPS, tile_y, levels))] * 2
                + [shaped((tile_x, SWEEPS, levels))] * 2,
                flops=36 * slots * full_u * full_u,
                moved=4 * 5 * full_u * full_u,
                scratch=[pltpu.VMEM((2, slots, side), BF)]
                + [pltpu.VMEM((2, slots // 2, side), BF)] * 2
                + [pltpu.VMEM((slots // 2, side), F32)] * 2
                + [
                    pltpu.VMEM((4, 2, side, side), BF),
                    pltpu.SemaphoreType.DMA((4,)),
                ],
                vmem=22,
                in_specs=[scalars] + [whole] * 4 + [far],
            )(sides, queries[v], one, one_t, scale, stack)
        )

    out = None
    for v in range(pairs):
        around_field = halo(sides, *fields[v][1:])
        carry = [] if out is None else [out]
        out = call(
            finish_kernel,
            shaped(vectors.shape),
            flops=40 * tall * around * deep,
            moved=12 * cells * deep,
            scratch=[
                pltpu.VMEM((tall, around, deep), F32),
                pltpu.VMEM((2, tall, around, LANES), F32),
                pltpu.VMEM((tile_x, tile_y, deep), F32),
            ],
            grid=(1,),
            vmem=14,
            in_specs=[scalars, whole, block(v)] + [whole] * 5
            + [pl.BlockSpec(memory_space=pl.ANY)] * len(carry),
            out_specs=block(v),
            input_output_aliases={8: 0} if carry else {},
        )(sides, fields[v][0], vectors, spread, *around_field, *carry)
    return out


def solution(mesh):
    in_specs = (
        P(None, "gx", "gy", None),
        P("gx", "gy"),
        P(),
        P(),
        P(),
        P(),
        P(),
        P(),
        P(),
        P(("gx", "gy")),
        P(("gx", "gy")),
        P(("gx", "gy"), None),
        P(),
    )
    out_specs = P(None, "gx", "gy", None)
    return jax.shard_map(body, mesh=mesh, in_specs=in_specs, out_specs=out_specs, check_vma=False)
```

```python
import functools

import jax
import jax.numpy as jnp
from jax import lax
from jax.experimental import pallas as pl
from jax.experimental.pallas import tpu as pltpu
from jax.sharding import PartitionSpec as P

SWEEPS = 4
WIDE = 256
LANES = 128
BF = jnp.bfloat16
F32 = jnp.float32
NN = ((1,), (0,))
NT = ((1,), (1,))


def up(size, unit):
    return -(-size // unit) * unit


def split(value):
    high = value.astype(BF)
    return high, (value - high.astype(F32)).astype(BF)


def mm(left, right, dims=NN):
    return lax.dot_general(left, right, (dims, ((), ())), preferred_element_type=F32)


def mm3(left_high, left_low, right_high, right_low, dims=NN):
    left = jnp.concatenate([left_high, left_low, left_high], axis=dims[0][0])
    right = jnp.concatenate([right_high, right_high, right_low], axis=dims[1][0])
    return mm(left, right, dims)


def halves(size):
    half = size // 2
    return [pl.ds(0, half), pl.ds(half, half)] if half % 16 == 0 else [pl.ds(0, size)]


def iota(shape, axis):
    return lax.broadcasted_iota(jnp.int32, shape, axis)


def call(kernel, out_shape, flops, moved, scratch=(), vmem=48, **more):
    return pl.pallas_call(
        kernel,
        out_shape=out_shape,
        scratch_shapes=list(scratch),
        compiler_params=pltpu.CompilerParams(vmem_limit_bytes=vmem * 1024 * 1024),
        cost_estimate=pl.CostEstimate(flops=flops, bytes_accessed=moved, transcendentals=0),
        **more,
    )


def shaped(shape, dtype=F32):
    return jax.ShapeDtypeStruct(shape, dtype)


def pack_kernel(bucket, dest_ref, cell_ref, state_ref, out_ref, high_ref, low_ref):
    levels, slots = state_ref.shape
    devices = slots // bucket
    dest = dest_ref[...]
    same = (iota((devices, slots), 0) == dest).astype(F32)
    before = (iota((slots, slots), 0) < iota((slots, slots), 1)).astype(BF)
    rank = jnp.sum(same * mm(same.astype(BF), before), axis=0, keepdims=True)
    place = dest * bucket + rank.astype(jnp.int32)
    pick = (iota((slots, slots), 0) == place).astype(BF)
    high_ref[...] = jnp.zeros_like(high_ref)
    low_ref[...] = jnp.zeros_like(low_ref)
    high, low = split(state_ref[...])
    high_ref[:levels, :] = high
    low_ref[:levels, :] = low
    mark = up(levels, 16)
    tall = jnp.where(iota((16, slots), 0) == 0, cell_ref[...], 0.0)
    high, low = split(tall)
    high_ref[mark : mark + 16, :] = high
    low_ref[mark : mark + 16, :] = low
    rows = mm(pick, high_ref[...], NT) + mm(pick, low_ref[...], NT)
    if out_ref.shape == rows.shape:
        out_ref[...] = rows
        return
    whole = rows.shape[1] // LANES - 1
    for k in range(whole):
        piece = rows[:, k * LANES : (k + 1) * LANES].reshape(devices, bucket, LANES)
        out_ref[:, k * bucket : (k + 1) * bucket, :] = piece
    tail = rows[:, whole * LANES :].reshape(devices, bucket, LANES)
    half = bucket // 2
    left = iota((devices, half, LANES), 2) < LANES // 2
    turned = pltpu.roll(tail[:, half:], LANES // 2, 2)
    out_ref[:, whole * bucket :, :] = jnp.where(left, tail[:, :half], turned)


def prep_kernel(*refs):
    ins, (first_out, stack_out), refs = refs[:5], refs[5:7], refs[7:]
    raw, (first, stack, turned, in_sem, out_sem) = refs[:5], refs[5:]
    fetch = [
        pltpu.make_async_copy(ins[k], raw[k], in_sem.at[k]) for k in range(5)
    ]
    for copy in fetch:
        copy.start()
    sends = []

    def send(source, target):
        copy = pltpu.make_async_copy(source, target, out_sem.at[len(sends)])
        copy.start()
        sends.append(copy)

    def put(values, ref):
        rows, cols = values.shape
        if (rows, cols) != ref.shape[1:]:
            ref[...] = jnp.zeros_like(ref)
        ref[0, :rows, :cols], ref[1, :rows, :cols] = split(values)

    fetch[0].wait()
    put(raw[0][...].T, turned)
    fetch[1].wait()
    put(raw[1][...], first)
    send(first, first_out)
    rows = up(raw[0].shape[1], LANES)
    stack[3, :, rows:, :] = jnp.zeros((2,) + (stack.shape[2] - rows, stack.shape[3]), BF)
    for part in halves(rows):
        got = mm3(turned[0, part, :], turned[1, part, :], first[0], first[1])
        stack[3, 0, part, :], stack[3, 1, part, :] = split(got)
    send(stack.at[3], stack_out.at[3])
    for k in range(3):
        fetch[k + 2].wait()
        put(raw[k + 2][...], stack.at[k])
        send(stack.at[k], stack_out.at[k])
    for copy in sends:
        copy.wait()


def coeff_column(coeff_ref, row):
    wide = coeff_ref.shape[1]
    spread = jnp.broadcast_to(coeff_ref[row : row + 1, :], (wide, wide))
    diagonal = iota((wide, wide), 0) == iota((wide, wide), 1)
    return jnp.sum(jnp.where(diagonal, spread, 0.0), axis=1, keepdims=True)


def cut_kernel(v, side_ref, vectors_ref, coeff_ref, xa, xb, yhead, ytail, *refs):
    bufs, sems = refs[:4], refs[4]
    rows, wide, levels = vectors_ref.shape[1:]
    w = SWEEPS
    parts = (
        vectors_ref.at[v, pl.ds(0, w)],
        vectors_ref.at[v, pl.ds(rows - w, w)],
        vectors_ref.at[v, :, pl.ds(0, 8)],
        vectors_ref.at[v, :, pl.ds(wide - 8, 8)],
    )
    copies = [pltpu.make_async_copy(parts[k], bufs[k], sems.at[k]) for k in range(4)]
    for copy in copies:
        copy.start()
    even = side_ref[0] == 0
    if v == 0:
        columns = [coeff_column(coeff_ref, row) for row in range(rows)]
        for row in range(w):
            head, tail = columns[row], columns[rows - w + row]
            xa[row, :, levels:] = jnp.where(even, tail, head)
            xb[row, :, levels:] = jnp.where(even, head, tail)
        for row in range(rows):
            yhead[row, :, levels:] = columns[row][:w]
            ytail[row, :, levels:] = columns[row][wide - w :]
    for copy in copies:
        copy.wait()
    head, tail = bufs[0][...], bufs[1][...]
    xa[:, :, :levels] = jnp.where(even, tail, head)
    xb[:, :, :levels] = jnp.where(even, head, tail)
    yhead[:, :, :levels] = bufs[2][:, :w]
    ytail[:, :, :levels] = bufs[3][:, 8 - w :]


def join_kernel(side_ref, ra, rb, yhead, ytail, ya, yb):
    w = SWEEPS
    rows = yhead.shape[0]
    wide = ra.shape[1]
    even_x, even_y = side_ref[0] == 0, side_ref[1] == 0

    for here, first, second in (
        (pl.ds(0, w), rb, ra),
        (pl.ds(w + rows, w), ra, rb),
    ):
        head = jnp.where(even_x, first[:, :w], second[:, :w])
        tail = jnp.where(even_x, first[:, wide - w :], second[:, wide - w :])
        ya[here] = jnp.where(even_y, tail, head)
        yb[here] = jnp.where(even_y, head, tail)
    here = pl.ds(w, rows)
    ya[here] = jnp.where(even_y, ytail[...], yhead[...])
    yb[here] = jnp.where(even_y, yhead[...], ytail[...])


def fill(ext, side_ref, tile, ra, rb, qa, qb, part):
    rows, wide = tile.shape[:2]
    w = SWEEPS
    even_y = side_ref[1] == 0
    upper = jnp.where(side_ref[0] == 0, w + rows, 0)
    tile_part, strip_part = part
    ext[w : w + rows, :wide, tile_part] = tile
    ext[pl.ds(upper, w), :wide, tile_part] = strip_part(ra)
    ext[pl.ds(w + rows - upper, w), :wide, tile_part] = strip_part(rb)
    qa, qb = strip_part(qa), strip_part(qb)
    ext[:, wide : wide + w, tile_part] = jnp.where(even_y, qa, qb)
    ext[:, wide + w :, tile_part] = jnp.where(even_y, qb, qa)


def fill_levels(ext, side_ref, tile, *strips):
    levels = tile.shape[2]
    last = up(levels, LANES) - LANES
    ext[:, :, last:] = jnp.zeros((ext.shape[0], ext.shape[1], ext.shape[2] - last), F32)
    part = (pl.ds(0, levels), lambda ref: ref[:, :, :levels])
    fill(ext, side_ref, tile, *strips, part)


def diffuse_kernel(v, side_ref, tile_ref, coeff_ref, *refs):
    strips, stack_ref, refs = refs[:4], refs[4], refs[5:]
    ext, work, high_ref, low_ref, both, sem = refs[-6:]
    out_ref = refs[0]
    fetch = pltpu.make_async_copy(stack_ref.at[3], both, sem)
    fetch.start()
    w = SWEEPS
    rows, wide, levels = tile_ref.shape[1:]
    tall = rows + 2 * w
    around = wide + 2 * w
    fill_levels(ext, side_ref, tile_ref[v], *strips)
    if v > 0:
        cb_ref = coeff_ref
    else:
        cb_ref = refs[1]

        def spread(ref):
            column = ref[:, :, levels : levels + 1]
            return jnp.broadcast_to(column, column.shape[:2] + (LANES,))

        own = jnp.stack(
            [jnp.broadcast_to(coeff_column(coeff_ref, k), (wide, LANES)) for k in range(rows)]
        )
        fill(cb_ref.at[0], side_ref, own, *strips, (pl.ds(0, LANES), spread))
        cb_ref[1] = 1.0 - 4.0 * cb_ref[0]

    def chunk(j, _):
        lanes = pl.ds(pl.multiple_of(j * LANES, LANES), LANES)
        for sweep in range(SWEEPS):
            for i in range(sweep + 1, tall - 1 - sweep):
                if sweep == 0:
                    above, mid, below = (ext[k, :, lanes] for k in (i - 1, i, i + 1))
                else:
                    above, mid, below = (work[(sweep + 1) % 2, k] for k in (i - 1, i, i + 1))
                beside = above + below + pltpu.roll(mid, 1, 0) + pltpu.roll(mid, around - 1, 0)
                new = cb_ref[1, i] * mid + cb_ref[0, i] * beside
                if sweep == SWEEPS - 1:
                    high, low = split(new[:wide])
                    here = pl.ds((i - w) * wide, wide)
                    high_ref[here, lanes] = high
                    low_ref[here, lanes] = low
                else:
                    work[sweep % 2, i] = new
        return 0

    lax.fori_loop(0, ext.shape[2] // LANES, chunk, 0)
    deep = ext.shape[2]
    fetch.wait()
    for part in halves(out_ref.shape[0]):
        out_ref[part, :] = mm3(
            high_ref[part, :], low_ref[part, :], both[0, :deep], both[1, :deep]
        )


def hidden_kernel(
    mark, bucket, x_ref, first_ref, b1_ref, stack_ref, b2_ref, mask_ref,
    scale_ref, one_ref, one_t_ref, high_ref, low_ref, x_buf, first, second, sems,
):
    fetch_x = pltpu.make_async_copy(x_ref, x_buf, sems.at[2])
    fetch_x.start()
    fetch_first = pltpu.make_async_copy(first_ref, first, sems.at[0])
    fetch_second = pltpu.make_async_copy(stack_ref.at[0], second, sems.at[1])
    fetch_first.start()
    fetch_second.start()
    s1_ref, s2_ref, gate_ref = (scale_ref.at[k] for k in range(3))
    slots, cells = one_ref.shape
    devices, channels = mask_ref.shape
    fetch_x.wait()
    if len(x_buf.shape) == 2:
        deep = x_buf.shape[1]
        pieces = [x_buf[:, k : k + LANES] for k in range(0, deep, LANES)]
    else:
        whole = x_buf.shape[1] // bucket
        deep = (whole + 1) * LANES
        pieces = [
            x_buf[:, k * bucket : (k + 1) * bucket, :].reshape(slots, LANES)
            for k in range(whole)
        ]
        tail = x_buf[:, whole * bucket :, :]
        tail = jnp.concatenate([tail, pltpu.roll(tail, LANES // 2, 2)], axis=1)
        pieces.append(tail.reshape(slots, LANES))
    index = pieces[-1][:, mark % LANES : mark % LANES + 1]
    cell = index.astype(jnp.int32) - 1
    live = index > 0.5
    one_ref[...] = (iota((slots, cells), 1) == cell).astype(BF)
    flat = jnp.broadcast_to(index, (slots, LANES)).T[0:1, :].astype(jnp.int32) - 1
    one_t_ref[...] = (iota((cells, slots), 0) == flat).astype(BF)
    begin = iota((slots, devices), 1) * bucket
    at = iota((slots, devices), 0)
    from_owner = ((at >= begin) & (at < begin + bucket) & live).astype(BF)
    gate_ref[...] = jnp.zeros_like(gate_ref)
    gate_ref[:, :channels] = mm(from_owner, mask_ref[...].astype(F32).astype(BF))
    for k, piece in enumerate(pieces):
        here = pl.ds(k * LANES, LANES)
        high_ref[:, here], low_ref[:, here] = split(piece)
    parts = halves(slots)
    fetch_first.wait()
    for part in parts:
        got = mm3(high_ref[part, :deep], low_ref[part, :deep], first[0, :deep], first[1, :deep])
        hidden = jnp.tanh(got + b1_ref[...])
        s1_ref[part, :] = 1.0 - hidden * hidden
        high, low = split(hidden)
        high_ref[part, :] = high
        low_ref[part, :] = low
    fetch_second.wait()
    for part in parts:
        got = mm3(high_ref[part, :], low_ref[part, :], second[0], second[1])
        hidden = jnp.tanh(got + b2_ref[...])
        s2_ref[part, :] = 1.0 - hidden * hidden


LAYERS = ((0, 0, 1), (1, 1, 2), (2, 0, 2), (1, 0, 1), (0, 1, 0))


def table(values, layer):
    value = jnp.int32(values[0])
    for k in range(1, len(values)):
        value = jnp.where(layer == k, values[k], value)
    return value


def net_kernel(
    side_ref, q_ref, one_ref, one_t_ref, scale_ref, stack_ref,
    out_ref, xa, xb, yhead, ytail, x1, top, low, acc_top, acc_low, stack, sems,
):
    fetch = [
        pltpu.make_async_copy(stack_ref.at[k], stack.at[k], sems.at[k]) for k in range(4)
    ]
    for copy in fetch:
        copy.start()
    slots = q_ref.shape[0]
    half = slots // 2
    first, second = pl.ds(0, half), pl.ds(half, half)

    def pick(picker):
        return mm(picker, x1[0]) + mm(picker, x1[1])

    def close(acc, scale, part, target):
        target[0], target[1] = split(acc[...] * scale_ref[scale, part, :])

    x1[0], x1[1] = split(q_ref[...])
    acc_top[...] = pick(one_ref[first, :])
    acc_low[...] = pick(one_ref[second, :])
    close(acc_top, 0, first, top)
    fetch[0].wait()
    scales = [0] + [entry[2] for entry in LAYERS]

    def step(layer, _):
        for k in (1, 2):

            @pl.when(layer == k)
            def _():
                fetch[k].wait()

        weight = table([entry[0] for entry in LAYERS], layer)
        turned = table([entry[1] for entry in LAYERS], layer)
        before, after = table(scales[:-1], layer), table(scales[1:], layer)

        def run(dims):
            acc_top[...] = mm3(top[0], top[1], stack[weight, 0], stack[weight, 1], dims)
            close(acc_low, before, second, low)
            acc_low[...] = mm3(low[0], low[1], stack[weight, 0], stack[weight, 1], dims)
            close(acc_top, after, first, top)

        @pl.when(turned == 0)
        def _():
            run(NN)

        @pl.when(turned == 1)
        def _():
            run(NT)

        return 0

    lax.fori_loop(0, len(LAYERS), step, 0)
    close(acc_low, scales[-1], second, low)
    for part in halves(one_t_ref.shape[0]):
        got = mm(one_t_ref[part, :half], top[0]) + mm(one_t_ref[part, :half], top[1])
        got = got + mm(one_t_ref[part, half:], low[0]) + mm(one_t_ref[part, half:], low[1])
        x1[0, part, :], x1[1, part, :] = split(got)
    fetch[3].wait()
    rows, wide, levels = out_ref.shape
    for k, part in enumerate(halves(rows * wide)):
        got = mm3(x1[0, part, :], x1[1, part, :], stack[3, 0], stack[3, 1], NT)
        tall = got.shape[0] // wide
        got = got.reshape(tall, wide, got.shape[1])[:, :, :levels]
        here = pl.ds(k * tall, tall)
        out_ref[here] = got
        yhead[here] = got[:, :SWEEPS]
        ytail[here] = got[:, wide - SWEEPS :]
    even = side_ref[0] == 0
    head, tail = out_ref[:SWEEPS], out_ref[rows - SWEEPS :]
    xa[...] = jnp.where(even, tail, head)
    xb[...] = jnp.where(even, head, tail)


def finish_kernel(v, side_ref, field_ref, base_ref, cb_ref, *refs):
    out_ref, ext, work, total, result, sems = refs[-6:]
    w = SWEEPS
    rows, wide, levels = field_ref.shape
    tall = rows + 2 * w
    fill_levels(ext, side_ref, field_ref[...], *refs[:4])
    around = wide + 2 * w

    def chunk(j, _):
        lanes = pl.ds(pl.multiple_of(j * LANES, LANES), LANES)
        for sweep in range(SWEEPS):

            def read(k):
                value = ext[k, :, lanes] if sweep == 0 else work[(sweep + 1) % 2, k]
                return value, cb_ref[0, k] * value

            above = read(sweep)
            mid = read(sweep + 1)
            for i in range(sweep + 1, tall - 1 - sweep):
                below = read(i + 1)
                scaled = mid[1]
                beside = (
                    above[1] + below[1]
                    + pltpu.roll(scaled, 1, 0) + pltpu.roll(scaled, around - 1, 0)
                )
                new = cb_ref[1, i] * mid[0] + beside
                if sweep == SWEEPS - 1:
                    total[i - w, :, lanes] = new[:wide]
                else:
                    work[sweep % 2, i] = new
                above, mid = mid, below
        return 0

    lax.fori_loop(0, ext.shape[2] // LANES, chunk, 0)
    sends = []
    for k in range(2):
        part = pl.ds(k * (rows // 2), rows // 2)
        result[part] = base_ref[v, part] + total[part, :, :levels]
        sends.append(pltpu.make_async_copy(result.at[part], out_ref.at[v, part], sems.at[k]))
        sends[-1].start()
    for copy in sends:
        copy.wait()


def swap(value, axis, start):
    pairs = [(i, i + 1) for i in range(start, lax.axis_size(axis) - 1, 2)]
    return lax.ppermute(value, axis, pairs + [(j, i) for i, j in pairs])


def halo(sides, xa, xb, yhead, ytail):
    ra = swap(xa, "gx", 0)
    rb = swap(xb, "gx", 1)
    whole = pl.BlockSpec(memory_space=pltpu.VMEM)
    tall = yhead.shape[0] + 2 * SWEEPS
    ya, yb = call(
        join_kernel,
        [shaped((tall,) + yhead.shape[1:])] * 2,
        flops=0,
        moved=16 * yhead.size,
        vmem=8,
        in_specs=[pl.BlockSpec(memory_space=pltpu.SMEM)] + [whole] * 4,
    )(sides, ra, rb, yhead, ytail)
    qa = swap(ya, "gy", 0)
    qb = swap(yb, "gy", 1)
    return ra, rb, qa, qb


def body(
    vectors, diffusivity, vertical_factor, weight_first, bias_first, weight_second,
    bias_second, weight_out, error_inverse, observed_column, owner_count,
    observed_state, channel_mask,
):
    pairs, tile_x, tile_y, levels = vectors.shape
    count_y = lax.axis_size("gy")
    devices = lax.axis_size("gx") * count_y
    slots = observed_column.shape[0]
    bucket = slots // devices
    cells = tile_x * tile_y
    grid_wide = tile_y * count_y
    units = weight_second.shape[0]
    deep = up(levels, LANES)
    tall, around = tile_x + 2 * SWEEPS, tile_y + 2 * SWEEPS
    full_l, full_u = up(levels, WIDE), up(units, WIDE)
    full_c = up(error_inverse.shape[0], WIDE)
    mark = up(levels, 16)

    sides = jnp.stack([lax.axis_index("gx") % 2, lax.axis_index("gy") % 2]).astype(jnp.int32)
    whole = pl.BlockSpec(memory_space=pltpu.VMEM)
    far = pl.BlockSpec(memory_space=pltpu.HBM)
    scalars = pl.BlockSpec(memory_space=pltpu.SMEM)
    base = pltpu.with_memory_space_constraint(vectors, pltpu.HBM)
    strips = []
    for v in range(pairs):
        deep_v = levels + (v == 0)
        cuts = call(
            functools.partial(cut_kernel, v),
            [shaped((SWEEPS, tile_y, deep_v))] * 2 + [shaped((tile_x, SWEEPS, deep_v))] * 2,
            flops=0,
            moved=4 * vectors.size,
            vmem=12,
            scratch=[pltpu.VMEM((SWEEPS, tile_y, levels), F32)] * 2
            + [pltpu.VMEM((tile_x, 8, levels), F32)] * 2
            + [pltpu.SemaphoreType.DMA((4,))],
            in_specs=[scalars, far, whole],
        )(sides, base, diffusivity)
        strips.append(halo(sides, *cuts))

    position = jnp.arange(slots, dtype=jnp.int32)
    grid_row = observed_column // grid_wide
    grid_col = observed_column % grid_wide
    target = grid_row // tile_x * count_y + grid_col // tile_y
    dest = jnp.where(position < owner_count[0], target, -1)
    cell = (grid_row % tile_x * tile_y + grid_col % tile_y + 1).astype(F32)
    tight = bucket % 16 == 0 and mark // LANES == deep // LANES - 1 and mark % LANES < LANES // 2
    packed_shape = (slots, deep)
    if tight:
        packed_shape = (devices, bucket * (deep // LANES - 1) + bucket // 2, LANES)
    packed = call(
        functools.partial(pack_kernel, bucket),
        shaped(packed_shape),
        flops=6 * slots * slots * deep,
        moved=8 * slots * deep,
        scratch=[pltpu.VMEM((deep, slots), BF)] * 2,
        vmem=12,
    )(dest[None, :], cell[None, :], observed_state.T)
    carried = lax.all_to_all(
        packed if tight else packed.reshape(devices, bucket, deep), ("gx", "gy"),
        split_axis=0, concat_axis=0, tiled=True,
    ).reshape(packed_shape)

    side = max(full_l, full_u, full_c)
    weights = (vertical_factor, weight_first, weight_second, weight_out.T, error_inverse)
    first, stack = call(
        prep_kernel,
        [pltpu.HBM((2, full_l, side), BF), pltpu.HBM((4, 2, side, side), BF)],
        flops=6 * full_l * full_l * full_u,
        moved=8 * 5 * full_u * full_u,
        scratch=[pltpu.VMEM(weight.shape, F32) for weight in weights]
        + [
            pltpu.VMEM((2, full_l, side), BF), pltpu.VMEM((4, 2, side, side), BF),
            pltpu.VMEM((2, side, full_l), BF),
            pltpu.SemaphoreType.DMA((5,)), pltpu.SemaphoreType.DMA((5,)),
        ],
        vmem=27,
        in_specs=[far] * 5,
        out_specs=[far] * 2,
    )(*[pltpu.with_memory_space_constraint(weight, pltpu.HBM) for weight in weights])
    first, stack = (pltpu.with_memory_space_constraint(x, pltpu.HBM) for x in (first, stack))

    def wide_bias(bias):
        return jnp.pad(bias, (0, side - bias.shape[0]))[None, :]

    queries = []
    for v in range(pairs):
        got = call(
            functools.partial(diffuse_kernel, v),
            [shaped((cells, side))] + [shaped((2, tall, around, LANES))] * (v == 0),
            flops=6 * cells * deep * full_u,
            moved=8 * tall * around * deep,
            scratch=[
                pltpu.VMEM((tall, around, deep), F32),
                pltpu.VMEM((2, tall, around, LANES), F32),
                pltpu.VMEM((cells, deep), BF),
                pltpu.VMEM((cells, deep), BF),
                pltpu.VMEM((2, side, side), BF),
                pltpu.SemaphoreType.DMA,
            ],
            vmem=16,
            in_specs=[scalars, whole] + [whole] * 5 + [far],
            out_specs=[whole] * (2 - (v > 0)),
        )(sides, vectors, spread if v else diffusivity, *strips[v], stack)
        queries.append(got[0])
        if v == 0:
            spread = got[1]

    scale, one, one_t = call(
        functools.partial(hidden_kernel, mark, bucket),
        [shaped((3, slots, side)), shaped((slots, cells), BF), shaped((cells, slots), BF)],
        flops=12 * slots * full_u * full_u,
        moved=8 * slots * full_u,
        scratch=[pltpu.VMEM((slots, side), BF)] * 2
        + [
            pltpu.VMEM(packed_shape, F32),
            pltpu.VMEM((2, full_l, side), BF), pltpu.VMEM((2, side, side), BF),
            pltpu.SemaphoreType.DMA((3,)),
        ],
        vmem=18,
        in_specs=[far, far, whole, far, whole, whole],
    )(pltpu.with_memory_space_constraint(carried, pltpu.HBM), first, wide_bias(bias_first), stack, wide_bias(bias_second), channel_mask)

    fields = []
    for v in range(pairs):
        fields.append(
            call(
                net_kernel,
                [shaped((tile_x, tile_y, levels))]
                + [shaped((SWEEPS, tile_y, levels))] * 2
                + [shaped((tile_x, SWEEPS, levels))] * 2,
                flops=36 * slots * full_u * full_u,
                moved=4 * 5 * full_u * full_u,
                scratch=[pltpu.VMEM((2, slots, side), BF)]
                + [pltpu.VMEM((2, slots // 2, side), BF)] * 2
                + [pltpu.VMEM((slots // 2, side), F32)] * 2
                + [
                    pltpu.VMEM((4, 2, side, side), BF),
                    pltpu.SemaphoreType.DMA((4,)),
                ],
                vmem=22,
                in_specs=[scalars] + [whole] * 4 + [far],
            )(sides, queries[v], one, one_t, scale, stack)
        )

    out = None
    for v in range(pairs):
        around_field = halo(sides, *fields[v][1:])
        carry = [] if out is None else [out]
        out = call(
            functools.partial(finish_kernel, v),
            pltpu.HBM(vectors.shape, F32),
            flops=40 * tall * around * deep,
            moved=12 * cells * deep,
            scratch=[
                pltpu.VMEM((tall, around, deep), F32),
                pltpu.VMEM((2, tall, around, LANES), F32),
                pltpu.VMEM((tile_x, tile_y, deep), F32),
                pltpu.VMEM((tile_x, tile_y, levels), F32),
                pltpu.SemaphoreType.DMA((2,)),
            ],
            vmem=16,
            in_specs=[scalars] + [whole] * 7 + [far] * len(carry),
            out_specs=far,
            input_output_aliases={8: 0} if carry else {},
        )(sides, fields[v][0], vectors, spread, *around_field, *carry)
    return out


def solution(mesh):
    in_specs = (
        P(None, "gx", "gy", None),
        P("gx", "gy"),
        P(),
        P(),
        P(),
        P(),
        P(),
        P(),
        P(),
        P(("gx", "gy")),
        P(("gx", "gy")),
        P(("gx", "gy"), None),
        P(),
    )
    out_specs = P(None, "gx", "gy", None)
    return jax.shard_map(body, mesh=mesh, in_specs=in_specs, out_specs=out_specs, check_vma=False)
```

```python
import functools

import jax
import jax.numpy as jnp
from jax import lax
from jax.experimental import pallas as pl
from jax.experimental.pallas import tpu as pltpu
from jax.sharding import PartitionSpec as P

SWEEPS = 4
WIDE = 256
LANES = 128
BF = jnp.bfloat16
F32 = jnp.float32
NN = ((1,), (0,))
NT = ((1,), (1,))


def up(size, unit):
    return -(-size // unit) * unit


def split(value):
    high = value.astype(BF)
    return high, (value - high.astype(F32)).astype(BF)


def mm(left, right, dims=NN):
    return lax.dot_general(left, right, (dims, ((), ())), preferred_element_type=F32)


def mm3(left_high, left_low, right_high, right_low, dims=NN):
    left = jnp.concatenate([left_high, left_low, left_high], axis=dims[0][0])
    right = jnp.concatenate([right_high, right_high, right_low], axis=dims[1][0])
    return mm(left, right, dims)


def halves(size):
    half = size // 2
    return [pl.ds(0, half), pl.ds(half, half)] if half % 16 == 0 else [pl.ds(0, size)]


def iota(shape, axis):
    return lax.broadcasted_iota(jnp.int32, shape, axis)


def call(kernel, out_shape, flops, moved, scratch=(), vmem=48, **more):
    return pl.pallas_call(
        kernel,
        out_shape=out_shape,
        scratch_shapes=list(scratch),
        compiler_params=pltpu.CompilerParams(vmem_limit_bytes=vmem * 1024 * 1024),
        cost_estimate=pl.CostEstimate(flops=flops, bytes_accessed=moved, transcendentals=0),
        **more,
    )


def shaped(shape, dtype=F32):
    return jax.ShapeDtypeStruct(shape, dtype)


def pack_kernel(bucket, dest_ref, cell_ref, state_ref, out_ref, high_ref, low_ref):
    levels, slots = state_ref.shape
    devices = slots // bucket
    dest = dest_ref[...]
    same = (iota((devices, slots), 0) == dest).astype(F32)
    before = (iota((slots, slots), 0) < iota((slots, slots), 1)).astype(BF)
    rank = jnp.sum(same * mm(same.astype(BF), before), axis=0, keepdims=True)
    place = dest * bucket + rank.astype(jnp.int32)
    pick = (iota((slots, slots), 0) == place).astype(BF)
    high_ref[...] = jnp.zeros_like(high_ref)
    low_ref[...] = jnp.zeros_like(low_ref)
    high, low = split(state_ref[...])
    high_ref[:levels, :] = high
    low_ref[:levels, :] = low
    mark = up(levels, 16)
    tall = jnp.where(iota((16, slots), 0) == 0, cell_ref[...], 0.0)
    high, low = split(tall)
    high_ref[mark : mark + 16, :] = high
    low_ref[mark : mark + 16, :] = low
    rows = mm(pick, high_ref[...], NT) + mm(pick, low_ref[...], NT)
    if out_ref.shape == rows.shape:
        out_ref[...] = rows
        return
    whole = rows.shape[1] // LANES - 1
    for k in range(whole):
        piece = rows[:, k * LANES : (k + 1) * LANES].reshape(devices, bucket, LANES)
        out_ref[:, k * bucket : (k + 1) * bucket, :] = piece
    tail = rows[:, whole * LANES :].reshape(devices, bucket, LANES)
    half = bucket // 2
    left = iota((devices, half, LANES), 2) < LANES // 2
    turned = pltpu.roll(tail[:, half:], LANES // 2, 2)
    out_ref[:, whole * bucket :, :] = jnp.where(left, tail[:, :half], turned)


def prep_kernel(*refs):
    ins, (first_out, stack_out), refs = refs[:5], refs[5:7], refs[7:]
    raw, (first, stack, turned, in_sem, out_sem) = refs[:5], refs[5:]
    fetch = [
        pltpu.make_async_copy(ins[k], raw[k], in_sem.at[k]) for k in range(5)
    ]
    for copy in fetch:
        copy.start()
    sends = []

    def send(source, target):
        copy = pltpu.make_async_copy(source, target, out_sem.at[len(sends)])
        copy.start()
        sends.append(copy)

    def put(values, ref):
        rows, cols = values.shape
        if (rows, cols) != ref.shape[1:]:
            ref[...] = jnp.zeros_like(ref)
        ref[0, :rows, :cols], ref[1, :rows, :cols] = split(values)

    fetch[0].wait()
    put(raw[0][...].T, turned)
    fetch[1].wait()
    put(raw[1][...], first)
    send(first, first_out)
    rows = up(raw[0].shape[1], LANES)
    stack[3, :, rows:, :] = jnp.zeros((2,) + (stack.shape[2] - rows, stack.shape[3]), BF)
    for part in halves(rows):
        got = mm3(turned[0, part, :], turned[1, part, :], first[0], first[1])
        stack[3, 0, part, :], stack[3, 1, part, :] = split(got)
    send(stack.at[3], stack_out.at[3])
    for k in range(3):
        fetch[k + 2].wait()
        put(raw[k + 2][...], stack.at[k])
        send(stack.at[k], stack_out.at[k])
    for copy in sends:
        copy.wait()


def coeff_column(coeff_ref, row):
    wide = coeff_ref.shape[1]
    spread = jnp.broadcast_to(coeff_ref[row : row + 1, :], (wide, wide))
    diagonal = iota((wide, wide), 0) == iota((wide, wide), 1)
    return jnp.sum(jnp.where(diagonal, spread, 0.0), axis=1, keepdims=True)


def cut_kernel(v, side_ref, vectors_ref, coeff_ref, xa, xb, yhead, ytail, *refs):
    bufs, sems = refs[:4], refs[4]
    rows, wide, levels = vectors_ref.shape[1:]
    w = SWEEPS
    parts = (
        vectors_ref.at[v, pl.ds(0, w)],
        vectors_ref.at[v, pl.ds(rows - w, w)],
        vectors_ref.at[v, :, pl.ds(0, 8)],
        vectors_ref.at[v, :, pl.ds(wide - 8, 8)],
    )
    copies = [pltpu.make_async_copy(parts[k], bufs[k], sems.at[k]) for k in range(4)]
    for copy in copies:
        copy.start()
    even = side_ref[0] == 0
    if v == 0:
        columns = [coeff_column(coeff_ref, row) for row in range(rows)]
        for row in range(w):
            head, tail = columns[row], columns[rows - w + row]
            xa[row, :, levels:] = jnp.where(even, tail, head)
            xb[row, :, levels:] = jnp.where(even, head, tail)
        for row in range(rows):
            yhead[row, :, levels:] = columns[row][:w]
            ytail[row, :, levels:] = columns[row][wide - w :]
    for copy in copies:
        copy.wait()
    head, tail = bufs[0][...], bufs[1][...]
    xa[:, :, :levels] = jnp.where(even, tail, head)
    xb[:, :, :levels] = jnp.where(even, head, tail)
    yhead[:, :, :levels] = bufs[2][:, :w]
    ytail[:, :, :levels] = bufs[3][:, 8 - w :]


def join_kernel(side_ref, ra, rb, yhead, ytail, ya, yb):
    w = SWEEPS
    rows = yhead.shape[0]
    wide = ra.shape[1]
    even_x, even_y = side_ref[0] == 0, side_ref[1] == 0

    for here, first, second in (
        (pl.ds(0, w), rb, ra),
        (pl.ds(w + rows, w), ra, rb),
    ):
        head = jnp.where(even_x, first[:, :w], second[:, :w])
        tail = jnp.where(even_x, first[:, wide - w :], second[:, wide - w :])
        ya[here] = jnp.where(even_y, tail, head)
        yb[here] = jnp.where(even_y, head, tail)
    here = pl.ds(w, rows)
    ya[here] = jnp.where(even_y, ytail[...], yhead[...])
    yb[here] = jnp.where(even_y, yhead[...], ytail[...])


def fill(ext, side_ref, tile, ra, rb, qa, qb, part):
    rows, wide = tile.shape[:2]
    w = SWEEPS
    even_y = side_ref[1] == 0
    upper = jnp.where(side_ref[0] == 0, w + rows, 0)
    tile_part, strip_part = part
    ext[w : w + rows, :wide, tile_part] = tile
    ext[pl.ds(upper, w), :wide, tile_part] = strip_part(ra)
    ext[pl.ds(w + rows - upper, w), :wide, tile_part] = strip_part(rb)
    qa, qb = strip_part(qa), strip_part(qb)
    ext[:, wide : wide + w, tile_part] = jnp.where(even_y, qa, qb)
    ext[:, wide + w :, tile_part] = jnp.where(even_y, qb, qa)


def fill_levels(ext, side_ref, tile, *strips):
    levels = tile.shape[2]
    last = up(levels, LANES) - LANES
    ext[:, :, last:] = jnp.zeros((ext.shape[0], ext.shape[1], ext.shape[2] - last), F32)
    part = (pl.ds(0, levels), lambda ref: ref[:, :, :levels])
    fill(ext, side_ref, tile, *strips, part)


def sweeps(load, cb_ref, work, emit, wide):
    tall, around = cb_ref.shape[1:3]

    def put(buffer, i, value):
        work[buffer, i, 8 : 8 + around] = value
        work[buffer, i, :8] = value[around - 8 :]
        work[buffer, i, 8 + around :] = value[:8]

    for i in range(tall):
        put(0, i, load(i))
    for sweep in range(SWEEPS):
        source = sweep % 2
        last = sweep == SWEEPS - 1
        size = wide if last else around
        for i in range(sweep + 1, tall - 1 - sweep):

            def near(row, by):
                return work[source, row, 8 + by : 8 + by + size]

            beside = (near(i - 1, 0) + near(i + 1, 0)) + (near(i, -1) + near(i, 1))
            new = cb_ref[1, i, :size] * near(i, 0) + cb_ref[0, i, :size] * beside
            if last:
                emit(i - SWEEPS, new)
            else:
                put(1 - source, i, new)


def diffuse_kernel(v, side_ref, tile_ref, coeff_ref, *refs):
    strips, stack_ref, refs = refs[:4], refs[4], refs[5:]
    ext, work, high_ref, low_ref, both, sem = refs[-6:]
    out_ref = refs[0]
    fetch = pltpu.make_async_copy(stack_ref.at[3], both, sem)
    fetch.start()
    rows, wide, levels = tile_ref.shape[1:]
    fill_levels(ext, side_ref, tile_ref[v], *strips)
    if v > 0:
        cb_ref = coeff_ref
    else:
        cb_ref = refs[1]

        def spread(ref):
            column = ref[:, :, levels : levels + 1]
            return jnp.broadcast_to(column, column.shape[:2] + (LANES,))

        own = jnp.stack(
            [jnp.broadcast_to(coeff_column(coeff_ref, k), (wide, LANES)) for k in range(rows)]
        )
        fill(cb_ref.at[0], side_ref, own, *strips, (pl.ds(0, LANES), spread))
        cb_ref[1] = 1.0 - 4.0 * cb_ref[0]
        cb_ref[2] = 1.0 / jnp.where(cb_ref[0] == 0.0, 1.0, cb_ref[0])

    def chunk(j, _):
        lanes = pl.ds(pl.multiple_of(j * LANES, LANES), LANES)

        def emit(row, value):
            here = pl.ds(row * wide, wide)
            high_ref[here, lanes], low_ref[here, lanes] = split(value)

        sweeps(lambda i: ext[i, :, lanes], cb_ref, work, emit, wide)
        return 0

    lax.fori_loop(0, ext.shape[2] // LANES, chunk, 0)
    deep = ext.shape[2]
    fetch.wait()
    for part in halves(out_ref.shape[0]):
        out_ref[part, :] = mm3(
            high_ref[part, :], low_ref[part, :], both[0, :deep], both[1, :deep]
        )


def hidden_kernel(
    mark, bucket, x_ref, first_ref, b1_ref, stack_ref, b2_ref, mask_ref,
    scale_ref, one_ref, one_t_ref, high_ref, low_ref, x_buf, first, second, sems,
):
    fetch_x = pltpu.make_async_copy(x_ref, x_buf, sems.at[2])
    fetch_x.start()
    fetch_first = pltpu.make_async_copy(first_ref, first, sems.at[0])
    fetch_second = pltpu.make_async_copy(stack_ref.at[0], second, sems.at[1])
    fetch_first.start()
    fetch_second.start()
    s1_ref, s2_ref, gate_ref = (scale_ref.at[k] for k in range(3))
    slots, cells = one_ref.shape
    devices, channels = mask_ref.shape
    fetch_x.wait()
    if len(x_buf.shape) == 2:
        deep = x_buf.shape[1]
        pieces = [x_buf[:, k : k + LANES] for k in range(0, deep, LANES)]
    else:
        whole = x_buf.shape[1] // bucket
        deep = (whole + 1) * LANES
        pieces = [
            x_buf[:, k * bucket : (k + 1) * bucket, :].reshape(slots, LANES)
            for k in range(whole)
        ]
        tail = x_buf[:, whole * bucket :, :]
        tail = jnp.concatenate([tail, pltpu.roll(tail, LANES // 2, 2)], axis=1)
        pieces.append(tail.reshape(slots, LANES))
    index = pieces[-1][:, mark % LANES : mark % LANES + 1]
    cell = index.astype(jnp.int32) - 1
    live = index > 0.5
    one_ref[...] = (iota((slots, cells), 1) == cell).astype(BF)
    flat = jnp.broadcast_to(index, (slots, LANES)).T[0:1, :].astype(jnp.int32) - 1
    one_t_ref[...] = (iota((cells, slots), 0) == flat).astype(BF)
    begin = iota((slots, devices), 1) * bucket
    at = iota((slots, devices), 0)
    from_owner = ((at >= begin) & (at < begin + bucket) & live).astype(BF)
    gate_ref[...] = jnp.zeros_like(gate_ref)
    gate_ref[:, :channels] = mm(from_owner, mask_ref[...].astype(F32).astype(BF))
    for k, piece in enumerate(pieces):
        here = pl.ds(k * LANES, LANES)
        high_ref[:, here], low_ref[:, here] = split(piece)
    parts = halves(slots)
    fetch_first.wait()
    for part in parts:
        got = mm3(high_ref[part, :deep], low_ref[part, :deep], first[0, :deep], first[1, :deep])
        hidden = jnp.tanh(got + b1_ref[...])
        s1_ref[part, :] = 1.0 - hidden * hidden
        high, low = split(hidden)
        high_ref[part, :] = high
        low_ref[part, :] = low
    fetch_second.wait()
    for part in parts:
        got = mm3(high_ref[part, :], low_ref[part, :], second[0], second[1])
        hidden = jnp.tanh(got + b2_ref[...])
        s2_ref[part, :] = 1.0 - hidden * hidden


LAYERS = ((0, 0, 1), (1, 1, 2), (2, 0, 2), (1, 0, 1), (0, 1, 0))


def table(values, layer):
    value = jnp.int32(values[0])
    for k in range(1, len(values)):
        value = jnp.where(layer == k, values[k], value)
    return value


def net_kernel(
    side_ref, q_ref, one_ref, one_t_ref, scale_ref, stack_ref,
    out_ref, xa, xb, yhead, ytail, x1, top, low, acc_top, acc_low, stack, sems,
):
    fetch = [
        pltpu.make_async_copy(stack_ref.at[k], stack.at[k], sems.at[k]) for k in range(4)
    ]
    for copy in fetch:
        copy.start()
    slots = q_ref.shape[0]
    half = slots // 2
    first, second = pl.ds(0, half), pl.ds(half, half)

    def pick(picker):
        return mm(picker, x1[0]) + mm(picker, x1[1])

    def close(acc, scale, part, target):
        target[0], target[1] = split(acc[...] * scale_ref[scale, part, :])

    x1[0], x1[1] = split(q_ref[...])
    acc_top[...] = pick(one_ref[first, :])
    acc_low[...] = pick(one_ref[second, :])
    close(acc_top, 0, first, top)
    fetch[0].wait()
    scales = [0] + [entry[2] for entry in LAYERS]

    def step(layer, _):
        for k in (1, 2):

            @pl.when(layer == k)
            def _():
                fetch[k].wait()

        weight = table([entry[0] for entry in LAYERS], layer)
        turned = table([entry[1] for entry in LAYERS], layer)
        before, after = table(scales[:-1], layer), table(scales[1:], layer)

        def run(dims):
            acc_top[...] = mm3(top[0], top[1], stack[weight, 0], stack[weight, 1], dims)
            close(acc_low, before, second, low)
            acc_low[...] = mm3(low[0], low[1], stack[weight, 0], stack[weight, 1], dims)
            close(acc_top, after, first, top)

        @pl.when(turned == 0)
        def _():
            run(NN)

        @pl.when(turned == 1)
        def _():
            run(NT)

        return 0

    lax.fori_loop(0, len(LAYERS), step, 0)
    close(acc_low, scales[-1], second, low)
    for part in halves(one_t_ref.shape[0]):
        got = mm(one_t_ref[part, :half], top[0]) + mm(one_t_ref[part, :half], top[1])
        got = got + mm(one_t_ref[part, half:], low[0]) + mm(one_t_ref[part, half:], low[1])
        x1[0, part, :], x1[1, part, :] = split(got)
    fetch[3].wait()
    rows, wide, levels = out_ref.shape
    for k, part in enumerate(halves(rows * wide)):
        got = mm3(x1[0, part, :], x1[1, part, :], stack[3, 0], stack[3, 1], NT)
        tall = got.shape[0] // wide
        got = got.reshape(tall, wide, got.shape[1])[:, :, :levels]
        here = pl.ds(k * tall, tall)
        out_ref[here] = got
        yhead[here] = got[:, :SWEEPS]
        ytail[here] = got[:, wide - SWEEPS :]
    even = side_ref[0] == 0
    head, tail = out_ref[:SWEEPS], out_ref[rows - SWEEPS :]
    xa[...] = jnp.where(even, tail, head)
    xb[...] = jnp.where(even, head, tail)


def finish_kernel(v, side_ref, field_ref, base_ref, cb_ref, *refs):
    out_ref, ext, work, total, result, sems = refs[-6:]
    w = SWEEPS
    rows, wide, levels = field_ref.shape
    fill_levels(ext, side_ref, field_ref[...], *refs[:4])

    def chunk(j, _):
        lanes = pl.ds(pl.multiple_of(j * LANES, LANES), LANES)

        def emit(row, value):
            total[row, :, lanes] = cb_ref[2, row + w, :wide] * value

        sweeps(lambda i: cb_ref[0, i] * ext[i, :, lanes], cb_ref, work, emit, wide)
        return 0

    lax.fori_loop(0, ext.shape[2] // LANES, chunk, 0)
    sends = []
    for k in range(2):
        part = pl.ds(k * (rows // 2), rows // 2)
        result[part] = base_ref[v, part] + total[part, :, :levels]
        sends.append(pltpu.make_async_copy(result.at[part], out_ref.at[v, part], sems.at[k]))
        sends[-1].start()
    for copy in sends:
        copy.wait()


def swap(value, axis, start):
    pairs = [(i, i + 1) for i in range(start, lax.axis_size(axis) - 1, 2)]
    return lax.ppermute(value, axis, pairs + [(j, i) for i, j in pairs])


def halo(sides, xa, xb, yhead, ytail):
    ra = swap(xa, "gx", 0)
    rb = swap(xb, "gx", 1)
    whole = pl.BlockSpec(memory_space=pltpu.VMEM)
    tall = yhead.shape[0] + 2 * SWEEPS
    ya, yb = call(
        join_kernel,
        [shaped((tall,) + yhead.shape[1:])] * 2,
        flops=0,
        moved=16 * yhead.size,
        vmem=8,
        in_specs=[pl.BlockSpec(memory_space=pltpu.SMEM)] + [whole] * 4,
    )(sides, ra, rb, yhead, ytail)
    qa = swap(ya, "gy", 0)
    qb = swap(yb, "gy", 1)
    return ra, rb, qa, qb


def body(
    vectors, diffusivity, vertical_factor, weight_first, bias_first, weight_second,
    bias_second, weight_out, error_inverse, observed_column, owner_count,
    observed_state, channel_mask,
):
    pairs, tile_x, tile_y, levels = vectors.shape
    count_y = lax.axis_size("gy")
    devices = lax.axis_size("gx") * count_y
    slots = observed_column.shape[0]
    bucket = slots // devices
    cells = tile_x * tile_y
    grid_wide = tile_y * count_y
    units = weight_second.shape[0]
    deep = up(levels, LANES)
    tall, around = tile_x + 2 * SWEEPS, tile_y + 2 * SWEEPS
    full_l, full_u = up(levels, WIDE), up(units, WIDE)
    full_c = up(error_inverse.shape[0], WIDE)
    mark = up(levels, 16)

    sides = jnp.stack([lax.axis_index("gx") % 2, lax.axis_index("gy") % 2]).astype(jnp.int32)
    whole = pl.BlockSpec(memory_space=pltpu.VMEM)
    far = pl.BlockSpec(memory_space=pltpu.HBM)
    scalars = pl.BlockSpec(memory_space=pltpu.SMEM)
    base = pltpu.with_memory_space_constraint(vectors, pltpu.HBM)
    strips = []
    for v in range(pairs):
        deep_v = levels + (v == 0)
        cuts = call(
            functools.partial(cut_kernel, v),
            [shaped((SWEEPS, tile_y, deep_v))] * 2 + [shaped((tile_x, SWEEPS, deep_v))] * 2,
            flops=0,
            moved=4 * vectors.size,
            vmem=12,
            scratch=[pltpu.VMEM((SWEEPS, tile_y, levels), F32)] * 2
            + [pltpu.VMEM((tile_x, 8, levels), F32)] * 2
            + [pltpu.SemaphoreType.DMA((4,))],
            in_specs=[scalars, far, whole],
        )(sides, base, diffusivity)
        strips.append(halo(sides, *cuts))

    position = jnp.arange(slots, dtype=jnp.int32)
    grid_row = observed_column // grid_wide
    grid_col = observed_column % grid_wide
    target = grid_row // tile_x * count_y + grid_col // tile_y
    dest = jnp.where(position < owner_count[0], target, -1)
    cell = (grid_row % tile_x * tile_y + grid_col % tile_y + 1).astype(F32)
    tight = bucket % 16 == 0 and mark // LANES == deep // LANES - 1 and mark % LANES < LANES // 2
    packed_shape = (slots, deep)
    if tight:
        packed_shape = (devices, bucket * (deep // LANES - 1) + bucket // 2, LANES)
    packed = call(
        functools.partial(pack_kernel, bucket),
        shaped(packed_shape),
        flops=6 * slots * slots * deep,
        moved=8 * slots * deep,
        scratch=[pltpu.VMEM((deep, slots), BF)] * 2,
        vmem=12,
    )(dest[None, :], cell[None, :], observed_state.T)
    carried = lax.all_to_all(
        packed if tight else packed.reshape(devices, bucket, deep), ("gx", "gy"),
        split_axis=0, concat_axis=0, tiled=True,
    ).reshape(packed_shape)

    side = max(full_l, full_u, full_c)
    weights = (vertical_factor, weight_first, weight_second, weight_out.T, error_inverse)
    first, stack = call(
        prep_kernel,
        [pltpu.HBM((2, full_l, side), BF), pltpu.HBM((4, 2, side, side), BF)],
        flops=6 * full_l * full_l * full_u,
        moved=8 * 5 * full_u * full_u,
        scratch=[pltpu.VMEM(weight.shape, F32) for weight in weights]
        + [
            pltpu.VMEM((2, full_l, side), BF), pltpu.VMEM((4, 2, side, side), BF),
            pltpu.VMEM((2, side, full_l), BF),
            pltpu.SemaphoreType.DMA((5,)), pltpu.SemaphoreType.DMA((5,)),
        ],
        vmem=27,
        in_specs=[far] * 5,
        out_specs=[far] * 2,
    )(*[pltpu.with_memory_space_constraint(weight, pltpu.HBM) for weight in weights])
    first, stack = (pltpu.with_memory_space_constraint(x, pltpu.HBM) for x in (first, stack))

    def wide_bias(bias):
        return jnp.pad(bias, (0, side - bias.shape[0]))[None, :]

    queries = []
    for v in range(pairs):
        got = call(
            functools.partial(diffuse_kernel, v),
            [shaped((cells, side))] + [shaped((3, tall, around, LANES))] * (v == 0),
            flops=6 * cells * deep * full_u,
            moved=8 * tall * around * deep,
            scratch=[
                pltpu.VMEM((tall, around, deep), F32),
                pltpu.VMEM((2, tall, around + 16, LANES), F32),
                pltpu.VMEM((cells, deep), BF),
                pltpu.VMEM((cells, deep), BF),
                pltpu.VMEM((2, side, side), BF),
                pltpu.SemaphoreType.DMA,
            ],
            vmem=16,
            in_specs=[scalars, whole] + [whole] * 5 + [far],
            out_specs=[whole] * (2 - (v > 0)),
        )(sides, vectors, spread if v else diffusivity, *strips[v], stack)
        queries.append(got[0])
        if v == 0:
            spread = got[1]

    scale, one, one_t = call(
        functools.partial(hidden_kernel, mark, bucket),
        [shaped((3, slots, side)), shaped((slots, cells), BF), shaped((cells, slots), BF)],
        flops=12 * slots * full_u * full_u,
        moved=8 * slots * full_u,
        scratch=[pltpu.VMEM((slots, side), BF)] * 2
        + [
            pltpu.VMEM(packed_shape, F32),
            pltpu.VMEM((2, full_l, side), BF), pltpu.VMEM((2, side, side), BF),
            pltpu.SemaphoreType.DMA((3,)),
        ],
        vmem=18,
        in_specs=[far, far, whole, far, whole, whole],
    )(pltpu.with_memory_space_constraint(carried, pltpu.HBM), first, wide_bias(bias_first), stack, wide_bias(bias_second), channel_mask)

    fields = []
    for v in range(pairs):
        fields.append(
            call(
                net_kernel,
                [shaped((tile_x, tile_y, levels))]
                + [shaped((SWEEPS, tile_y, levels))] * 2
                + [shaped((tile_x, SWEEPS, levels))] * 2,
                flops=36 * slots * full_u * full_u,
                moved=4 * 5 * full_u * full_u,
                scratch=[pltpu.VMEM((2, slots, side), BF)]
                + [pltpu.VMEM((2, slots // 2, side), BF)] * 2
                + [pltpu.VMEM((slots // 2, side), F32)] * 2
                + [
                    pltpu.VMEM((4, 2, side, side), BF),
                    pltpu.SemaphoreType.DMA((4,)),
                ],
                vmem=22,
                in_specs=[scalars] + [whole] * 4 + [far],
            )(sides, queries[v], one, one_t, scale, stack)
        )

    out = None
    for v in range(pairs):
        around_field = halo(sides, *fields[v][1:])
        carry = [] if out is None else [out]
        out = call(
            functools.partial(finish_kernel, v),
            pltpu.HBM(vectors.shape, F32),
            flops=40 * tall * around * deep,
            moved=12 * cells * deep,
            scratch=[
                pltpu.VMEM((tall, around, deep), F32),
                pltpu.VMEM((2, tall, around + 16, LANES), F32),
                pltpu.VMEM((tile_x, tile_y, deep), F32),
                pltpu.VMEM((tile_x, tile_y, levels), F32),
                pltpu.SemaphoreType.DMA((2,)),
            ],
            vmem=16,
            in_specs=[scalars] + [whole] * 7 + [far] * len(carry),
            out_specs=far,
            input_output_aliases={8: 0} if carry else {},
        )(sides, fields[v][0], vectors, spread, *around_field, *carry)
    return out


def solution(mesh):
    in_specs = (
        P(None, "gx", "gy", None),
        P("gx", "gy"),
        P(),
        P(),
        P(),
        P(),
        P(),
        P(),
        P(),
        P(("gx", "gy")),
        P(("gx", "gy")),
        P(("gx", "gy"), None),
        P(),
    )
    out_specs = P(None, "gx", "gy", None)
    return jax.shard_map(body, mesh=mesh, in_specs=in_specs, out_specs=out_specs, check_vma=False)
```

```python
import functools

import jax
import jax.numpy as jnp
from jax import lax
from jax.experimental import pallas as pl
from jax.experimental.pallas import tpu as pltpu
from jax.sharding import PartitionSpec as P

SWEEPS = 4
WIDE = 256
LANES = 128
BF = jnp.bfloat16
F32 = jnp.float32
NN = ((1,), (0,))
NT = ((1,), (1,))


def up(size, unit):
    return -(-size // unit) * unit


def split(value):
    high = value.astype(BF)
    return high, (value - high.astype(F32)).astype(BF)


def mm(left, right, dims=NN):
    return lax.dot_general(left, right, (dims, ((), ())), preferred_element_type=F32)


def mm3(left_high, left_low, right_high, right_low, dims=NN):
    left = jnp.concatenate([left_high, left_low, left_high], axis=dims[0][0])
    right = jnp.concatenate([right_high, right_high, right_low], axis=dims[1][0])
    return mm(left, right, dims)


def halves(size):
    half = size // 2
    return [pl.ds(0, half), pl.ds(half, half)] if half % 16 == 0 else [pl.ds(0, size)]


def each_half(size, work):
    parts = halves(size)
    step = parts[0].size

    def run(k, _):
        work(pl.ds(pl.multiple_of(k * step, step), step))
        return 0

    lax.fori_loop(0, len(parts), run, 0)


def iota(shape, axis):
    return lax.broadcasted_iota(jnp.int32, shape, axis)


def call(kernel, out_shape, flops, moved, scratch=(), vmem=48, **more):
    return pl.pallas_call(
        kernel,
        out_shape=out_shape,
        scratch_shapes=list(scratch),
        compiler_params=pltpu.CompilerParams(vmem_limit_bytes=vmem * 1024 * 1024),
        cost_estimate=pl.CostEstimate(flops=flops, bytes_accessed=moved, transcendentals=0),
        **more,
    )


def shaped(shape, dtype=F32):
    return jax.ShapeDtypeStruct(shape, dtype)


def pack_kernel(bucket, dest_ref, cell_ref, state_ref, out_ref, high_ref, low_ref):
    levels, slots = state_ref.shape
    devices = slots // bucket
    dest = dest_ref[...]
    same = (iota((devices, slots), 0) == dest).astype(F32)
    before = (iota((slots, slots), 0) < iota((slots, slots), 1)).astype(BF)
    rank = jnp.sum(same * mm(same.astype(BF), before), axis=0, keepdims=True)
    place = dest * bucket + rank.astype(jnp.int32)
    pick = (iota((slots, slots), 0) == place).astype(BF)
    high_ref[...] = jnp.zeros_like(high_ref)
    low_ref[...] = jnp.zeros_like(low_ref)
    high, low = split(state_ref[...])
    high_ref[:levels, :] = high
    low_ref[:levels, :] = low
    mark = up(levels, 16)
    tall = jnp.where(iota((16, slots), 0) == 0, cell_ref[...], 0.0)
    high, low = split(tall)
    high_ref[mark : mark + 16, :] = high
    low_ref[mark : mark + 16, :] = low
    rows = mm(pick, high_ref[...], NT) + mm(pick, low_ref[...], NT)
    if out_ref.shape == rows.shape:
        out_ref[...] = rows
        return
    whole = rows.shape[1] // LANES - 1
    for k in range(whole):
        piece = rows[:, k * LANES : (k + 1) * LANES].reshape(devices, bucket, LANES)
        out_ref[:, k * bucket : (k + 1) * bucket, :] = piece
    tail = rows[:, whole * LANES :].reshape(devices, bucket, LANES)
    half = bucket // 2
    left = iota((devices, half, LANES), 2) < LANES // 2
    turned = pltpu.roll(tail[:, half:], LANES // 2, 2)
    out_ref[:, whole * bucket :, :] = jnp.where(left, tail[:, :half], turned)


def prep_kernel(*refs):
    ins, (first_out, stack_out), refs = refs[:5], refs[5:7], refs[7:]
    raw, (first, stack, turned, in_sem, out_sem) = refs[:5], refs[5:]
    fetch = [
        pltpu.make_async_copy(ins[k], raw[k], in_sem.at[k]) for k in range(5)
    ]
    for copy in fetch:
        copy.start()
    sends = []

    def send(source, target):
        copy = pltpu.make_async_copy(source, target, out_sem.at[len(sends)])
        copy.start()
        sends.append(copy)

    def put(values, ref):
        rows, cols = values.shape
        if (rows, cols) != ref.shape[1:]:
            ref[...] = jnp.zeros_like(ref)
        ref[0, :rows, :cols], ref[1, :rows, :cols] = split(values)

    fetch[0].wait()
    put(raw[0][...].T, turned)
    fetch[1].wait()
    put(raw[1][...], first)
    send(first, first_out)
    rows = up(raw[0].shape[1], LANES)
    stack[3, :, rows:, :] = jnp.zeros((2,) + (stack.shape[2] - rows, stack.shape[3]), BF)

    def half(part):
        got = mm3(turned[0, part, :], turned[1, part, :], first[0], first[1])
        stack[3, 0, part, :], stack[3, 1, part, :] = split(got)

    each_half(rows, half)
    send(stack.at[3], stack_out.at[3])
    for k in range(3):
        fetch[k + 2].wait()
        put(raw[k + 2][...], stack.at[k])
        send(stack.at[k], stack_out.at[k])
    for copy in sends:
        copy.wait()


def coeff_column(coeff_ref, row):
    wide = coeff_ref.shape[1]
    spread = jnp.broadcast_to(coeff_ref[row : row + 1, :], (wide, wide))
    diagonal = iota((wide, wide), 0) == iota((wide, wide), 1)
    return jnp.sum(jnp.where(diagonal, spread, 0.0), axis=1, keepdims=True)


def cut_kernel(v, side_ref, vectors_ref, coeff_ref, xa, xb, yhead, ytail, *refs):
    bufs, sems = refs[:4], refs[4]
    rows, wide, levels = vectors_ref.shape[1:]
    w = SWEEPS
    parts = (
        vectors_ref.at[v, pl.ds(0, w)],
        vectors_ref.at[v, pl.ds(rows - w, w)],
        vectors_ref.at[v, :, pl.ds(0, 8)],
        vectors_ref.at[v, :, pl.ds(wide - 8, 8)],
    )
    copies = [pltpu.make_async_copy(parts[k], bufs[k], sems.at[k]) for k in range(4)]
    for copy in copies:
        copy.start()
    even = side_ref[0] == 0
    if v == 0:
        columns = [coeff_column(coeff_ref, row) for row in range(rows)]
        for row in range(w):
            head, tail = columns[row], columns[rows - w + row]
            xa[row, :, levels:] = jnp.where(even, tail, head)
            xb[row, :, levels:] = jnp.where(even, head, tail)
        for row in range(rows):
            yhead[row, :, levels:] = columns[row][:w]
            ytail[row, :, levels:] = columns[row][wide - w :]
    for copy in copies:
        copy.wait()
    head, tail = bufs[0][...], bufs[1][...]
    xa[:, :, :levels] = jnp.where(even, tail, head)
    xb[:, :, :levels] = jnp.where(even, head, tail)
    yhead[:, :, :levels] = bufs[2][:, :w]
    ytail[:, :, :levels] = bufs[3][:, 8 - w :]


def join_kernel(side_ref, ra, rb, yhead, ytail, ya, yb):
    w = SWEEPS
    rows = yhead.shape[0]
    wide = ra.shape[1]
    even_x, even_y = side_ref[0] == 0, side_ref[1] == 0

    for here, first, second in (
        (pl.ds(0, w), rb, ra),
        (pl.ds(w + rows, w), ra, rb),
    ):
        head = jnp.where(even_x, first[:, :w], second[:, :w])
        tail = jnp.where(even_x, first[:, wide - w :], second[:, wide - w :])
        ya[here] = jnp.where(even_y, tail, head)
        yb[here] = jnp.where(even_y, head, tail)
    here = pl.ds(w, rows)
    ya[here] = jnp.where(even_y, ytail[...], yhead[...])
    yb[here] = jnp.where(even_y, yhead[...], ytail[...])


def fill(ext, side_ref, tile, ra, rb, qa, qb, part):
    rows, wide = tile.shape[:2]
    w = SWEEPS
    even_y = side_ref[1] == 0
    upper = jnp.where(side_ref[0] == 0, w + rows, 0)
    tile_part, strip_part = part
    ext[w : w + rows, :wide, tile_part] = tile
    ext[pl.ds(upper, w), :wide, tile_part] = strip_part(ra)
    ext[pl.ds(w + rows - upper, w), :wide, tile_part] = strip_part(rb)
    qa, qb = strip_part(qa), strip_part(qb)
    ext[:, wide : wide + w, tile_part] = jnp.where(even_y, qa, qb)
    ext[:, wide + w :, tile_part] = jnp.where(even_y, qb, qa)


def fill_levels(ext, side_ref, tile, *strips):
    levels = tile.shape[2]
    last = up(levels, LANES) - LANES
    ext[:, :, last:] = jnp.zeros((ext.shape[0], ext.shape[1], ext.shape[2] - last), F32)
    part = (pl.ds(0, levels), lambda ref: ref[:, :, :levels])
    fill(ext, side_ref, tile, *strips, part)


def sweeps(load, cb_ref, work, emit, wide):
    tall, around = cb_ref.shape[1:3]

    def put(buffer, i, value):
        work[buffer, i, 8 : 8 + around] = value
        work[buffer, i, :8] = value[around - 8 :]
        work[buffer, i, 8 + around :] = value[:8]

    for i in range(tall):
        put(0, i, load(i))
    for sweep in range(SWEEPS):
        source = sweep % 2
        last = sweep == SWEEPS - 1
        size = wide if last else around
        for i in range(sweep + 1, tall - 1 - sweep):

            def near(row, by):
                return work[source, row, 8 + by : 8 + by + size]

            beside = (near(i - 1, 0) + near(i + 1, 0)) + (near(i, -1) + near(i, 1))
            new = cb_ref[1, i, :size] * near(i, 0) + cb_ref[0, i, :size] * beside
            if last:
                emit(i - SWEEPS, new)
            else:
                put(1 - source, i, new)


def diffuse_kernel(v, side_ref, tile_ref, coeff_ref, *refs):
    strips, stack_ref, refs = refs[:4], refs[4], refs[5:]
    ext, work, high_ref, low_ref, both, sem = refs[-6:]
    out_ref = refs[0]
    fetch = pltpu.make_async_copy(stack_ref.at[3], both, sem)
    fetch.start()
    rows, wide, levels = tile_ref.shape[1:]
    fill_levels(ext, side_ref, tile_ref[v], *strips)
    if v > 0:
        cb_ref = coeff_ref
    else:
        cb_ref = refs[1]

        def spread(ref):
            column = ref[:, :, levels : levels + 1]
            return jnp.broadcast_to(column, column.shape[:2] + (LANES,))

        own = jnp.stack(
            [jnp.broadcast_to(coeff_column(coeff_ref, k), (wide, LANES)) for k in range(rows)]
        )
        fill(cb_ref.at[0], side_ref, own, *strips, (pl.ds(0, LANES), spread))
        cb_ref[1] = 1.0 - 4.0 * cb_ref[0]
        cb_ref[2] = 1.0 / jnp.where(cb_ref[0] == 0.0, 1.0, cb_ref[0])

    def chunk(j, _):
        lanes = pl.ds(pl.multiple_of(j * LANES, LANES), LANES)

        def emit(row, value):
            here = pl.ds(row * wide, wide)
            high_ref[here, lanes], low_ref[here, lanes] = split(value)

        sweeps(lambda i: ext[i, :, lanes], cb_ref, work, emit, wide)
        return 0

    lax.fori_loop(0, ext.shape[2] // LANES, chunk, 0)
    deep = ext.shape[2]
    fetch.wait()

    def half(part):
        out_ref[part, :] = mm3(
            high_ref[part, :], low_ref[part, :], both[0, :deep], both[1, :deep]
        )

    each_half(out_ref.shape[0], half)


def hidden_kernel(
    mark, bucket, x_ref, first_ref, b1_ref, stack_ref, b2_ref, mask_ref,
    scale_ref, one_ref, one_t_ref, high_ref, low_ref, x_buf, first, second, sems,
):
    fetch_x = pltpu.make_async_copy(x_ref, x_buf, sems.at[2])
    fetch_x.start()
    fetch_first = pltpu.make_async_copy(first_ref, first, sems.at[0])
    fetch_second = pltpu.make_async_copy(stack_ref.at[0], second, sems.at[1])
    fetch_first.start()
    fetch_second.start()
    s1_ref, s2_ref, gate_ref = (scale_ref.at[k] for k in range(3))
    slots, cells = one_ref.shape
    devices, channels = mask_ref.shape
    fetch_x.wait()
    if len(x_buf.shape) == 2:
        deep = x_buf.shape[1]
        pieces = [x_buf[:, k : k + LANES] for k in range(0, deep, LANES)]
    else:
        whole = x_buf.shape[1] // bucket
        deep = (whole + 1) * LANES
        pieces = [
            x_buf[:, k * bucket : (k + 1) * bucket, :].reshape(slots, LANES)
            for k in range(whole)
        ]
        tail = x_buf[:, whole * bucket :, :]
        tail = jnp.concatenate([tail, pltpu.roll(tail, LANES // 2, 2)], axis=1)
        pieces.append(tail.reshape(slots, LANES))
    index = pieces[-1][:, mark % LANES : mark % LANES + 1]
    cell = index.astype(jnp.int32) - 1
    live = index > 0.5
    one_ref[...] = (iota((slots, cells), 1) == cell).astype(BF)
    flat = jnp.broadcast_to(index, (slots, LANES)).T[0:1, :].astype(jnp.int32) - 1
    one_t_ref[...] = (iota((cells, slots), 0) == flat).astype(BF)
    begin = iota((slots, devices), 1) * bucket
    at = iota((slots, devices), 0)
    from_owner = ((at >= begin) & (at < begin + bucket) & live).astype(BF)
    gate_ref[...] = jnp.zeros_like(gate_ref)
    gate_ref[:, :channels] = mm(from_owner, mask_ref[...].astype(F32).astype(BF))
    for k, piece in enumerate(pieces):
        here = pl.ds(k * LANES, LANES)
        high_ref[:, here], low_ref[:, here] = split(piece)
    fetch_first.wait()
    fetch_second.wait()

    def both_layers(part):
        got = mm3(high_ref[part, :deep], low_ref[part, :deep], first[0, :deep], first[1, :deep])
        hidden = jnp.tanh(got + b1_ref[...])
        s1_ref[part, :] = 1.0 - hidden * hidden
        high, low = split(hidden)
        got = mm3(high, low, second[0], second[1])
        hidden = jnp.tanh(got + b2_ref[...])
        s2_ref[part, :] = 1.0 - hidden * hidden

    each_half(slots, both_layers)


LAYERS = ((0, NN, 1), (1, NT, 2), (2, NN, 2), (1, NN, 1), (0, NT, 0))


def net_kernel(
    side_ref, q_ref, one_ref, one_t_ref, scale_ref, stack_ref,
    out_ref, xa, xb, yhead, ytail, x1, top, low, acc_top, acc_low, stack, sems,
):
    fetch = [
        pltpu.make_async_copy(stack_ref.at[k], stack.at[k], sems.at[k]) for k in range(4)
    ]
    for copy in fetch:
        copy.start()
    slots = q_ref.shape[0]
    half = slots // 2
    first, second = pl.ds(0, half), pl.ds(half, half)

    def pick(picker):
        return mm(picker, x1[0]) + mm(picker, x1[1])

    def close(acc, scale, part, target):
        target[0], target[1] = split(acc[...] * scale_ref[scale, part, :])

    x1[0], x1[1] = split(q_ref[...])
    acc_top[...] = pick(one_ref[first, :])
    acc_low[...] = pick(one_ref[second, :])
    close(acc_top, 0, first, top)
    fetch[0].wait()
    before = 0
    for layer, (weight, dims, scale) in enumerate(LAYERS):
        if layer in (1, 2):
            fetch[layer].wait()
        acc_top[...] = mm3(top[0], top[1], stack[weight, 0], stack[weight, 1], dims)
        close(acc_low, before, second, low)
        acc_low[...] = mm3(low[0], low[1], stack[weight, 0], stack[weight, 1], dims)
        close(acc_top, scale, first, top)
        before = scale
    close(acc_low, before, second, low)

    def scatter(part):
        got = mm(one_t_ref[part, :half], top[0]) + mm(one_t_ref[part, :half], top[1])
        got = got + mm(one_t_ref[part, half:], low[0]) + mm(one_t_ref[part, half:], low[1])
        x1[0, part, :], x1[1, part, :] = split(got)

    each_half(one_t_ref.shape[0], scatter)
    fetch[3].wait()
    rows, wide, levels = out_ref.shape
    parts = halves(rows * wide)
    size = parts[0].size
    tall = size // wide

    def place(k, _):
        part = pl.ds(pl.multiple_of(k * size, size), size)
        got = mm3(x1[0, part, :], x1[1, part, :], stack[3, 0], stack[3, 1], NT)
        got = got.reshape(tall, wide, got.shape[1])[:, :, :levels]
        here = pl.ds(k * tall, tall)
        out_ref[here] = got
        yhead[here] = got[:, :SWEEPS]
        ytail[here] = got[:, wide - SWEEPS :]
        return 0

    lax.fori_loop(0, len(parts), place, 0)
    even = side_ref[0] == 0
    head, tail = out_ref[:SWEEPS], out_ref[rows - SWEEPS :]
    xa[...] = jnp.where(even, tail, head)
    xb[...] = jnp.where(even, head, tail)


def finish_kernel(v, side_ref, field_ref, base_ref, cb_ref, *refs):
    out_ref, ext, work, total, result, sems = refs[-6:]
    w = SWEEPS
    rows, wide, levels = field_ref.shape
    fill_levels(ext, side_ref, field_ref[...], *refs[:4])

    def chunk(j, _):
        lanes = pl.ds(pl.multiple_of(j * LANES, LANES), LANES)

        def emit(row, value):
            total[row, :, lanes] = cb_ref[2, row + w, :wide] * value

        sweeps(lambda i: cb_ref[0, i] * ext[i, :, lanes], cb_ref, work, emit, wide)
        return 0

    lax.fori_loop(0, ext.shape[2] // LANES, chunk, 0)
    sends = []
    for k in range(2):
        part = pl.ds(k * (rows // 2), rows // 2)
        result[part] = base_ref[v, part] + total[part, :, :levels]
        sends.append(pltpu.make_async_copy(result.at[part], out_ref.at[v, part], sems.at[k]))
        sends[-1].start()
    for copy in sends:
        copy.wait()


def swap(value, axis, start):
    pairs = [(i, i + 1) for i in range(start, lax.axis_size(axis) - 1, 2)]
    return lax.ppermute(value, axis, pairs + [(j, i) for i, j in pairs])


def halo(sides, xa, xb, yhead, ytail):
    ra = swap(xa, "gx", 0)
    rb = swap(xb, "gx", 1)
    whole = pl.BlockSpec(memory_space=pltpu.VMEM)
    tall = yhead.shape[0] + 2 * SWEEPS
    ya, yb = call(
        join_kernel,
        [shaped((tall,) + yhead.shape[1:])] * 2,
        flops=0,
        moved=16 * yhead.size,
        vmem=8,
        in_specs=[pl.BlockSpec(memory_space=pltpu.SMEM)] + [whole] * 4,
    )(sides, ra, rb, yhead, ytail)
    qa = swap(ya, "gy", 0)
    qb = swap(yb, "gy", 1)
    return ra, rb, qa, qb


def body(
    vectors, diffusivity, vertical_factor, weight_first, bias_first, weight_second,
    bias_second, weight_out, error_inverse, observed_column, owner_count,
    observed_state, channel_mask,
):
    pairs, tile_x, tile_y, levels = vectors.shape
    count_y = lax.axis_size("gy")
    devices = lax.axis_size("gx") * count_y
    slots = observed_column.shape[0]
    bucket = slots // devices
    cells = tile_x * tile_y
    grid_wide = tile_y * count_y
    units = weight_second.shape[0]
    deep = up(levels, LANES)
    tall, around = tile_x + 2 * SWEEPS, tile_y + 2 * SWEEPS
    full_l, full_u = up(levels, WIDE), up(units, WIDE)
    full_c = up(error_inverse.shape[0], WIDE)
    mark = up(levels, 16)

    sides = jnp.stack([lax.axis_index("gx") % 2, lax.axis_index("gy") % 2]).astype(jnp.int32)
    whole = pl.BlockSpec(memory_space=pltpu.VMEM)
    far = pl.BlockSpec(memory_space=pltpu.HBM)
    scalars = pl.BlockSpec(memory_space=pltpu.SMEM)
    base = pltpu.with_memory_space_constraint(vectors, pltpu.HBM)
    strips = []
    for v in range(pairs):
        deep_v = levels + (v == 0)
        cuts = call(
            functools.partial(cut_kernel, v),
            [shaped((SWEEPS, tile_y, deep_v))] * 2 + [shaped((tile_x, SWEEPS, deep_v))] * 2,
            flops=0,
            moved=4 * vectors.size,
            vmem=12,
            scratch=[pltpu.VMEM((SWEEPS, tile_y, levels), F32)] * 2
            + [pltpu.VMEM((tile_x, 8, levels), F32)] * 2
            + [pltpu.SemaphoreType.DMA((4,))],
            in_specs=[scalars, far, whole],
        )(sides, base, diffusivity)
        strips.append(halo(sides, *cuts))

    position = jnp.arange(slots, dtype=jnp.int32)
    grid_row = observed_column // grid_wide
    grid_col = observed_column % grid_wide
    target = grid_row // tile_x * count_y + grid_col // tile_y
    dest = jnp.where(position < owner_count[0], target, -1)
    cell = (grid_row % tile_x * tile_y + grid_col % tile_y + 1).astype(F32)
    tight = bucket % 16 == 0 and mark // LANES == deep // LANES - 1 and mark % LANES < LANES // 2
    packed_shape = (slots, deep)
    if tight:
        packed_shape = (devices, bucket * (deep // LANES - 1) + bucket // 2, LANES)
    packed = call(
        functools.partial(pack_kernel, bucket),
        shaped(packed_shape),
        flops=6 * slots * slots * deep,
        moved=8 * slots * deep,
        scratch=[pltpu.VMEM((deep, slots), BF)] * 2,
        vmem=12,
    )(dest[None, :], cell[None, :], observed_state.T)
    carried = lax.all_to_all(
        packed if tight else packed.reshape(devices, bucket, deep), ("gx", "gy"),
        split_axis=0, concat_axis=0, tiled=True,
    ).reshape(packed_shape)

    side = max(full_l, full_u, full_c)
    weights = (vertical_factor, weight_first, weight_second, weight_out.T, error_inverse)
    first, stack = call(
        prep_kernel,
        [pltpu.HBM((2, full_l, side), BF), pltpu.HBM((4, 2, side, side), BF)],
        flops=6 * full_l * full_l * full_u,
        moved=8 * 5 * full_u * full_u,
        scratch=[pltpu.VMEM(weight.shape, F32) for weight in weights]
        + [
            pltpu.VMEM((2, full_l, side), BF), pltpu.VMEM((4, 2, side, side), BF),
            pltpu.VMEM((2, side, full_l), BF),
            pltpu.SemaphoreType.DMA((5,)), pltpu.SemaphoreType.DMA((5,)),
        ],
        vmem=27,
        in_specs=[far] * 5,
        out_specs=[far] * 2,
    )(*[pltpu.with_memory_space_constraint(weight, pltpu.HBM) for weight in weights])
    first, stack = (pltpu.with_memory_space_constraint(x, pltpu.HBM) for x in (first, stack))

    def wide_bias(bias):
        return jnp.pad(bias, (0, side - bias.shape[0]))[None, :]

    queries = []
    for v in range(pairs):
        got = call(
            functools.partial(diffuse_kernel, v),
            [shaped((cells, side))] + [shaped((3, tall, around, LANES))] * (v == 0),
            flops=6 * cells * deep * full_u,
            moved=8 * tall * around * deep,
            scratch=[
                pltpu.VMEM((tall, around, deep), F32),
                pltpu.VMEM((2, tall, around + 16, LANES), F32),
                pltpu.VMEM((cells, deep), BF),
                pltpu.VMEM((cells, deep), BF),
                pltpu.VMEM((2, side, side), BF),
                pltpu.SemaphoreType.DMA,
            ],
            vmem=16,
            in_specs=[scalars, whole] + [whole] * 5 + [far],
            out_specs=[whole] * (2 - (v > 0)),
        )(sides, vectors, spread if v else diffusivity, *strips[v], stack)
        queries.append(got[0])
        if v == 0:
            spread = got[1]

    scale, one, one_t = call(
        functools.partial(hidden_kernel, mark, bucket),
        [shaped((3, slots, side)), shaped((slots, cells), BF), shaped((cells, slots), BF)],
        flops=12 * slots * full_u * full_u,
        moved=8 * slots * full_u,
        scratch=[pltpu.VMEM((slots, side), BF)] * 2
        + [
            pltpu.VMEM(packed_shape, F32),
            pltpu.VMEM((2, full_l, side), BF), pltpu.VMEM((2, side, side), BF),
            pltpu.SemaphoreType.DMA((3,)),
        ],
        vmem=18,
        in_specs=[far, far, whole, far, whole, whole],
    )(pltpu.with_memory_space_constraint(carried, pltpu.HBM), first, wide_bias(bias_first), stack, wide_bias(bias_second), channel_mask)

    fields = []
    for v in range(pairs):
        fields.append(
            call(
                net_kernel,
                [shaped((tile_x, tile_y, levels))]
                + [shaped((SWEEPS, tile_y, levels))] * 2
                + [shaped((tile_x, SWEEPS, levels))] * 2,
                flops=36 * slots * full_u * full_u,
                moved=4 * 5 * full_u * full_u,
                scratch=[pltpu.VMEM((2, slots, side), BF)]
                + [pltpu.VMEM((2, slots // 2, side), BF)] * 2
                + [pltpu.VMEM((slots // 2, side), F32)] * 2
                + [
                    pltpu.VMEM((4, 2, side, side), BF),
                    pltpu.SemaphoreType.DMA((4,)),
                ],
                vmem=22,
                in_specs=[scalars] + [whole] * 4 + [far],
            )(sides, queries[v], one, one_t, scale, stack)
        )

    out = None
    for v in range(pairs):
        around_field = halo(sides, *fields[v][1:])
        carry = [] if out is None else [out]
        out = call(
            functools.partial(finish_kernel, v),
            pltpu.HBM(vectors.shape, F32),
            flops=40 * tall * around * deep,
            moved=12 * cells * deep,
            scratch=[
                pltpu.VMEM((tall, around, deep), F32),
                pltpu.VMEM((2, tall, around + 16, LANES), F32),
                pltpu.VMEM((tile_x, tile_y, deep), F32),
                pltpu.VMEM((tile_x, tile_y, levels), F32),
                pltpu.SemaphoreType.DMA((2,)),
            ],
            vmem=16,
            in_specs=[scalars] + [whole] * 7 + [far] * len(carry),
            out_specs=far,
            input_output_aliases={8: 0} if carry else {},
        )(sides, fields[v][0], vectors, spread, *around_field, *carry)
    return out


def solution(mesh):
    in_specs = (
        P(None, "gx", "gy", None),
        P("gx", "gy"),
        P(),
        P(),
        P(),
        P(),
        P(),
        P(),
        P(),
        P(("gx", "gy")),
        P(("gx", "gy")),
        P(("gx", "gy"), None),
        P(),
    )
    out_specs = P(None, "gx", "gy", None)
    return jax.shard_map(body, mesh=mesh, in_specs=in_specs, out_specs=out_specs, check_vma=False)
```

```python
import functools

import jax
import jax.numpy as jnp
from jax import lax
from jax.experimental import pallas as pl
from jax.experimental.pallas import tpu as pltpu
from jax.sharding import PartitionSpec as P

SWEEPS = 4
WIDE = 256
LANES = 128
BF = jnp.bfloat16
F32 = jnp.float32
NN = ((1,), (0,))
NT = ((1,), (1,))


def up(size, unit):
    return -(-size // unit) * unit


def split(value):
    high = value.astype(BF)
    return high, (value - high.astype(F32)).astype(BF)


def mm(left, right, dims=NN):
    return lax.dot_general(left, right, (dims, ((), ())), preferred_element_type=F32)


def mm3(left_high, left_low, right_high, right_low, dims=NN):
    left = jnp.concatenate([left_high, left_low, left_high], axis=dims[0][0])
    right = jnp.concatenate([right_high, right_high, right_low], axis=dims[1][0])
    return mm(left, right, dims)


def halves(size):
    half = size // 2
    return [pl.ds(0, half), pl.ds(half, half)] if half % 16 == 0 else [pl.ds(0, size)]


class Fetch:
    def __init__(self, source, target, sems):
        half = target.shape[1] // 2
        self.copies = [
            pltpu.make_async_copy(
                source.at[term, pl.ds(k * half, half)],
                target.at[term, pl.ds(k * half, half)],
                sems.at[2 * term + k],
            )
            for term in range(2)
            for k in range(2)
        ]

    def start(self):
        for copy in self.copies:
            copy.start()

    def wait(self):
        for copy in self.copies:
            copy.wait()


def iota(shape, axis):
    return lax.broadcasted_iota(jnp.int32, shape, axis)


def call(kernel, out_shape, flops, moved, scratch=(), vmem=48, **more):
    return pl.pallas_call(
        kernel,
        out_shape=out_shape,
        scratch_shapes=list(scratch),
        compiler_params=pltpu.CompilerParams(vmem_limit_bytes=vmem * 1024 * 1024),
        cost_estimate=pl.CostEstimate(flops=flops, bytes_accessed=moved, transcendentals=0),
        **more,
    )


def shaped(shape, dtype=F32):
    return jax.ShapeDtypeStruct(shape, dtype)


def pack_kernel(bucket, dest_ref, cell_ref, state_ref, out_ref, high_ref, low_ref):
    levels, slots = state_ref.shape
    devices = slots // bucket
    dest = dest_ref[...]
    same = (iota((devices, slots), 0) == dest).astype(F32)
    before = (iota((slots, slots), 0) < iota((slots, slots), 1)).astype(BF)
    rank = jnp.sum(same * mm(same.astype(BF), before), axis=0, keepdims=True)
    place = dest * bucket + rank.astype(jnp.int32)
    pick = (iota((slots, slots), 0) == place).astype(BF)
    high_ref[...] = jnp.zeros_like(high_ref)
    low_ref[...] = jnp.zeros_like(low_ref)
    high, low = split(state_ref[...])
    high_ref[:levels, :] = high
    low_ref[:levels, :] = low
    mark = up(levels, 16)
    tall = jnp.where(iota((16, slots), 0) == 0, cell_ref[...], 0.0)
    high, low = split(tall)
    high_ref[mark : mark + 16, :] = high
    low_ref[mark : mark + 16, :] = low
    rows = mm(pick, high_ref[...], NT) + mm(pick, low_ref[...], NT)
    if out_ref.shape == rows.shape:
        out_ref[...] = rows
        return
    whole = rows.shape[1] // LANES - 1
    for k in range(whole):
        piece = rows[:, k * LANES : (k + 1) * LANES].reshape(devices, bucket, LANES)
        out_ref[:, k * bucket : (k + 1) * bucket, :] = piece
    tail = rows[:, whole * LANES :].reshape(devices, bucket, LANES)
    half = bucket // 2
    left = iota((devices, half, LANES), 2) < LANES // 2
    turned = pltpu.roll(tail[:, half:], LANES // 2, 2)
    out_ref[:, whole * bucket :, :] = jnp.where(left, tail[:, :half], turned)


def prep_kernel(*refs):
    ins, (first_out, stack_out), refs = refs[:5], refs[5:7], refs[7:]
    raw, (first, stack, turned, in_sem, out_sem) = refs[:5], refs[5:]
    fetch = [
        pltpu.make_async_copy(ins[k], raw[k], in_sem.at[k]) for k in range(5)
    ]
    for copy in fetch:
        copy.start()
    sends = []

    def send(source, target):
        copy = pltpu.make_async_copy(source, target, out_sem.at[len(sends)])
        copy.start()
        sends.append(copy)

    def put(values, ref):
        rows, cols = values.shape
        if (rows, cols) != ref.shape[1:]:
            ref[...] = jnp.zeros_like(ref)
        ref[0, :rows, :cols], ref[1, :rows, :cols] = split(values)

    fetch[0].wait()
    put(raw[0][...].T, turned)
    fetch[1].wait()
    put(raw[1][...], first)
    send(first, first_out)
    rows = up(raw[0].shape[1], LANES)
    stack[3, :, rows:, :] = jnp.zeros((2,) + (stack.shape[2] - rows, stack.shape[3]), BF)
    for part in halves(rows):
        got = mm3(turned[0, part, :], turned[1, part, :], first[0], first[1])
        stack[3, 0, part, :], stack[3, 1, part, :] = split(got)
    send(stack.at[3], stack_out.at[3])
    for k in range(3):
        fetch[k + 2].wait()
        put(raw[k + 2][...], stack.at[k])
        send(stack.at[k], stack_out.at[k])
    for copy in sends:
        copy.wait()


def coeff_column(coeff_ref, row):
    wide = coeff_ref.shape[1]
    spread = jnp.broadcast_to(coeff_ref[row : row + 1, :], (wide, wide))
    diagonal = iota((wide, wide), 0) == iota((wide, wide), 1)
    return jnp.sum(jnp.where(diagonal, spread, 0.0), axis=1, keepdims=True)


def cut_kernel(v, side_ref, vectors_ref, coeff_ref, xa, xb, yhead, ytail, *refs):
    bufs, sems = refs[:4], refs[4]
    rows, wide, levels = vectors_ref.shape[1:]
    w = SWEEPS
    parts = (
        vectors_ref.at[v, pl.ds(0, w)],
        vectors_ref.at[v, pl.ds(rows - w, w)],
        vectors_ref.at[v, :, pl.ds(0, 8)],
        vectors_ref.at[v, :, pl.ds(wide - 8, 8)],
    )
    copies = [pltpu.make_async_copy(parts[k], bufs[k], sems.at[k]) for k in range(4)]
    for copy in copies:
        copy.start()
    even = side_ref[0] == 0
    if v == 0:
        columns = [coeff_column(coeff_ref, row) for row in range(rows)]
        for row in range(w):
            head, tail = columns[row], columns[rows - w + row]
            xa[row, :, levels:] = jnp.where(even, tail, head)
            xb[row, :, levels:] = jnp.where(even, head, tail)
        for row in range(rows):
            yhead[row, :, levels:] = columns[row][:w]
            ytail[row, :, levels:] = columns[row][wide - w :]
    for copy in copies:
        copy.wait()
    head, tail = bufs[0][...], bufs[1][...]
    xa[:, :, :levels] = jnp.where(even, tail, head)
    xb[:, :, :levels] = jnp.where(even, head, tail)
    yhead[:, :, :levels] = bufs[2][:, :w]
    ytail[:, :, :levels] = bufs[3][:, 8 - w :]


def join_kernel(side_ref, ra, rb, yhead, ytail, ya, yb):
    w = SWEEPS
    rows = yhead.shape[0]
    wide = ra.shape[1]
    even_x, even_y = side_ref[0] == 0, side_ref[1] == 0

    for here, first, second in (
        (pl.ds(0, w), rb, ra),
        (pl.ds(w + rows, w), ra, rb),
    ):
        head = jnp.where(even_x, first[:, :w], second[:, :w])
        tail = jnp.where(even_x, first[:, wide - w :], second[:, wide - w :])
        ya[here] = jnp.where(even_y, tail, head)
        yb[here] = jnp.where(even_y, head, tail)
    here = pl.ds(w, rows)
    ya[here] = jnp.where(even_y, ytail[...], yhead[...])
    yb[here] = jnp.where(even_y, yhead[...], ytail[...])


def fill(ext, side_ref, tile, ra, rb, qa, qb, part):
    rows, wide = tile.shape[:2]
    w = SWEEPS
    even_y = side_ref[1] == 0
    upper = jnp.where(side_ref[0] == 0, w + rows, 0)
    tile_part, strip_part = part
    ext[w : w + rows, :wide, tile_part] = tile
    ext[pl.ds(upper, w), :wide, tile_part] = strip_part(ra)
    ext[pl.ds(w + rows - upper, w), :wide, tile_part] = strip_part(rb)
    qa, qb = strip_part(qa), strip_part(qb)
    ext[:, wide : wide + w, tile_part] = jnp.where(even_y, qa, qb)
    ext[:, wide + w :, tile_part] = jnp.where(even_y, qb, qa)


def fill_levels(ext, side_ref, tile, *strips):
    levels = tile.shape[2]
    last = up(levels, LANES) - LANES
    ext[:, :, last:] = jnp.zeros((ext.shape[0], ext.shape[1], ext.shape[2] - last), F32)
    part = (pl.ds(0, levels), lambda ref: ref[:, :, :levels])
    fill(ext, side_ref, tile, *strips, part)


def sweeps(load, cb_ref, work, emit, wide):
    tall, around = cb_ref.shape[1:3]

    def put(buffer, i, value):
        work[buffer, i, 8 : 8 + around] = value
        work[buffer, i, :8] = value[around - 8 :]
        work[buffer, i, 8 + around :] = value[:8]

    for i in range(tall):
        put(0, i, load(i))
    for sweep in range(SWEEPS):
        source = sweep % 2
        last = sweep == SWEEPS - 1
        size = wide if last else around
        for i in range(sweep + 1, tall - 1 - sweep):

            def near(row, by):
                return work[source, row, 8 + by : 8 + by + size]

            beside = (near(i - 1, 0) + near(i + 1, 0)) + (near(i, -1) + near(i, 1))
            new = cb_ref[1, i, :size] * near(i, 0) + cb_ref[0, i, :size] * beside
            if last:
                emit(i - SWEEPS, new)
            else:
                put(1 - source, i, new)


def diffuse_kernel(v, side_ref, tile_ref, coeff_ref, *refs):
    strips, stack_ref, refs = refs[:4], refs[4], refs[5:]
    ext, work, high_ref, low_ref, both, sem = refs[-6:]
    out_ref = refs[0]
    fetch = Fetch(stack_ref.at[3], both, sem)
    fetch.start()
    rows, wide, levels = tile_ref.shape[1:]
    fill_levels(ext, side_ref, tile_ref[v], *strips)
    if v > 0:
        cb_ref = coeff_ref
    else:
        cb_ref = refs[1]

        def spread(ref):
            column = ref[:, :, levels : levels + 1]
            return jnp.broadcast_to(column, column.shape[:2] + (LANES,))

        own = jnp.stack(
            [jnp.broadcast_to(coeff_column(coeff_ref, k), (wide, LANES)) for k in range(rows)]
        )
        fill(cb_ref.at[0], side_ref, own, *strips, (pl.ds(0, LANES), spread))
        cb_ref[1] = 1.0 - 4.0 * cb_ref[0]
        cb_ref[2] = 1.0 / jnp.where(cb_ref[0] == 0.0, 1.0, cb_ref[0])

    def chunk(j, _):
        lanes = pl.ds(pl.multiple_of(j * LANES, LANES), LANES)

        def emit(row, value):
            here = pl.ds(row * wide, wide)
            high_ref[here, lanes], low_ref[here, lanes] = split(value)

        sweeps(lambda i: ext[i, :, lanes], cb_ref, work, emit, wide)
        return 0

    lax.fori_loop(0, ext.shape[2] // LANES, chunk, 0)
    deep = ext.shape[2]
    fetch.wait()
    for part in halves(out_ref.shape[0]):
        out_ref[part, :] = mm3(
            high_ref[part, :], low_ref[part, :], both[0, :deep], both[1, :deep]
        )


def hidden_kernel(
    mark, bucket, x_ref, first_ref, b1_ref, stack_ref, b2_ref, mask_ref,
    scale_ref, one_ref, one_t_ref, high_ref, low_ref, x_buf, first, second, sems,
):
    fetch_x = pltpu.make_async_copy(x_ref, x_buf, sems.at[2, 0])
    fetch_x.start()
    fetch_first = Fetch(first_ref, first, sems.at[0])
    fetch_second = Fetch(stack_ref.at[0], second, sems.at[1])
    fetch_first.start()
    s1_ref, s2_ref, gate_ref = (scale_ref.at[k] for k in range(3))
    slots, cells = one_ref.shape
    devices, channels = mask_ref.shape
    fetch_x.wait()
    if len(x_buf.shape) == 2:
        deep = x_buf.shape[1]
        pieces = [x_buf[:, k : k + LANES] for k in range(0, deep, LANES)]
    else:
        whole = x_buf.shape[1] // bucket
        deep = (whole + 1) * LANES
        pieces = [
            x_buf[:, k * bucket : (k + 1) * bucket, :].reshape(slots, LANES)
            for k in range(whole)
        ]
        tail = x_buf[:, whole * bucket :, :]
        tail = jnp.concatenate([tail, pltpu.roll(tail, LANES // 2, 2)], axis=1)
        pieces.append(tail.reshape(slots, LANES))
    index = pieces[-1][:, mark % LANES : mark % LANES + 1]
    cell = index.astype(jnp.int32) - 1
    live = index > 0.5
    one_ref[...] = (iota((slots, cells), 1) == cell).astype(BF)
    flat = jnp.broadcast_to(index, (slots, LANES)).T[0:1, :].astype(jnp.int32) - 1
    one_t_ref[...] = (iota((cells, slots), 0) == flat).astype(BF)
    begin = iota((slots, devices), 1) * bucket
    at = iota((slots, devices), 0)
    from_owner = ((at >= begin) & (at < begin + bucket) & live).astype(BF)
    gate_ref[...] = jnp.zeros_like(gate_ref)
    gate_ref[:, :channels] = mm(from_owner, mask_ref[...].astype(F32).astype(BF))
    for k, piece in enumerate(pieces):
        here = pl.ds(k * LANES, LANES)
        high_ref[:, here], low_ref[:, here] = split(piece)
    parts = halves(slots)
    fetch_first.wait()
    fetch_second.start()
    for part in parts:
        got = mm3(high_ref[part, :deep], low_ref[part, :deep], first[0, :deep], first[1, :deep])
        hidden = jnp.tanh(got + b1_ref[...])
        s1_ref[part, :] = 1.0 - hidden * hidden
        high, low = split(hidden)
        high_ref[part, :] = high
        low_ref[part, :] = low
    fetch_second.wait()
    for part in parts:
        got = mm3(high_ref[part, :], low_ref[part, :], second[0], second[1])
        hidden = jnp.tanh(got + b2_ref[...])
        s2_ref[part, :] = 1.0 - hidden * hidden


LAYERS = ((0, 0, 1), (1, 1, 2), (2, 0, 2), (1, 0, 1), (0, 1, 0))


def table(values, layer):
    value = jnp.int32(values[0])
    for k in range(1, len(values)):
        value = jnp.where(layer == k, values[k], value)
    return value


def net_kernel(
    side_ref, q_ref, one_ref, one_t_ref, scale_ref, stack_ref,
    out_ref, xa, xb, yhead, ytail, x1, top, low, acc_top, acc_low, stack, sems,
):
    fetch = [Fetch(stack_ref.at[k], stack.at[k], sems.at[k]) for k in range(4)]
    fetch[0].start()
    slots = q_ref.shape[0]
    half = slots // 2
    first, second = pl.ds(0, half), pl.ds(half, half)

    def pick(picker):
        return mm(picker, x1[0]) + mm(picker, x1[1])

    def close(acc, scale, part, target):
        target[0], target[1] = split(acc[...] * scale_ref[scale, part, :])

    x1[0], x1[1] = split(q_ref[...])
    acc_top[...] = pick(one_ref[first, :])
    acc_low[...] = pick(one_ref[second, :])
    close(acc_top, 0, first, top)
    fetch[0].wait()
    fetch[1].start()
    scales = [0] + [entry[2] for entry in LAYERS]

    def step(layer, _):
        for k in (1, 2):

            @pl.when(layer == k)
            def _():
                fetch[k].wait()
                fetch[k + 1].start()

        weight = table([entry[0] for entry in LAYERS], layer)
        turned = table([entry[1] for entry in LAYERS], layer)
        before, after = table(scales[:-1], layer), table(scales[1:], layer)

        def run(dims):
            acc_top[...] = mm3(top[0], top[1], stack[weight, 0], stack[weight, 1], dims)
            close(acc_low, before, second, low)
            acc_low[...] = mm3(low[0], low[1], stack[weight, 0], stack[weight, 1], dims)
            close(acc_top, after, first, top)

        @pl.when(turned == 0)
        def _():
            run(NN)

        @pl.when(turned == 1)
        def _():
            run(NT)

        return 0

    lax.fori_loop(0, len(LAYERS), step, 0)
    close(acc_low, scales[-1], second, low)
    for part in halves(one_t_ref.shape[0]):
        got = mm(one_t_ref[part, :half], top[0]) + mm(one_t_ref[part, :half], top[1])
        got = got + mm(one_t_ref[part, half:], low[0]) + mm(one_t_ref[part, half:], low[1])
        x1[0, part, :], x1[1, part, :] = split(got)
    fetch[3].wait()
    rows, wide, levels = out_ref.shape
    for k, part in enumerate(halves(rows * wide)):
        got = mm3(x1[0, part, :], x1[1, part, :], stack[3, 0], stack[3, 1], NT)
        tall = got.shape[0] // wide
        got = got.reshape(tall, wide, got.shape[1])[:, :, :levels]
        here = pl.ds(k * tall, tall)
        out_ref[here] = got
        yhead[here] = got[:, :SWEEPS]
        ytail[here] = got[:, wide - SWEEPS :]
    even = side_ref[0] == 0
    head, tail = out_ref[:SWEEPS], out_ref[rows - SWEEPS :]
    xa[...] = jnp.where(even, tail, head)
    xb[...] = jnp.where(even, head, tail)


def finish_kernel(v, side_ref, field_ref, base_ref, cb_ref, *refs):
    out_ref, ext, work, total, result, sems = refs[-6:]
    w = SWEEPS
    rows, wide, levels = field_ref.shape
    fill_levels(ext, side_ref, field_ref[...], *refs[:4])

    def chunk(j, _):
        lanes = pl.ds(pl.multiple_of(j * LANES, LANES), LANES)

        def emit(row, value):
            total[row, :, lanes] = cb_ref[2, row + w, :wide] * value

        sweeps(lambda i: cb_ref[0, i] * ext[i, :, lanes], cb_ref, work, emit, wide)
        return 0

    lax.fori_loop(0, ext.shape[2] // LANES, chunk, 0)
    sends = []
    for k in range(2):
        part = pl.ds(k * (rows // 2), rows // 2)
        result[part] = base_ref[v, part] + total[part, :, :levels]
        sends.append(pltpu.make_async_copy(result.at[part], out_ref.at[v, part], sems.at[k]))
        sends[-1].start()
    for copy in sends:
        copy.wait()


def swap(value, axis, start):
    pairs = [(i, i + 1) for i in range(start, lax.axis_size(axis) - 1, 2)]
    return lax.ppermute(value, axis, pairs + [(j, i) for i, j in pairs])


def halo(sides, xa, xb, yhead, ytail):
    ra = swap(xa, "gx", 0)
    rb = swap(xb, "gx", 1)
    whole = pl.BlockSpec(memory_space=pltpu.VMEM)
    tall = yhead.shape[0] + 2 * SWEEPS
    ya, yb = call(
        join_kernel,
        [shaped((tall,) + yhead.shape[1:])] * 2,
        flops=0,
        moved=16 * yhead.size,
        vmem=8,
        in_specs=[pl.BlockSpec(memory_space=pltpu.SMEM)] + [whole] * 4,
    )(sides, ra, rb, yhead, ytail)
    qa = swap(ya, "gy", 0)
    qb = swap(yb, "gy", 1)
    return ra, rb, qa, qb


def body(
    vectors, diffusivity, vertical_factor, weight_first, bias_first, weight_second,
    bias_second, weight_out, error_inverse, observed_column, owner_count,
    observed_state, channel_mask,
):
    pairs, tile_x, tile_y, levels = vectors.shape
    count_y = lax.axis_size("gy")
    devices = lax.axis_size("gx") * count_y
    slots = observed_column.shape[0]
    bucket = slots // devices
    cells = tile_x * tile_y
    grid_wide = tile_y * count_y
    units = weight_second.shape[0]
    deep = up(levels, LANES)
    tall, around = tile_x + 2 * SWEEPS, tile_y + 2 * SWEEPS
    full_l, full_u = up(levels, WIDE), up(units, WIDE)
    full_c = up(error_inverse.shape[0], WIDE)
    mark = up(levels, 16)

    sides = jnp.stack([lax.axis_index("gx") % 2, lax.axis_index("gy") % 2]).astype(jnp.int32)
    whole = pl.BlockSpec(memory_space=pltpu.VMEM)
    far = pl.BlockSpec(memory_space=pltpu.HBM)
    scalars = pl.BlockSpec(memory_space=pltpu.SMEM)
    base = pltpu.with_memory_space_constraint(vectors, pltpu.HBM)
    strips = []
    for v in range(pairs):
        deep_v = levels + (v == 0)
        cuts = call(
            functools.partial(cut_kernel, v),
            [shaped((SWEEPS, tile_y, deep_v))] * 2 + [shaped((tile_x, SWEEPS, deep_v))] * 2,
            flops=0,
            moved=4 * vectors.size,
            vmem=12,
            scratch=[pltpu.VMEM((SWEEPS, tile_y, levels), F32)] * 2
            + [pltpu.VMEM((tile_x, 8, levels), F32)] * 2
            + [pltpu.SemaphoreType.DMA((4,))],
            in_specs=[scalars, far, whole],
        )(sides, base, diffusivity)
        strips.append(halo(sides, *cuts))

    position = jnp.arange(slots, dtype=jnp.int32)
    grid_row = observed_column // grid_wide
    grid_col = observed_column % grid_wide
    target = grid_row // tile_x * count_y + grid_col // tile_y
    dest = jnp.where(position < owner_count[0], target, -1)
    cell = (grid_row % tile_x * tile_y + grid_col % tile_y + 1).astype(F32)
    tight = bucket % 16 == 0 and mark // LANES == deep // LANES - 1 and mark % LANES < LANES // 2
    packed_shape = (slots, deep)
    if tight:
        packed_shape = (devices, bucket * (deep // LANES - 1) + bucket // 2, LANES)
    packed = call(
        functools.partial(pack_kernel, bucket),
        shaped(packed_shape),
        flops=6 * slots * slots * deep,
        moved=8 * slots * deep,
        scratch=[pltpu.VMEM((deep, slots), BF)] * 2,
        vmem=12,
    )(dest[None, :], cell[None, :], observed_state.T)
    carried = lax.all_to_all(
        packed if tight else packed.reshape(devices, bucket, deep), ("gx", "gy"),
        split_axis=0, concat_axis=0, tiled=True,
    ).reshape(packed_shape)

    side = max(full_l, full_u, full_c)
    weights = (vertical_factor, weight_first, weight_second, weight_out.T, error_inverse)
    first, stack = call(
        prep_kernel,
        [pltpu.HBM((2, full_l, side), BF), pltpu.HBM((4, 2, side, side), BF)],
        flops=6 * full_l * full_l * full_u,
        moved=8 * 5 * full_u * full_u,
        scratch=[pltpu.VMEM(weight.shape, F32) for weight in weights]
        + [
            pltpu.VMEM((2, full_l, side), BF), pltpu.VMEM((4, 2, side, side), BF),
            pltpu.VMEM((2, side, full_l), BF),
            pltpu.SemaphoreType.DMA((5,)), pltpu.SemaphoreType.DMA((5,)),
        ],
        vmem=27,
        in_specs=[far] * 5,
        out_specs=[far] * 2,
    )(*[pltpu.with_memory_space_constraint(weight, pltpu.HBM) for weight in weights])
    first, stack = (pltpu.with_memory_space_constraint(x, pltpu.HBM) for x in (first, stack))

    def wide_bias(bias):
        return jnp.pad(bias, (0, side - bias.shape[0]))[None, :]

    queries = []
    for v in range(pairs):
        got = call(
            functools.partial(diffuse_kernel, v),
            [shaped((cells, side))] + [shaped((3, tall, around, LANES))] * (v == 0),
            flops=6 * cells * deep * full_u,
            moved=8 * tall * around * deep,
            scratch=[
                pltpu.VMEM((tall, around, deep), F32),
                pltpu.VMEM((2, tall, around + 16, LANES), F32),
                pltpu.VMEM((cells, deep), BF),
                pltpu.VMEM((cells, deep), BF),
                pltpu.VMEM((2, side, side), BF),
                pltpu.SemaphoreType.DMA((4,)),
            ],
            vmem=16,
            in_specs=[scalars, whole] + [whole] * 5 + [far],
            out_specs=[whole] * (2 - (v > 0)),
        )(sides, vectors, spread if v else diffusivity, *strips[v], stack)
        queries.append(got[0])
        if v == 0:
            spread = got[1]

    scale, one, one_t = call(
        functools.partial(hidden_kernel, mark, bucket),
        [shaped((3, slots, side)), shaped((slots, cells), BF), shaped((cells, slots), BF)],
        flops=12 * slots * full_u * full_u,
        moved=8 * slots * full_u,
        scratch=[pltpu.VMEM((slots, side), BF)] * 2
        + [
            pltpu.VMEM(packed_shape, F32),
            pltpu.VMEM((2, full_l, side), BF), pltpu.VMEM((2, side, side), BF),
            pltpu.SemaphoreType.DMA((3, 4)),
        ],
        vmem=18,
        in_specs=[far, far, whole, far, whole, whole],
    )(pltpu.with_memory_space_constraint(carried, pltpu.HBM), first, wide_bias(bias_first), stack, wide_bias(bias_second), channel_mask)

    fields = []
    for v in range(pairs):
        fields.append(
            call(
                net_kernel,
                [shaped((tile_x, tile_y, levels))]
                + [shaped((SWEEPS, tile_y, levels))] * 2
                + [shaped((tile_x, SWEEPS, levels))] * 2,
                flops=36 * slots * full_u * full_u,
                moved=4 * 5 * full_u * full_u,
                scratch=[pltpu.VMEM((2, slots, side), BF)]
                + [pltpu.VMEM((2, slots // 2, side), BF)] * 2
                + [pltpu.VMEM((slots // 2, side), F32)] * 2
                + [
                    pltpu.VMEM((4, 2, side, side), BF),
                    pltpu.SemaphoreType.DMA((4, 4)),
                ],
                vmem=22,
                in_specs=[scalars] + [whole] * 4 + [far],
            )(sides, queries[v], one, one_t, scale, stack)
        )

    out = None
    for v in range(pairs):
        around_field = halo(sides, *fields[v][1:])
        carry = [] if out is None else [out]
        out = call(
            functools.partial(finish_kernel, v),
            pltpu.HBM(vectors.shape, F32),
            flops=40 * tall * around * deep,
            moved=12 * cells * deep,
            scratch=[
                pltpu.VMEM((tall, around, deep), F32),
                pltpu.VMEM((2, tall, around + 16, LANES), F32),
                pltpu.VMEM((tile_x, tile_y, deep), F32),
                pltpu.VMEM((tile_x, tile_y, levels), F32),
                pltpu.SemaphoreType.DMA((2,)),
            ],
            vmem=16,
            in_specs=[scalars] + [whole] * 7 + [far] * len(carry),
            out_specs=far,
            input_output_aliases={8: 0} if carry else {},
        )(sides, fields[v][0], vectors, spread, *around_field, *carry)
    return out


def solution(mesh):
    in_specs = (
        P(None, "gx", "gy", None),
        P("gx", "gy"),
        P(),
        P(),
        P(),
        P(),
        P(),
        P(),
        P(),
        P(("gx", "gy")),
        P(("gx", "gy")),
        P(("gx", "gy"), None),
        P(),
    )
    out_specs = P(None, "gx", "gy", None)
    return jax.shard_map(body, mesh=mesh, in_specs=in_specs, out_specs=out_specs, check_vma=False)
```

```python
import functools

import jax
import jax.numpy as jnp
from jax import lax
from jax.experimental import pallas as pl
from jax.experimental.pallas import tpu as pltpu
from jax.sharding import PartitionSpec as P

SWEEPS = 4
WIDE = 256
LANES = 128
BF = jnp.bfloat16
F32 = jnp.float32
NN = ((1,), (0,))
NT = ((1,), (1,))


def up(size, unit):
    return -(-size // unit) * unit


def split(value):
    high = value.astype(BF)
    return high, (value - high.astype(F32)).astype(BF)


def mm(left, right, dims=NN):
    return lax.dot_general(left, right, (dims, ((), ())), preferred_element_type=F32)


def mm3(left_high, left_low, right_high, right_low, dims=NN):
    if left_high.shape[dims[0][0]] % WIDE == 0:
        return mm(left_high, right_high, dims) + (
            mm(left_high, right_low, dims) + mm(left_low, right_high, dims)
        )
    left = jnp.concatenate([left_high, left_low, left_high], axis=dims[0][0])
    right = jnp.concatenate([right_high, right_high, right_low], axis=dims[1][0])
    return mm(left, right, dims)


def halves(size):
    half = size // 2
    return [pl.ds(0, half), pl.ds(half, half)] if half % 16 == 0 else [pl.ds(0, size)]


def each_part(size, work, count=2):
    step = size // count if size % (16 * count) == 0 else size

    def run(k, _):
        work(pl.ds(pl.multiple_of(k * step, step), step))
        return 0

    lax.fori_loop(0, size // step, run, 0)


def iota(shape, axis):
    return lax.broadcasted_iota(jnp.int32, shape, axis)


def call(kernel, out_shape, flops, moved, scratch=(), vmem=48, **more):
    return pl.pallas_call(
        kernel,
        out_shape=out_shape,
        scratch_shapes=list(scratch),
        compiler_params=pltpu.CompilerParams(vmem_limit_bytes=vmem * 1024 * 1024),
        cost_estimate=pl.CostEstimate(flops=flops, bytes_accessed=moved, transcendentals=0),
        **more,
    )


def shaped(shape, dtype=F32):
    return jax.ShapeDtypeStruct(shape, dtype)


def pack_kernel(bucket, dest_ref, cell_ref, state_ref, out_ref, high_ref, low_ref):
    levels, slots = state_ref.shape
    devices = slots // bucket
    dest = dest_ref[...]
    same = (iota((devices, slots), 0) == dest).astype(F32)
    before = (iota((slots, slots), 0) < iota((slots, slots), 1)).astype(BF)
    rank = jnp.sum(same * mm(same.astype(BF), before), axis=0, keepdims=True)
    place = dest * bucket + rank.astype(jnp.int32)
    pick = (iota((slots, slots), 0) == place).astype(BF)
    high_ref[...] = jnp.zeros_like(high_ref)
    low_ref[...] = jnp.zeros_like(low_ref)
    high, low = split(state_ref[...])
    high_ref[:levels, :] = high
    low_ref[:levels, :] = low
    mark = up(levels, 16)
    tall = jnp.where(iota((16, slots), 0) == 0, cell_ref[...], 0.0)
    high, low = split(tall)
    high_ref[mark : mark + 16, :] = high
    low_ref[mark : mark + 16, :] = low
    rows = mm(pick, high_ref[...], NT) + mm(pick, low_ref[...], NT)
    if out_ref.shape == rows.shape:
        out_ref[...] = rows
        return
    whole = rows.shape[1] // LANES - 1
    for k in range(whole):
        piece = rows[:, k * LANES : (k + 1) * LANES].reshape(devices, bucket, LANES)
        out_ref[:, k * bucket : (k + 1) * bucket, :] = piece
    tail = rows[:, whole * LANES :].reshape(devices, bucket, LANES)
    half = bucket // 2
    left = iota((devices, half, LANES), 2) < LANES // 2
    turned = pltpu.roll(tail[:, half:], LANES // 2, 2)
    out_ref[:, whole * bucket :, :] = jnp.where(left, tail[:, :half], turned)


def prep_kernel(*refs):
    ins, (first_out, stack_out), refs = refs[:5], refs[5:7], refs[7:]
    raw, (first, stack, turned, in_sem, out_sem) = refs[:5], refs[5:]
    fetch = [
        pltpu.make_async_copy(ins[k], raw[k], in_sem.at[k]) for k in range(5)
    ]
    for copy in fetch:
        copy.start()
    sends = []

    def send(source, target):
        copy = pltpu.make_async_copy(source, target, out_sem.at[len(sends)])
        copy.start()
        sends.append(copy)

    def put(values, ref):
        rows, cols = values.shape
        if (rows, cols) != ref.shape[1:]:
            ref[...] = jnp.zeros_like(ref)
        ref[0, :rows, :cols], ref[1, :rows, :cols] = split(values)

    fetch[0].wait()
    put(raw[0][...].T, turned)
    fetch[1].wait()
    put(raw[1][...], first)
    send(first, first_out)
    rows = up(raw[0].shape[1], LANES)
    stack[3, :, rows:, :] = jnp.zeros((2,) + (stack.shape[2] - rows, stack.shape[3]), BF)

    def half(part):
        got = mm3(turned[0, part, :], turned[1, part, :], first[0], first[1])
        stack[3, 0, part, :], stack[3, 1, part, :] = split(got)

    each_part(rows, half)
    send(stack.at[3], stack_out.at[3])
    for k in range(3):
        fetch[k + 2].wait()
        if raw[k + 2].shape == stack.shape[2:]:

            def rows_of(part, k=k):
                stack[k, 0, part, :], stack[k, 1, part, :] = split(raw[k + 2][part, :])

            each_part(stack.shape[2], rows_of, 4)
        else:
            put(raw[k + 2][...], stack.at[k])
        send(stack.at[k], stack_out.at[k])
    for copy in sends:
        copy.wait()


def coeff_column(coeff_ref, row):
    wide = coeff_ref.shape[1]
    spread = jnp.broadcast_to(coeff_ref[row : row + 1, :], (wide, wide))
    diagonal = iota((wide, wide), 0) == iota((wide, wide), 1)
    return jnp.sum(jnp.where(diagonal, spread, 0.0), axis=1, keepdims=True)


def cut_kernel(v, side_ref, vectors_ref, coeff_ref, xa, xb, yhead, ytail, *refs):
    bufs, sems = refs[:4], refs[4]
    rows, wide, levels = vectors_ref.shape[1:]
    w = SWEEPS
    parts = (
        vectors_ref.at[v, pl.ds(0, w)],
        vectors_ref.at[v, pl.ds(rows - w, w)],
        vectors_ref.at[v, :, pl.ds(0, 8)],
        vectors_ref.at[v, :, pl.ds(wide - 8, 8)],
    )
    copies = [pltpu.make_async_copy(parts[k], bufs[k], sems.at[k]) for k in range(4)]
    for copy in copies:
        copy.start()
    even = side_ref[0] == 0
    if v == 0:
        columns = [coeff_column(coeff_ref, row) for row in range(rows)]
        for row in range(w):
            head, tail = columns[row], columns[rows - w + row]
            xa[row, :, levels:] = jnp.where(even, tail, head)
            xb[row, :, levels:] = jnp.where(even, head, tail)
        for row in range(rows):
            yhead[row, :, levels:] = columns[row][:w]
            ytail[row, :, levels:] = columns[row][wide - w :]
    for copy in copies:
        copy.wait()
    head, tail = bufs[0][...], bufs[1][...]
    xa[:, :, :levels] = jnp.where(even, tail, head)
    xb[:, :, :levels] = jnp.where(even, head, tail)
    yhead[:, :, :levels] = bufs[2][:, :w]
    ytail[:, :, :levels] = bufs[3][:, 8 - w :]


def join_kernel(side_ref, ra, rb, yhead, ytail, ya, yb):
    w = SWEEPS
    rows = yhead.shape[0]
    wide = ra.shape[1]
    even_x, even_y = side_ref[0] == 0, side_ref[1] == 0

    for here, first, second in (
        (pl.ds(0, w), rb, ra),
        (pl.ds(w + rows, w), ra, rb),
    ):
        head = jnp.where(even_x, first[:, :w], second[:, :w])
        tail = jnp.where(even_x, first[:, wide - w :], second[:, wide - w :])
        ya[here] = jnp.where(even_y, tail, head)
        yb[here] = jnp.where(even_y, head, tail)
    here = pl.ds(w, rows)
    ya[here] = jnp.where(even_y, ytail[...], yhead[...])
    yb[here] = jnp.where(even_y, yhead[...], ytail[...])


def fill(ext, side_ref, tile, ra, rb, qa, qb, part):
    rows, wide = tile.shape[:2]
    w = SWEEPS
    even_y = side_ref[1] == 0
    upper = jnp.where(side_ref[0] == 0, w + rows, 0)
    tile_part, strip_part = part
    ext[w : w + rows, :wide, tile_part] = tile
    ext[pl.ds(upper, w), :wide, tile_part] = strip_part(ra)
    ext[pl.ds(w + rows - upper, w), :wide, tile_part] = strip_part(rb)
    qa, qb = strip_part(qa), strip_part(qb)
    ext[:, wide : wide + w, tile_part] = jnp.where(even_y, qa, qb)
    ext[:, wide + w :, tile_part] = jnp.where(even_y, qb, qa)


def fill_levels(ext, side_ref, tile, *strips):
    levels = tile.shape[2]
    last = up(levels, LANES) - LANES
    ext[:, :, last:] = jnp.zeros((ext.shape[0], ext.shape[1], ext.shape[2] - last), F32)
    part = (pl.ds(0, levels), lambda ref: ref[:, :, :levels])
    fill(ext, side_ref, tile, *strips, part)


def sweeps(load, cb_ref, work, emit, wide):
    tall, around = cb_ref.shape[1:3]

    def put(buffer, i, value):
        work[buffer, i, 8 : 8 + around] = value
        work[buffer, i, :8] = value[around - 8 :]
        work[buffer, i, 8 + around :] = value[:8]

    for i in range(tall):
        put(0, i, load(i))
    for sweep in range(SWEEPS):
        source = sweep % 2
        last = sweep == SWEEPS - 1
        size = wide if last else around
        for i in range(sweep + 1, tall - 1 - sweep):

            def near(row, by):
                return work[source, row, 8 + by : 8 + by + size]

            beside = (near(i - 1, 0) + near(i + 1, 0)) + (near(i, -1) + near(i, 1))
            new = cb_ref[1, i, :size] * near(i, 0) + cb_ref[0, i, :size] * beside
            if last:
                emit(i - SWEEPS, new)
            else:
                put(1 - source, i, new)


def diffuse_kernel(v, side_ref, tile_ref, coeff_ref, *refs):
    strips, stack_ref, refs = refs[:4], refs[4], refs[5:]
    ext, work, high_ref, low_ref, both, sem = refs[-6:]
    out_ref = refs[0]
    fetch = pltpu.make_async_copy(stack_ref.at[3], both, sem)
    fetch.start()
    rows, wide, levels = tile_ref.shape[1:]
    fill_levels(ext, side_ref, tile_ref[v], *strips)
    if v > 0:
        cb_ref = coeff_ref
    else:
        cb_ref = refs[1]

        def spread(ref):
            column = ref[:, :, levels : levels + 1]
            return jnp.broadcast_to(column, column.shape[:2] + (LANES,))

        own = jnp.stack(
            [jnp.broadcast_to(coeff_column(coeff_ref, k), (wide, LANES)) for k in range(rows)]
        )
        fill(cb_ref.at[0], side_ref, own, *strips, (pl.ds(0, LANES), spread))
        cb_ref[1] = 1.0 - 4.0 * cb_ref[0]
        cb_ref[2] = 1.0 / jnp.where(cb_ref[0] == 0.0, 1.0, cb_ref[0])

    def chunk(j, _):
        lanes = pl.ds(pl.multiple_of(j * LANES, LANES), LANES)

        def emit(row, value):
            here = pl.ds(row * wide, wide)
            high_ref[here, lanes], low_ref[here, lanes] = split(value)

        sweeps(lambda i: ext[i, :, lanes], cb_ref, work, emit, wide)
        return 0

    lax.fori_loop(0, ext.shape[2] // LANES, chunk, 0)
    deep = ext.shape[2]
    fetch.wait()

    def half(part):
        out_ref[part, :] = mm3(
            high_ref[part, :], low_ref[part, :], both[0, :deep], both[1, :deep]
        )

    each_part(out_ref.shape[0], half)


def hidden_kernel(
    mark, bucket, x_ref, first_ref, b1_ref, stack_ref, b2_ref, mask_ref,
    scale_ref, one_ref, one_t_ref, high_ref, low_ref, x_buf, first, second, sems,
):
    fetch_x = pltpu.make_async_copy(x_ref, x_buf, sems.at[2])
    fetch_x.start()
    fetch_first = pltpu.make_async_copy(first_ref, first, sems.at[0])
    fetch_second = pltpu.make_async_copy(stack_ref.at[0], second, sems.at[1])
    fetch_first.start()
    fetch_second.start()
    s1_ref, s2_ref, gate_ref = (scale_ref.at[k] for k in range(3))
    slots, cells = one_ref.shape
    devices, channels = mask_ref.shape
    fetch_x.wait()
    if len(x_buf.shape) == 2:
        deep = x_buf.shape[1]
        pieces = [x_buf[:, k : k + LANES] for k in range(0, deep, LANES)]
    else:
        whole = x_buf.shape[1] // bucket
        deep = (whole + 1) * LANES
        pieces = [
            x_buf[:, k * bucket : (k + 1) * bucket, :].reshape(slots, LANES)
            for k in range(whole)
        ]
        tail = x_buf[:, whole * bucket :, :]
        tail = jnp.concatenate([tail, pltpu.roll(tail, LANES // 2, 2)], axis=1)
        pieces.append(tail.reshape(slots, LANES))
    index = pieces[-1][:, mark % LANES : mark % LANES + 1]
    cell = index.astype(jnp.int32) - 1
    live = index > 0.5
    one_ref[...] = (iota((slots, cells), 1) == cell).astype(BF)
    flat = jnp.broadcast_to(index, (slots, LANES)).T[0:1, :].astype(jnp.int32) - 1
    one_t_ref[...] = (iota((cells, slots), 0) == flat).astype(BF)
    begin = iota((slots, devices), 1) * bucket
    at = iota((slots, devices), 0)
    from_owner = ((at >= begin) & (at < begin + bucket) & live).astype(BF)
    gate_ref[...] = jnp.zeros_like(gate_ref)
    gate_ref[:, :channels] = mm(from_owner, mask_ref[...].astype(F32).astype(BF))
    for k, piece in enumerate(pieces):
        here = pl.ds(k * LANES, LANES)
        high_ref[:, here], low_ref[:, here] = split(piece)
    fetch_first.wait()
    parts = halves(slots)
    for part in parts:
        got = mm3(high_ref[part, :deep], low_ref[part, :deep], first[0, :deep], first[1, :deep])
        hidden = jnp.tanh(got + b1_ref[...])
        s1_ref[part, :] = 1.0 - hidden * hidden
        high_ref[part, :], low_ref[part, :] = split(hidden)
    fetch_second.wait()
    for part in parts:
        got = mm3(high_ref[part, :], low_ref[part, :], second[0], second[1])
        hidden = jnp.tanh(got + b2_ref[...])
        s2_ref[part, :] = 1.0 - hidden * hidden


LAYERS = ((0, NN, 1), (1, NT, 2), (2, NN, 2), (1, NN, 1), (0, NT, 0))


def net_kernel(
    side_ref, q_ref, one_ref, one_t_ref, scale_ref, stack_ref,
    out_ref, xa, xb, yhead, ytail, x1, top, low, acc_top, acc_low, stack, sems,
):
    fetch = [
        pltpu.make_async_copy(stack_ref.at[k], stack.at[k], sems.at[k]) for k in range(4)
    ]
    for copy in fetch:
        copy.start()
    slots = q_ref.shape[0]
    half = slots // 2
    first, second = pl.ds(0, half), pl.ds(half, half)

    def pick(picker):
        return mm(picker, x1[0]) + mm(picker, x1[1])

    def close(acc, scale, part, target):
        target[0], target[1] = split(acc[...] * scale_ref[scale, part, :])


    def take(part):
        x1[0, part, :], x1[1, part, :] = split(q_ref[part, :])

    each_part(slots, take, 4)
    acc_top[...] = pick(one_ref[first, :])
    acc_low[...] = pick(one_ref[second, :])
    close(acc_top, 0, first, top)
    fetch[0].wait()
    before = 0
    for layer, (weight, dims, scale) in enumerate(LAYERS):
        if layer in (1, 2):
            fetch[layer].wait()
        acc_top[...] = mm3(top[0], top[1], stack[weight, 0], stack[weight, 1], dims)
        close(acc_low, before, second, low)
        acc_low[...] = mm3(low[0], low[1], stack[weight, 0], stack[weight, 1], dims)
        close(acc_top, scale, first, top)
        before = scale
    close(acc_low, before, second, low)

    def scatter(part):
        got = mm(one_t_ref[part, :half], top[0]) + mm(one_t_ref[part, :half], top[1])
        got = got + mm(one_t_ref[part, half:], low[0]) + mm(one_t_ref[part, half:], low[1])
        x1[0, part, :], x1[1, part, :] = split(got)

    each_part(one_t_ref.shape[0], scatter)
    fetch[3].wait()
    rows, wide, levels = out_ref.shape
    parts = halves(rows * wide)
    size = parts[0].size
    tall = size // wide

    def place(k, _):
        part = pl.ds(pl.multiple_of(k * size, size), size)
        got = mm3(x1[0, part, :], x1[1, part, :], stack[3, 0], stack[3, 1], NT)
        got = got.reshape(tall, wide, got.shape[1])[:, :, :levels]
        here = pl.ds(k * tall, tall)
        out_ref[here] = got
        yhead[here] = got[:, :SWEEPS]
        ytail[here] = got[:, wide - SWEEPS :]
        return 0

    lax.fori_loop(0, len(parts), place, 0)
    even = side_ref[0] == 0
    head, tail = out_ref[:SWEEPS], out_ref[rows - SWEEPS :]
    xa[...] = jnp.where(even, tail, head)
    xb[...] = jnp.where(even, head, tail)


def finish_kernel(v, side_ref, field_ref, base_ref, cb_ref, *refs):
    out_ref, ext, work, total, result, sems = refs[-6:]
    w = SWEEPS
    rows, wide, levels = field_ref.shape
    fill_levels(ext, side_ref, field_ref[...], *refs[:4])

    def chunk(j, _):
        lanes = pl.ds(pl.multiple_of(j * LANES, LANES), LANES)

        def emit(row, value):
            total[row, :, lanes] = cb_ref[2, row + w, :wide] * value

        sweeps(lambda i: cb_ref[0, i] * ext[i, :, lanes], cb_ref, work, emit, wide)
        return 0

    lax.fori_loop(0, ext.shape[2] // LANES, chunk, 0)
    sends = []
    for k in range(2):
        part = pl.ds(k * (rows // 2), rows // 2)
        result[part] = base_ref[v, part] + total[part, :, :levels]
        sends.append(pltpu.make_async_copy(result.at[part], out_ref.at[v, part], sems.at[k]))
        sends[-1].start()
    for copy in sends:
        copy.wait()


def swap(value, axis, start):
    pairs = [(i, i + 1) for i in range(start, lax.axis_size(axis) - 1, 2)]
    return lax.ppermute(value, axis, pairs + [(j, i) for i, j in pairs])


def halo(sides, xa, xb, yhead, ytail):
    ra = swap(xa, "gx", 0)
    rb = swap(xb, "gx", 1)
    whole = pl.BlockSpec(memory_space=pltpu.VMEM)
    tall = yhead.shape[0] + 2 * SWEEPS
    ya, yb = call(
        join_kernel,
        [shaped((tall,) + yhead.shape[1:])] * 2,
        flops=0,
        moved=16 * yhead.size,
        vmem=8,
        in_specs=[pl.BlockSpec(memory_space=pltpu.SMEM)] + [whole] * 4,
    )(sides, ra, rb, yhead, ytail)
    qa = swap(ya, "gy", 0)
    qb = swap(yb, "gy", 1)
    return ra, rb, qa, qb


def body(
    vectors, diffusivity, vertical_factor, weight_first, bias_first, weight_second,
    bias_second, weight_out, error_inverse, observed_column, owner_count,
    observed_state, channel_mask,
):
    pairs, tile_x, tile_y, levels = vectors.shape
    count_y = lax.axis_size("gy")
    devices = lax.axis_size("gx") * count_y
    slots = observed_column.shape[0]
    bucket = slots // devices
    cells = tile_x * tile_y
    grid_wide = tile_y * count_y
    units = weight_second.shape[0]
    deep = up(levels, LANES)
    tall, around = tile_x + 2 * SWEEPS, tile_y + 2 * SWEEPS
    full_l, full_u = up(levels, WIDE), up(units, WIDE)
    full_c = up(error_inverse.shape[0], WIDE)
    mark = up(levels, 16)

    sides = jnp.stack([lax.axis_index("gx") % 2, lax.axis_index("gy") % 2]).astype(jnp.int32)
    whole = pl.BlockSpec(memory_space=pltpu.VMEM)
    far = pl.BlockSpec(memory_space=pltpu.HBM)
    scalars = pl.BlockSpec(memory_space=pltpu.SMEM)
    base = pltpu.with_memory_space_constraint(vectors, pltpu.HBM)
    strips = []
    for v in range(pairs):
        deep_v = levels + (v == 0)
        cuts = call(
            functools.partial(cut_kernel, v),
            [shaped((SWEEPS, tile_y, deep_v))] * 2 + [shaped((tile_x, SWEEPS, deep_v))] * 2,
            flops=0,
            moved=4 * vectors.size,
            vmem=12,
            scratch=[pltpu.VMEM((SWEEPS, tile_y, levels), F32)] * 2
            + [pltpu.VMEM((tile_x, 8, levels), F32)] * 2
            + [pltpu.SemaphoreType.DMA((4,))],
            in_specs=[scalars, far, whole],
        )(sides, base, diffusivity)
        strips.append(halo(sides, *cuts))

    position = jnp.arange(slots, dtype=jnp.int32)
    grid_row = observed_column // grid_wide
    grid_col = observed_column % grid_wide
    target = grid_row // tile_x * count_y + grid_col // tile_y
    dest = jnp.where(position < owner_count[0], target, -1)
    cell = (grid_row % tile_x * tile_y + grid_col % tile_y + 1).astype(F32)
    tight = bucket % 16 == 0 and mark // LANES == deep // LANES - 1 and mark % LANES < LANES // 2
    packed_shape = (slots, deep)
    if tight:
        packed_shape = (devices, bucket * (deep // LANES - 1) + bucket // 2, LANES)
    packed = call(
        functools.partial(pack_kernel, bucket),
        shaped(packed_shape),
        flops=6 * slots * slots * deep,
        moved=8 * slots * deep,
        scratch=[pltpu.VMEM((deep, slots), BF)] * 2,
        vmem=12,
    )(dest[None, :], cell[None, :], observed_state.T)
    carried = lax.all_to_all(
        packed if tight else packed.reshape(devices, bucket, deep), ("gx", "gy"),
        split_axis=0, concat_axis=0, tiled=True,
    ).reshape(packed_shape)

    side = max(full_l, full_u, full_c)
    weights = (vertical_factor, weight_first, weight_second, weight_out.T, error_inverse)
    first, stack = call(
        prep_kernel,
        [pltpu.HBM((2, full_l, side), BF), pltpu.HBM((4, 2, side, side), BF)],
        flops=6 * full_l * full_l * full_u,
        moved=8 * 5 * full_u * full_u,
        scratch=[pltpu.VMEM(weight.shape, F32) for weight in weights]
        + [
            pltpu.VMEM((2, full_l, side), BF), pltpu.VMEM((4, 2, side, side), BF),
            pltpu.VMEM((2, side, full_l), BF),
            pltpu.SemaphoreType.DMA((5,)), pltpu.SemaphoreType.DMA((5,)),
        ],
        vmem=27,
        in_specs=[far] * 5,
        out_specs=[far] * 2,
    )(*[pltpu.with_memory_space_constraint(weight, pltpu.HBM) for weight in weights])
    first, stack = (pltpu.with_memory_space_constraint(x, pltpu.HBM) for x in (first, stack))

    def wide_bias(bias):
        return jnp.pad(bias, (0, side - bias.shape[0]))[None, :]

    queries = []
    for v in range(pairs):
        got = call(
            functools.partial(diffuse_kernel, v),
            [shaped((cells, side))] + [shaped((3, tall, around, LANES))] * (v == 0),
            flops=6 * cells * deep * full_u,
            moved=8 * tall * around * deep,
            scratch=[
                pltpu.VMEM((tall, around, deep), F32),
                pltpu.VMEM((2, tall, around + 16, LANES), F32),
                pltpu.VMEM((cells, deep), BF),
                pltpu.VMEM((cells, deep), BF),
                pltpu.VMEM((2, side, side), BF),
                pltpu.SemaphoreType.DMA,
            ],
            vmem=16,
            in_specs=[scalars, whole] + [whole] * 5 + [far],
            out_specs=[whole] * (2 - (v > 0)),
        )(sides, vectors, spread if v else diffusivity, *strips[v], stack)
        queries.append(got[0])
        if v == 0:
            spread = got[1]

    scale, one, one_t = call(
        functools.partial(hidden_kernel, mark, bucket),
        [shaped((3, slots, side)), shaped((slots, cells), BF), shaped((cells, slots), BF)],
        flops=12 * slots * full_u * full_u,
        moved=8 * slots * full_u,
        scratch=[pltpu.VMEM((slots, side), BF)] * 2
        + [
            pltpu.VMEM(packed_shape, F32),
            pltpu.VMEM((2, full_l, side), BF), pltpu.VMEM((2, side, side), BF),
            pltpu.SemaphoreType.DMA((3,)),
        ],
        vmem=18,
        in_specs=[far, far, whole, far, whole, whole],
    )(pltpu.with_memory_space_constraint(carried, pltpu.HBM), first, wide_bias(bias_first), stack, wide_bias(bias_second), channel_mask)

    fields = []
    for v in range(pairs):
        fields.append(
            call(
                net_kernel,
                [shaped((tile_x, tile_y, levels))]
                + [shaped((SWEEPS, tile_y, levels))] * 2
                + [shaped((tile_x, SWEEPS, levels))] * 2,
                flops=36 * slots * full_u * full_u,
                moved=4 * 5 * full_u * full_u,
                scratch=[pltpu.VMEM((2, slots, side), BF)]
                + [pltpu.VMEM((2, slots // 2, side), BF)] * 2
                + [pltpu.VMEM((slots // 2, side), F32)] * 2
                + [
                    pltpu.VMEM((4, 2, side, side), BF),
                    pltpu.SemaphoreType.DMA((4,)),
                ],
                vmem=22,
                in_specs=[scalars] + [whole] * 4 + [far],
            )(sides, queries[v], one, one_t, scale, stack)
        )

    out = None
    for v in range(pairs):
        around_field = halo(sides, *fields[v][1:])
        carry = [] if out is None else [out]
        out = call(
            functools.partial(finish_kernel, v),
            pltpu.HBM(vectors.shape, F32),
            flops=40 * tall * around * deep,
            moved=12 * cells * deep,
            scratch=[
                pltpu.VMEM((tall, around, deep), F32),
                pltpu.VMEM((2, tall, around + 16, LANES), F32),
                pltpu.VMEM((tile_x, tile_y, deep), F32),
                pltpu.VMEM((tile_x, tile_y, levels), F32),
                pltpu.SemaphoreType.DMA((2,)),
            ],
            vmem=16,
            in_specs=[scalars] + [whole] * 7 + [far] * len(carry),
            out_specs=far,
            input_output_aliases={8: 0} if carry else {},
        )(sides, fields[v][0], vectors, spread, *around_field, *carry)
    return out


def solution(mesh):
    in_specs = (
        P(None, "gx", "gy", None),
        P("gx", "gy"),
        P(),
        P(),
        P(),
        P(),
        P(),
        P(),
        P(),
        P(("gx", "gy")),
        P(("gx", "gy")),
        P(("gx", "gy"), None),
        P(),
    )
    out_specs = P(None, "gx", "gy", None)
    return jax.shard_map(body, mesh=mesh, in_specs=in_specs, out_specs=out_specs, check_vma=False)
```

```python
import functools

import jax
import jax.numpy as jnp
from jax import lax
from jax.experimental import pallas as pl
from jax.experimental.pallas import tpu as pltpu
from jax.sharding import PartitionSpec as P

SWEEPS = 4
WIDE = 256
LANES = 128
BF = jnp.bfloat16
F32 = jnp.float32
NN = ((1,), (0,))
NT = ((1,), (1,))


def up(size, unit):
    return -(-size // unit) * unit


def split(value):
    high = value.astype(BF)
    return high, (value - high.astype(F32)).astype(BF)


def mm(left, right, dims=NN):
    return lax.dot_general(left, right, (dims, ((), ())), preferred_element_type=F32)


def mm3(left_high, left_low, right_high, right_low, dims=NN):
    left = jnp.concatenate([left_high, left_low, left_high], axis=dims[0][0])
    right = jnp.concatenate([right_high, right_high, right_low], axis=dims[1][0])
    return mm(left, right, dims)


def halves(size):
    half = size // 2
    return [pl.ds(0, half), pl.ds(half, half)] if half % 16 == 0 else [pl.ds(0, size)]


class Fetch:
    def __init__(self, source, target, sems):
        half = target.shape[1] // 2
        self.copies = [
            pltpu.make_async_copy(
                source.at[term, pl.ds(k * half, half)],
                target.at[term, pl.ds(k * half, half)],
                sems.at[2 * term + k],
            )
            for term in range(2)
            for k in range(2)
        ]

    def start(self):
        for copy in self.copies:
            copy.start()

    def wait(self):
        for copy in self.copies:
            copy.wait()


def iota(shape, axis):
    return lax.broadcasted_iota(jnp.int32, shape, axis)


def call(kernel, out_shape, flops, moved, scratch=(), vmem=48, **more):
    return pl.pallas_call(
        kernel,
        out_shape=out_shape,
        scratch_shapes=list(scratch),
        compiler_params=pltpu.CompilerParams(vmem_limit_bytes=vmem * 1024 * 1024),
        cost_estimate=pl.CostEstimate(flops=flops, bytes_accessed=moved, transcendentals=0),
        **more,
    )


def shaped(shape, dtype=F32):
    return jax.ShapeDtypeStruct(shape, dtype)


def pack_kernel(bucket, dest_ref, cell_ref, state_ref, out_ref, high_ref, low_ref):
    levels, slots = state_ref.shape
    devices = slots // bucket
    dest = dest_ref[...]
    same = (iota((devices, slots), 0) == dest).astype(F32)
    before = (iota((slots, slots), 0) < iota((slots, slots), 1)).astype(BF)
    rank = jnp.sum(same * mm(same.astype(BF), before), axis=0, keepdims=True)
    place = dest * bucket + rank.astype(jnp.int32)
    pick = (iota((slots, slots), 0) == place).astype(BF)
    high_ref[...] = jnp.zeros_like(high_ref)
    low_ref[...] = jnp.zeros_like(low_ref)
    high, low = split(state_ref[...])
    high_ref[:levels, :] = high
    low_ref[:levels, :] = low
    mark = up(levels, 16)
    tall = jnp.where(iota((16, slots), 0) == 0, cell_ref[...], 0.0)
    high, low = split(tall)
    high_ref[mark : mark + 16, :] = high
    low_ref[mark : mark + 16, :] = low
    rows = mm(pick, high_ref[...], NT) + mm(pick, low_ref[...], NT)
    if out_ref.shape == rows.shape:
        out_ref[...] = rows
        return
    whole = rows.shape[1] // LANES - 1
    for k in range(whole):
        piece = rows[:, k * LANES : (k + 1) * LANES].reshape(devices, bucket, LANES)
        out_ref[:, k * bucket : (k + 1) * bucket, :] = piece
    tail = rows[:, whole * LANES :].reshape(devices, bucket, LANES)
    half = bucket // 2
    left = iota((devices, half, LANES), 2) < LANES // 2
    turned = pltpu.roll(tail[:, half:], LANES // 2, 2)
    out_ref[:, whole * bucket :, :] = jnp.where(left, tail[:, :half], turned)


def prep_kernel(*refs):
    ins, (first_out, stack_out), refs = refs[:5], refs[5:7], refs[7:]
    raw, (first, stack, turned, in_sem, out_sem) = refs[:5], refs[5:]
    fetch = [
        pltpu.make_async_copy(ins[k], raw[k], in_sem.at[k]) for k in range(5)
    ]
    for copy in fetch:
        copy.start()
    sends = []

    def send(source, target):
        copy = pltpu.make_async_copy(source, target, out_sem.at[len(sends)])
        copy.start()
        sends.append(copy)

    def put(values, ref):
        rows, cols = values.shape
        if (rows, cols) != ref.shape[1:]:
            ref[...] = jnp.zeros_like(ref)
        ref[0, :rows, :cols], ref[1, :rows, :cols] = split(values)

    fetch[0].wait()
    put(raw[0][...].T, turned)
    fetch[1].wait()
    put(raw[1][...], first)
    send(first, first_out)
    rows = up(raw[0].shape[1], LANES)
    stack[3, :, rows:, :] = jnp.zeros((2,) + (stack.shape[2] - rows, stack.shape[3]), BF)
    for part in halves(rows):
        got = mm3(turned[0, part, :], turned[1, part, :], first[0], first[1])
        stack[3, 0, part, :], stack[3, 1, part, :] = split(got)
    send(stack.at[3], stack_out.at[3])
    for k in range(3):
        fetch[k + 2].wait()
        put(raw[k + 2][...], stack.at[k])
        send(stack.at[k], stack_out.at[k])
    for copy in sends:
        copy.wait()


def coeff_column(coeff_ref, row):
    wide = coeff_ref.shape[1]
    spread = jnp.broadcast_to(coeff_ref[row : row + 1, :], (wide, wide))
    diagonal = iota((wide, wide), 0) == iota((wide, wide), 1)
    return jnp.sum(jnp.where(diagonal, spread, 0.0), axis=1, keepdims=True)


def cut_kernel(v, side_ref, vectors_ref, coeff_far, xa, xb, yhead, ytail, *refs):
    bufs, coeff_ref, sems = refs[:4], refs[4], refs[5]
    rows, wide, levels = vectors_ref.shape[1:]
    w = SWEEPS
    parts = (
        vectors_ref.at[v, pl.ds(0, w)],
        vectors_ref.at[v, pl.ds(rows - w, w)],
        vectors_ref.at[v, :, pl.ds(0, 8)],
        vectors_ref.at[v, :, pl.ds(wide - 8, 8)],
    )
    copies = [pltpu.make_async_copy(parts[k], bufs[k], sems.at[k]) for k in range(4)]
    if v == 0:
        fetch = pltpu.make_async_copy(coeff_far, coeff_ref, sems.at[4])
        fetch.start()
    for copy in copies:
        copy.start()
    even = side_ref[0] == 0
    if v == 0:
        fetch.wait()
        columns = [coeff_column(coeff_ref, row) for row in range(rows)]
        for row in range(w):
            head, tail = columns[row], columns[rows - w + row]
            xa[row, :, levels:] = jnp.where(even, tail, head)
            xb[row, :, levels:] = jnp.where(even, head, tail)
        for row in range(rows):
            yhead[row, :, levels:] = columns[row][:w]
            ytail[row, :, levels:] = columns[row][wide - w :]
    for copy in copies:
        copy.wait()
    head, tail = bufs[0][...], bufs[1][...]
    xa[:, :, :levels] = jnp.where(even, tail, head)
    xb[:, :, :levels] = jnp.where(even, head, tail)
    yhead[:, :, :levels] = bufs[2][:, :w]
    ytail[:, :, :levels] = bufs[3][:, 8 - w :]


def join_kernel(side_ref, ra, rb, yhead, ytail, ya, yb):
    w = SWEEPS
    rows = yhead.shape[0]
    wide = ra.shape[1]
    even_x, even_y = side_ref[0] == 0, side_ref[1] == 0

    for here, first, second in (
        (pl.ds(0, w), rb, ra),
        (pl.ds(w + rows, w), ra, rb),
    ):
        head = jnp.where(even_x, first[:, :w], second[:, :w])
        tail = jnp.where(even_x, first[:, wide - w :], second[:, wide - w :])
        ya[here] = jnp.where(even_y, tail, head)
        yb[here] = jnp.where(even_y, head, tail)
    here = pl.ds(w, rows)
    ya[here] = jnp.where(even_y, ytail[...], yhead[...])
    yb[here] = jnp.where(even_y, yhead[...], ytail[...])


def fill(ext, side_ref, tile, ra, rb, qa, qb, part):
    rows, wide = tile.shape[:2]
    w = SWEEPS
    even_y = side_ref[1] == 0
    upper = jnp.where(side_ref[0] == 0, w + rows, 0)
    tile_part, strip_part = part
    ext[w : w + rows, :wide, tile_part] = tile
    ext[pl.ds(upper, w), :wide, tile_part] = strip_part(ra)
    ext[pl.ds(w + rows - upper, w), :wide, tile_part] = strip_part(rb)
    qa, qb = strip_part(qa), strip_part(qb)
    ext[:, wide : wide + w, tile_part] = jnp.where(even_y, qa, qb)
    ext[:, wide + w :, tile_part] = jnp.where(even_y, qb, qa)


def fill_levels(ext, side_ref, tile, *strips):
    levels = tile.shape[2]
    last = up(levels, LANES) - LANES
    ext[:, :, last:] = jnp.zeros((ext.shape[0], ext.shape[1], ext.shape[2] - last), F32)
    part = (pl.ds(0, levels), lambda ref: ref[:, :, :levels])
    fill(ext, side_ref, tile, *strips, part)


def sweeps(load, cb_ref, work, emit, wide):
    tall, around = cb_ref.shape[1:3]

    def put(buffer, i, value):
        work[buffer, i, 8 : 8 + around] = value
        work[buffer, i, :8] = value[around - 8 :]
        work[buffer, i, 8 + around :] = value[:8]

    for i in range(tall):
        put(0, i, load(i))
    for sweep in range(SWEEPS):
        source = sweep % 2
        last = sweep == SWEEPS - 1
        size = wide if last else around
        for i in range(sweep + 1, tall - 1 - sweep):

            def near(row, by):
                return work[source, row, 8 + by : 8 + by + size]

            beside = (near(i - 1, 0) + near(i + 1, 0)) + (near(i, -1) + near(i, 1))
            new = cb_ref[1, i, :size] * near(i, 0) + cb_ref[0, i, :size] * beside
            if last:
                emit(i - SWEEPS, new)
            else:
                put(1 - source, i, new)


def diffuse_kernel(v, side_ref, tile_ref, coeff_ref, *refs):
    strips, stack_ref, refs = refs[:4], refs[4], refs[5:]
    ext, work, high_ref, low_ref, both, sem = refs[-6:]
    out_ref = refs[0]
    fetch = Fetch(stack_ref.at[3], both, sem)
    fetch.start()
    rows, wide, levels = tile_ref.shape[1:]
    fill_levels(ext, side_ref, tile_ref[v], *strips)
    if v > 0:
        cb_ref = coeff_ref
    else:
        cb_ref = refs[1]

        def spread(ref):
            column = ref[:, :, levels : levels + 1]
            return jnp.broadcast_to(column, column.shape[:2] + (LANES,))

        own = jnp.stack(
            [jnp.broadcast_to(coeff_column(coeff_ref, k), (wide, LANES)) for k in range(rows)]
        )
        fill(cb_ref.at[0], side_ref, own, *strips, (pl.ds(0, LANES), spread))
        cb_ref[1] = 1.0 - 4.0 * cb_ref[0]
        cb_ref[2] = 1.0 / jnp.where(cb_ref[0] == 0.0, 1.0, cb_ref[0])

    def chunk(j, _):
        lanes = pl.ds(pl.multiple_of(j * LANES, LANES), LANES)

        def emit(row, value):
            here = pl.ds(row * wide, wide)
            high_ref[here, lanes], low_ref[here, lanes] = split(value)

        sweeps(lambda i: ext[i, :, lanes], cb_ref, work, emit, wide)
        return 0

    lax.fori_loop(0, ext.shape[2] // LANES, chunk, 0)
    deep = ext.shape[2]
    fetch.wait()
    for part in halves(out_ref.shape[0]):
        out_ref[part, :] = mm3(
            high_ref[part, :], low_ref[part, :], both[0, :deep], both[1, :deep]
        )


def hidden_kernel(
    mark, bucket, x_ref, first_ref, b1_ref, stack_ref, b2_ref, mask_ref,
    scale_ref, one_ref, one_t_ref, high_ref, low_ref, x_buf, first, second, sems,
):
    fetch_x = pltpu.make_async_copy(x_ref, x_buf, sems.at[2, 0])
    fetch_x.start()
    fetch_first = Fetch(first_ref, first, sems.at[0])
    fetch_second = Fetch(stack_ref.at[0], second, sems.at[1])
    fetch_first.start()
    s1_ref, s2_ref, gate_ref = (scale_ref.at[k] for k in range(3))
    slots, cells = one_ref.shape
    devices, channels = mask_ref.shape
    fetch_x.wait()
    if len(x_buf.shape) == 2:
        deep = x_buf.shape[1]
        pieces = [x_buf[:, k : k + LANES] for k in range(0, deep, LANES)]
    else:
        whole = x_buf.shape[1] // bucket
        deep = (whole + 1) * LANES
        pieces = [
            x_buf[:, k * bucket : (k + 1) * bucket, :].reshape(slots, LANES)
            for k in range(whole)
        ]
        tail = x_buf[:, whole * bucket :, :]
        tail = jnp.concatenate([tail, pltpu.roll(tail, LANES // 2, 2)], axis=1)
        pieces.append(tail.reshape(slots, LANES))
    index = pieces[-1][:, mark % LANES : mark % LANES + 1]
    cell = index.astype(jnp.int32) - 1
    live = index > 0.5
    one_ref[...] = (iota((slots, cells), 1) == cell).astype(BF)
    flat = jnp.broadcast_to(index, (slots, LANES)).T[0:1, :].astype(jnp.int32) - 1
    one_t_ref[...] = (iota((cells, slots), 0) == flat).astype(BF)
    begin = iota((slots, devices), 1) * bucket
    at = iota((slots, devices), 0)
    from_owner = ((at >= begin) & (at < begin + bucket) & live).astype(BF)
    gate_ref[...] = jnp.zeros_like(gate_ref)
    gate_ref[:, :channels] = mm(from_owner, mask_ref[...].astype(F32).astype(BF))
    for k, piece in enumerate(pieces):
        here = pl.ds(k * LANES, LANES)
        high_ref[:, here], low_ref[:, here] = split(piece)
    parts = halves(slots)
    fetch_first.wait()
    fetch_second.start()
    for part in parts:
        got = mm3(high_ref[part, :deep], low_ref[part, :deep], first[0, :deep], first[1, :deep])
        hidden = jnp.tanh(got + b1_ref[...])
        s1_ref[part, :] = 1.0 - hidden * hidden
        high, low = split(hidden)
        high_ref[part, :] = high
        low_ref[part, :] = low
    fetch_second.wait()
    for part in parts:
        got = mm3(high_ref[part, :], low_ref[part, :], second[0], second[1])
        hidden = jnp.tanh(got + b2_ref[...])
        s2_ref[part, :] = 1.0 - hidden * hidden


LAYERS = ((0, 0, 1), (1, 1, 2), (2, 0, 2), (1, 0, 1), (0, 1, 0))


def table(values, layer):
    value = jnp.int32(values[0])
    for k in range(1, len(values)):
        value = jnp.where(layer == k, values[k], value)
    return value


def net_kernel(
    side_ref, q_ref, one_ref, one_t_ref, scale_ref, stack_ref,
    out_ref, xa, xb, yhead, ytail, x1, top, low, acc_top, acc_low, stack, sems,
):
    fetch = [Fetch(stack_ref.at[k], stack.at[k], sems.at[k]) for k in range(4)]
    fetch[0].start()
    slots = q_ref.shape[0]
    half = slots // 2
    first, second = pl.ds(0, half), pl.ds(half, half)

    def pick(picker):
        return mm(picker, x1[0]) + mm(picker, x1[1])

    def close(acc, scale, part, target):
        target[0], target[1] = split(acc[...] * scale_ref[scale, part, :])

    x1[0], x1[1] = split(q_ref[...])
    acc_top[...] = pick(one_ref[first, :])
    acc_low[...] = pick(one_ref[second, :])
    close(acc_top, 0, first, top)
    fetch[0].wait()
    fetch[1].start()
    scales = [0] + [entry[2] for entry in LAYERS]

    def step(layer, _):
        for k in (1, 2):

            @pl.when(layer == k)
            def _():
                fetch[k].wait()
                fetch[k + 1].start()

        weight = table([entry[0] for entry in LAYERS], layer)
        turned = table([entry[1] for entry in LAYERS], layer)
        before, after = table(scales[:-1], layer), table(scales[1:], layer)

        def run(dims):
            acc_top[...] = mm3(top[0], top[1], stack[weight, 0], stack[weight, 1], dims)
            close(acc_low, before, second, low)
            acc_low[...] = mm3(low[0], low[1], stack[weight, 0], stack[weight, 1], dims)
            close(acc_top, after, first, top)

        @pl.when(turned == 0)
        def _():
            run(NN)

        @pl.when(turned == 1)
        def _():
            run(NT)

        return 0

    lax.fori_loop(0, len(LAYERS), step, 0)
    close(acc_low, scales[-1], second, low)
    for part in halves(one_t_ref.shape[0]):
        got = mm(one_t_ref[part, :half], top[0]) + mm(one_t_ref[part, :half], top[1])
        got = got + mm(one_t_ref[part, half:], low[0]) + mm(one_t_ref[part, half:], low[1])
        x1[0, part, :], x1[1, part, :] = split(got)
    fetch[3].wait()
    rows, wide, levels = out_ref.shape
    for k, part in enumerate(halves(rows * wide)):
        got = mm3(x1[0, part, :], x1[1, part, :], stack[3, 0], stack[3, 1], NT)
        tall = got.shape[0] // wide
        got = got.reshape(tall, wide, got.shape[1])[:, :, :levels]
        here = pl.ds(k * tall, tall)
        out_ref[here] = got
        yhead[here] = got[:, :SWEEPS]
        ytail[here] = got[:, wide - SWEEPS :]
    even = side_ref[0] == 0
    head, tail = out_ref[:SWEEPS], out_ref[rows - SWEEPS :]
    xa[...] = jnp.where(even, tail, head)
    xb[...] = jnp.where(even, head, tail)


def finish_kernel(v, side_ref, field_ref, base_ref, cb_ref, *refs):
    out_ref, ext, work, total, result, sems = refs[-6:]
    w = SWEEPS
    rows, wide, levels = field_ref.shape
    fill_levels(ext, side_ref, field_ref[...], *refs[:4])

    def chunk(j, _):
        lanes = pl.ds(pl.multiple_of(j * LANES, LANES), LANES)

        def emit(row, value):
            total[row, :, lanes] = cb_ref[2, row + w, :wide] * value

        sweeps(lambda i: cb_ref[0, i] * ext[i, :, lanes], cb_ref, work, emit, wide)
        return 0

    lax.fori_loop(0, ext.shape[2] // LANES, chunk, 0)
    sends = []
    for k in range(2):
        part = pl.ds(k * (rows // 2), rows // 2)
        result[part] = base_ref[v, part] + total[part, :, :levels]
        sends.append(pltpu.make_async_copy(result.at[part], out_ref.at[v, part], sems.at[k]))
        sends[-1].start()
    for copy in sends:
        copy.wait()


def swap(value, axis, start):
    pairs = [(i, i + 1) for i in range(start, lax.axis_size(axis) - 1, 2)]
    return lax.ppermute(value, axis, pairs + [(j, i) for i, j in pairs])


def halo(sides, xa, xb, yhead, ytail):
    ra = swap(xa, "gx", 0)
    rb = swap(xb, "gx", 1)
    whole = pl.BlockSpec(memory_space=pltpu.VMEM)
    tall = yhead.shape[0] + 2 * SWEEPS
    ya, yb = call(
        join_kernel,
        [shaped((tall,) + yhead.shape[1:])] * 2,
        flops=0,
        moved=16 * yhead.size,
        vmem=8,
        in_specs=[pl.BlockSpec(memory_space=pltpu.SMEM)] + [whole] * 4,
    )(sides, ra, rb, yhead, ytail)
    qa = swap(ya, "gy", 0)
    qb = swap(yb, "gy", 1)
    return ra, rb, qa, qb


def body(
    vectors, diffusivity, vertical_factor, weight_first, bias_first, weight_second,
    bias_second, weight_out, error_inverse, observed_column, owner_count,
    observed_state, channel_mask,
):
    pairs, tile_x, tile_y, levels = vectors.shape
    count_y = lax.axis_size("gy")
    devices = lax.axis_size("gx") * count_y
    slots = observed_column.shape[0]
    bucket = slots // devices
    cells = tile_x * tile_y
    grid_wide = tile_y * count_y
    units = weight_second.shape[0]
    deep = up(levels, LANES)
    tall, around = tile_x + 2 * SWEEPS, tile_y + 2 * SWEEPS
    full_l, full_u = up(levels, WIDE), up(units, WIDE)
    full_c = up(error_inverse.shape[0], WIDE)
    mark = up(levels, 16)

    sides = jnp.stack([lax.axis_index("gx") % 2, lax.axis_index("gy") % 2]).astype(jnp.int32)
    whole = pl.BlockSpec(memory_space=pltpu.VMEM)
    far = pl.BlockSpec(memory_space=pltpu.HBM)
    scalars = pl.BlockSpec(memory_space=pltpu.SMEM)
    base = pltpu.with_memory_space_constraint(vectors, pltpu.HBM)
    strips = []
    for v in range(pairs):
        deep_v = levels + (v == 0)
        cuts = call(
            functools.partial(cut_kernel, v),
            [shaped((SWEEPS, tile_y, deep_v))] * 2 + [shaped((tile_x, SWEEPS, deep_v))] * 2,
            flops=0,
            moved=4 * vectors.size,
            vmem=12,
            scratch=[pltpu.VMEM((SWEEPS, tile_y, levels), F32)] * 2
            + [pltpu.VMEM((tile_x, 8, levels), F32)] * 2
            + [pltpu.VMEM(diffusivity.shape, F32), pltpu.SemaphoreType.DMA((5,))],
            in_specs=[scalars, far, far],
        )(sides, base, pltpu.with_memory_space_constraint(diffusivity, pltpu.HBM))
        strips.append(halo(sides, *cuts))

    position = jnp.arange(slots, dtype=jnp.int32)
    grid_row = observed_column // grid_wide
    grid_col = observed_column % grid_wide
    target = grid_row // tile_x * count_y + grid_col // tile_y
    dest = jnp.where(position < owner_count[0], target, -1)
    cell = (grid_row % tile_x * tile_y + grid_col % tile_y + 1).astype(F32)
    tight = bucket % 16 == 0 and mark // LANES == deep // LANES - 1 and mark % LANES < LANES // 2
    packed_shape = (slots, deep)
    if tight:
        packed_shape = (devices, bucket * (deep // LANES - 1) + bucket // 2, LANES)
    packed = call(
        functools.partial(pack_kernel, bucket),
        shaped(packed_shape),
        flops=6 * slots * slots * deep,
        moved=8 * slots * deep,
        scratch=[pltpu.VMEM((deep, slots), BF)] * 2,
        vmem=12,
    )(dest[None, :], cell[None, :], observed_state.T)
    carried = lax.all_to_all(
        packed if tight else packed.reshape(devices, bucket, deep), ("gx", "gy"),
        split_axis=0, concat_axis=0, tiled=True,
    ).reshape(packed_shape)

    side = max(full_l, full_u, full_c)
    weights = (vertical_factor, weight_first, weight_second, weight_out.T, error_inverse)
    first, stack = call(
        prep_kernel,
        [pltpu.HBM((2, full_l, side), BF), pltpu.HBM((4, 2, side, side), BF)],
        flops=6 * full_l * full_l * full_u,
        moved=8 * 5 * full_u * full_u,
        scratch=[pltpu.VMEM(weight.shape, F32) for weight in weights]
        + [
            pltpu.VMEM((2, full_l, side), BF), pltpu.VMEM((4, 2, side, side), BF),
            pltpu.VMEM((2, side, full_l), BF),
            pltpu.SemaphoreType.DMA((5,)), pltpu.SemaphoreType.DMA((5,)),
        ],
        vmem=27,
        in_specs=[far] * 5,
        out_specs=[far] * 2,
    )(*[pltpu.with_memory_space_constraint(weight, pltpu.HBM) for weight in weights])
    first, stack = (pltpu.with_memory_space_constraint(x, pltpu.HBM) for x in (first, stack))

    def wide_bias(bias):
        return jnp.pad(bias, (0, side - bias.shape[0]))[None, :]

    queries = []
    for v in range(pairs):
        got = call(
            functools.partial(diffuse_kernel, v),
            [shaped((cells, side))] + [shaped((3, tall, around, LANES))] * (v == 0),
            flops=6 * cells * deep * full_u,
            moved=8 * tall * around * deep,
            scratch=[
                pltpu.VMEM((tall, around, deep), F32),
                pltpu.VMEM((2, tall, around + 16, LANES), F32),
                pltpu.VMEM((cells, deep), BF),
                pltpu.VMEM((cells, deep), BF),
                pltpu.VMEM((2, side, side), BF),
                pltpu.SemaphoreType.DMA((4,)),
            ],
            vmem=16,
            in_specs=[scalars, whole] + [whole] * 5 + [far],
            out_specs=[whole] * (2 - (v > 0)),
        )(sides, vectors, spread if v else diffusivity, *strips[v], stack)
        queries.append(got[0])
        if v == 0:
            spread = got[1]

    scale, one, one_t = call(
        functools.partial(hidden_kernel, mark, bucket),
        [shaped((3, slots, side)), shaped((slots, cells), BF), shaped((cells, slots), BF)],
        flops=12 * slots * full_u * full_u,
        moved=8 * slots * full_u,
        scratch=[pltpu.VMEM((slots, side), BF)] * 2
        + [
            pltpu.VMEM(packed_shape, F32),
            pltpu.VMEM((2, full_l, side), BF), pltpu.VMEM((2, side, side), BF),
            pltpu.SemaphoreType.DMA((3, 4)),
        ],
        vmem=18,
        in_specs=[far, far, whole, far, whole, whole],
    )(pltpu.with_memory_space_constraint(carried, pltpu.HBM), first, wide_bias(bias_first), stack, wide_bias(bias_second), channel_mask)

    fields = []
    for v in range(pairs):
        fields.append(
            call(
                net_kernel,
                [shaped((tile_x, tile_y, levels))]
                + [shaped((SWEEPS, tile_y, levels))] * 2
                + [shaped((tile_x, SWEEPS, levels))] * 2,
                flops=36 * slots * full_u * full_u,
                moved=4 * 5 * full_u * full_u,
                scratch=[pltpu.VMEM((2, slots, side), BF)]
                + [pltpu.VMEM((2, slots // 2, side), BF)] * 2
                + [pltpu.VMEM((slots // 2, side), F32)] * 2
                + [
                    pltpu.VMEM((4, 2, side, side), BF),
                    pltpu.SemaphoreType.DMA((4, 4)),
                ],
                vmem=22,
                in_specs=[scalars] + [whole] * 4 + [far],
            )(sides, queries[v], one, one_t, scale, stack)
        )

    out = None
    for v in range(pairs):
        around_field = halo(sides, *fields[v][1:])
        carry = [] if out is None else [out]
        out = call(
            functools.partial(finish_kernel, v),
            pltpu.HBM(vectors.shape, F32),
            flops=40 * tall * around * deep,
            moved=12 * cells * deep,
            scratch=[
                pltpu.VMEM((tall, around, deep), F32),
                pltpu.VMEM((2, tall, around + 16, LANES), F32),
                pltpu.VMEM((tile_x, tile_y, deep), F32),
                pltpu.VMEM((tile_x, tile_y, levels), F32),
                pltpu.SemaphoreType.DMA((2,)),
            ],
            vmem=16,
            in_specs=[scalars] + [whole] * 7 + [far] * len(carry),
            out_specs=far,
            input_output_aliases={8: 0} if carry else {},
        )(sides, fields[v][0], vectors, spread, *around_field, *carry)
    return out


def solution(mesh):
    in_specs = (
        P(None, "gx", "gy", None),
        P("gx", "gy"),
        P(),
        P(),
        P(),
        P(),
        P(),
        P(),
        P(),
        P(("gx", "gy")),
        P(("gx", "gy")),
        P(("gx", "gy"), None),
        P(),
    )
    out_specs = P(None, "gx", "gy", None)
    return jax.shard_map(body, mesh=mesh, in_specs=in_specs, out_specs=out_specs, check_vma=False)
```
